512 devices in a mesh: grp: 32 (over y, x, core), shard: 16 (over z).
Axes of the slice: x: 4, y: 4, z: 16, core: 2. Of those that a mesh axis runs over, the one named last changes fastest.
Arguments:
- grads: bfloat16 [2, 32, 16, 768, 768], P(None, 'grp', 'shard')
- vec_grads: bfloat16 [2, 32, 16, 8, 768], P(None, 'grp', 'shard'), may hold values from -0.5 to 0.5
- weight: float32 [768, 768], P('shard'), may hold values from -0.21875 to 0.21875
- basis: float32 [768, 256], replicated, may hold values from -0.21875 to 0.21875
- moment: float32 [768, 256], P('shard'), may hold values from -4 to 4
- second: float32 [768, 256], P('shard'), may hold values from 0.01 to 1
- vectors: float32 [8, 768], P(None, 'shard'), may hold values from -6 to 6
- vec_moment: float32 [8, 768], P(None, 'shard'), may hold values from -1.5 to 1.5
- vec_second: float32 [8, 768], P(None, 'shard'), may hold values from 0.001 to 0.1
Outputs:
- new_weight: float32 [768, 768], P('shard')
- update: bfloat16 [768, 768], P('shard')
- new_moment: float32 [768, 256], P('shard')
- new_second: float32 [768, 256], P('shard')
- new_basis: float32 [768, 256], replicated
- new_vectors: float32 [8, 768], P(None, 'shard')
- new_vec_moment: float32 [8, 768], P(None, 'shard')
- new_vec_second: float32 [8, 768], P(None, 'shard')
The draws below stay inside these ranges and needn't reach their ends.
All inputs are finite; a program needn't handle non-finite values.
Results may differ from the reference program's by a relative error of at most 0.001.
Values sent between devices are 32-bit elements; how exact they have to be, the bound alone decides.
A program may use at most 64 MiB of HBM per device.

```python
import math
import jax
import jax.numpy as jnp
from jax import lax

D = 768
RANK = 256
VEC = 8
NS_STEPS = 5
STEP = 100
MICRO = 1024
COUNT = 595968
N_GRP = 32
N_SHARD = 16


def draw_grads(key, part):
    shape = (2, N_GRP, N_SHARD, D, D)
    index = jnp.arange(D, dtype=jnp.float32)
    rising = 10.0 ** (index / (D - 1)) / 3.0
    scale = rising[:, None] * rising[None, :]
    noise = jax.random.truncated_normal(key, -6.0, 6.0, shape, jnp.float32)
    values = noise * scale / MICRO ** 0.5
    return values.astype(jnp.bfloat16)


def block_levels(stream_key, shape, cuts, low, high):
    gain, own = 1.0, jax.random.fold_in(stream_key, 6)
    for axis_at, parts in cuts:
        draws = jnp.exp(jax.random.uniform(jax.random.fold_in(own, axis_at), (parts,), jnp.float32, low / len(cuts), high / len(cuts)))
        gain = gain * jnp.repeat(draws, shape[axis_at] // parts).reshape([-1 if axis == axis_at else 1 for axis in range(len(shape))])
    return gain


def gaussian(rng, shape, deviation, most, shards=(), kind=jnp.bfloat16):
    array = jax.random.normal(rng, shape, jnp.float32) * deviation
    if len(shards) > 0:
        array = block_levels(rng, shape, shards, -0.22, 0.18) * array
    return jnp.clip(array, min=-most, max=most).astype(kind)


def setup_inputs(seed: int = 0) -> dict:
    streams_of = jax.random.split(jax.random.key(seed), 10)
    grads = draw_grads(jax.random.fold_in(streams_of[9], 71), 0)
    vec_grads = gaussian(streams_of[1], (2, N_GRP, N_SHARD, VEC, D), (MICRO ** -0.5), 0.5, ((1, 32), (2, 16)))
    weight = gaussian(streams_of[2], (D, D), D ** -0.5, 0.21875, ((0, 16),), jnp.float32)
    basis = gaussian(streams_of[3], (D, RANK), D ** -0.5, 0.21875, (), jnp.float32)
    moment = gaussian(streams_of[4], (D, RANK), 0.3, 4.0, ((0, 16),), jnp.float32)
    second = jnp.clip(jnp.exp(math.log(1.0) - 4.6051702 * jax.random.uniform(streams_of[5], (D, RANK), jnp.float32) ** block_levels(streams_of[5], (D, RANK), ((0, 16),), -0.2, 0.2)), 0.01, 1.0)
    vectors = gaussian(streams_of[6], (VEC, D), 1.0, 6.0, ((1, 16),), jnp.float32)
    vec_moment = gaussian(streams_of[7], (VEC, D), 0.1, 1.5, ((1, 16),), jnp.float32)
    vec_second = jnp.clip(jnp.exp(math.log(0.1) - 4.6051702 * jax.random.uniform(streams_of[8], (VEC, D), jnp.float32) ** block_levels(streams_of[8], (VEC, D), ((1, 16),), -0.2, 0.2)), 0.001, 0.1)
    return {"grads": grads, "vec_grads": vec_grads, "weight": weight, "basis": basis, "moment": moment, "second": second, "vectors": vectors, "vec_moment": vec_moment, "vec_second": vec_second}


HIGH = lax.Precision.HIGHEST

def reference(grads, vec_grads, weight, basis, moment, second, vectors, vec_moment, vec_second):

    def add_group(index, total):
        piece = lax.dynamic_index_in_dim(grads, index, axis=1, keepdims=False)
        return total + lax.optimization_barrier(jnp.sum(piece.astype(jnp.float32), axis=(0, 1)))
    total = lax.fori_loop(0, grads.shape[1], add_group, jnp.zeros((D, D), jnp.float32))
    vec_total = lax.optimization_barrier(jnp.sum(vec_grads.astype(jnp.float32), axis=(0, 1, 2)))
    squares = jnp.sum(total * total) + jnp.sum(vec_total * vec_total)
    factor = 1.0 / jnp.maximum(jnp.sqrt(squares / COUNT), 1.0)
    projected = jnp.dot(total, basis, precision=HIGH, preferred_element_type=jnp.float32)
    subspace = jnp.dot(total.T, projected, precision=HIGH, preferred_element_type=jnp.float32)
    iterate = subspace / jnp.sqrt(jnp.sum(subspace * subspace) + 1e-06)
    for step in range(NS_STEPS):
        gram = jnp.dot(iterate.T, iterate, precision=HIGH, preferred_element_type=jnp.float32)
        iterate = 1.5 * iterate - 0.5 * jnp.dot(iterate, gram, precision=HIGH, preferred_element_type=jnp.float32)
    first_fix = 1.0 - 0.9 ** STEP
    second_fix = 1.0 - 0.999 ** STEP
    grad_low = factor * projected
    new_moment = 0.9 * moment + 0.1 * grad_low
    new_second = 0.999 * second + 0.001 * grad_low * grad_low
    normalized = new_moment / first_fix / (jnp.sqrt(new_second / second_fix) + 1e-08)
    full = jnp.dot(normalized, basis.T, precision=HIGH, preferred_element_type=jnp.float32)
    new_weight = weight - 0.001 * (0.25 * full + 0.01 * weight)
    vec_grad = factor * vec_total
    new_vec_moment = 0.9 * vec_moment + 0.1 * vec_grad
    new_vec_second = 0.999 * vec_second + 0.001 * vec_grad * vec_grad
    vec_step = new_vec_moment / first_fix / (jnp.sqrt(new_vec_second / second_fix) + 1e-08)
    new_vectors = vectors - 0.001 * (vec_step + 0.01 * vectors)
    return (new_weight, full.astype(jnp.bfloat16), new_moment, new_second, iterate, new_vectors, new_vec_moment, new_vec_second)
```

```python
import jax
import jax.numpy as jnp
from jax import lax
from jax.sharding import PartitionSpec as P

NS_STEPS = 5
STEP = 100


HIGH = lax.Precision.HIGHEST


def matmul(left, right):
    return jnp.dot(left, right, precision=HIGH, preferred_element_type=jnp.float32)


def per_device(grads, vec_grads, weight, basis, moment, second, vectors, vec_moment, vec_second):
    shards = lax.axis_size("shard")
    width = grads.shape[-1]
    rows = weight.shape[0]
    cols = vectors.shape[1]
    me = lax.axis_index("shard")
    summed = grads[0, 0, 0].astype(jnp.float32) + grads[1, 0, 0].astype(jnp.float32)
    vec_local = vec_grads[0, 0, 0].astype(jnp.float32) + vec_grads[1, 0, 0].astype(jnp.float32)
    packed = jnp.concatenate([summed, vec_local], axis=0)
    packed = lax.psum(packed, ("grp", "shard"))
    total = packed[:width]
    vec_total = packed[width:]
    projected_all = matmul(total, basis)
    subspace = lax.dot_general(
        total,
        projected_all,
        (((0,), (0,)), ((), ())),
        precision=HIGH,
        preferred_element_type=jnp.float32,
    )
    squares = jnp.sum(total * total) + jnp.sum(vec_total * vec_total)
    iterate = subspace / jnp.sqrt(jnp.sum(subspace * subspace) + 1e-06)
    for step in range(NS_STEPS):
        gram = matmul(iterate.T, iterate)
        iterate = 1.5 * iterate - 0.5 * matmul(iterate, gram)
    factor = 1.0 / jnp.maximum(jnp.sqrt(squares / (width * width + vec_total.size)), 1.0)
    projected = lax.dynamic_slice_in_dim(projected_all, me * rows, rows, axis=0)
    vec_sum = lax.dynamic_slice_in_dim(vec_total, me * cols, cols, axis=1)
    first_fix = 1.0 - 0.9**STEP
    second_fix = 1.0 - 0.999**STEP
    grad_low = factor * projected
    new_moment = 0.9 * moment + 0.1 * grad_low
    new_second = 0.999 * second + 0.001 * grad_low * grad_low
    normalized = new_moment / first_fix / (jnp.sqrt(new_second / second_fix) + 1e-08)
    full = lax.dot_general(
        normalized,
        basis,
        (((1,), (1,)), ((), ())),
        precision=HIGH,
        preferred_element_type=jnp.float32,
    )
    new_weight = weight - 0.001 * (0.25 * full + 0.01 * weight)
    vec_grad = factor * vec_sum
    new_vec_moment = 0.9 * vec_moment + 0.1 * vec_grad
    new_vec_second = 0.999 * vec_second + 0.001 * vec_grad * vec_grad
    vec_step = new_vec_moment / first_fix / (jnp.sqrt(new_vec_second / second_fix) + 1e-08)
    new_vectors = vectors - 0.001 * (vec_step + 0.01 * vectors)
    return (
        new_weight,
        full.astype(jnp.bfloat16),
        new_moment,
        new_second,
        iterate,
        new_vectors,
        new_vec_moment,
        new_vec_second,
    )


def solution(mesh):
    return jax.shard_map(
        per_device,
        mesh=mesh,
        in_specs=(
            P(None, "grp", "shard", None, None),
            P(None, "grp", "shard", None, None),
            P("shard", None),
            P(),
            P("shard", None),
            P("shard", None),
            P(None, "shard"),
            P(None, "shard"),
            P(None, "shard"),
        ),
        out_specs=(
            P("shard", None),
            P("shard", None),
            P("shard", None),
            P("shard", None),
            P(),
            P(None, "shard"),
            P(None, "shard"),
            P(None, "shard"),
        ),
        check_vma=False,
    )
```

```python
import functools
import math

import jax
import jax.numpy as jnp
from jax import lax
from jax.experimental import pallas as pl
from jax.experimental.pallas import tpu as pltpu
from jax.sharding import PartitionSpec as P

NS_STEPS = 5
STEP = 100
MESH = pl.DeviceIdType.MESH


HIGH = lax.Precision.HIGHEST


def matmul(left, right):
    return jnp.dot(left, right, precision=HIGH, preferred_element_type=jnp.float32)


def _allreduce_kernel(nx, ny, nz, x_ref, out_ref, core_recv, core_sum, x_recv, x_sum, y_recv, y_sum,
                      z_recv, z_sum, pair_recv, z_full, y_out, x_out, core_out, send_sem, recv_sem):
    rows, cols = x_ref.shape
    nh = nz // 2
    rc, rx, ry, cz = rows // 2, rows // 2 // nx, rows // 2 // nx // ny, cols // nh
    g = lax.axis_index("grp")
    z = lax.axis_index("shard")
    core = g % 2
    xi = (g // 2) % nx
    yi = g // (2 * nx)
    zp = z % 2
    zi = z // 2

    def core_dev(_):
        return (g + 1 - 2 * core, z)

    def x_dev(j):
        return (g + 2 * (j - xi), z)

    def y_dev(j):
        return (g + 2 * nx * (j - yi), z)

    def z_dev(j):
        return (g, zp + 2 * j)

    pair_dev = (g, z + 1 - 2 * zp)

    barrier = pltpu.get_barrier_semaphore()
    peers = [core_dev(0), pair_dev]
    peers += [x_dev((xi + k) % nx) for k in range(1, nx)]
    peers += [y_dev((yi + k) % ny) for k in range(1, ny)]
    peers += [z_dev((zi + k) % nh) for k in range(1, nh)]
    for dev in peers:
        pl.semaphore_signal(barrier, inc=1, device_id=dev, device_id_type=MESH)
    pl.semaphore_wait(barrier, len(peers))

    counter = [0]

    def next_sem():
        s = counter[0]
        counter[0] += 1
        return s

    def row_slice(j, size):
        return pl.ds(pl.multiple_of(j * size, 8), size)

    def col_slice(j, size):
        return (slice(None), pl.ds(pl.multiple_of(j * size, 128), size))

    def reduce_stage(src, n, me, dev_of, recv, dst, piece):
        copies = []
        for k in range(1, n):
            j = (me + k) % n
            s = next_sem()
            c = pltpu.make_async_remote_copy(
                src_ref=src.at[piece(j)], dst_ref=recv.at[k - 1], send_sem=send_sem.at[s],
                recv_sem=recv_sem.at[s], device_id=dev_of(j), device_id_type=MESH)
            c.start()
            copies.append(c)
        for c in copies:
            c.wait()
        acc = src[piece(me)]
        for k in range(1, n):
            acc = acc + recv[k - 1]
        dst[...] = acc

    def gather_stage(src, n, me, dev_of, dst, piece):
        copies = []
        for k in range(1, n):
            j = (me + k) % n
            s = next_sem()
            c = pltpu.make_async_remote_copy(
                src_ref=src, dst_ref=dst.at[piece(me)], send_sem=send_sem.at[s],
                recv_sem=recv_sem.at[s], device_id=dev_of(j), device_id_type=MESH)
            c.start()
            copies.append((c, s, k))
        dst[piece(me)] = src[...]
        for c, s, k in copies:
            c.wait_send()
            j = (me + n - k) % n
            pltpu.make_async_remote_copy(
                src_ref=src, dst_ref=dst.at[piece(j)], send_sem=send_sem.at[s],
                recv_sem=recv_sem.at[s], device_id=dev_of(j), device_id_type=MESH).wait_recv()

    core_piece = lambda j: row_slice(j, rc)
    x_piece = lambda j: row_slice(j, rx)
    y_piece = lambda j: row_slice(j, ry)
    z_piece = lambda j: col_slice(j, cz)

    reduce_stage(x_ref, 2, core, core_dev, core_recv, core_sum, core_piece)
    reduce_stage(core_sum, nx, xi, x_dev, x_recv, x_sum, x_piece)
    reduce_stage(x_sum, ny, yi, y_dev, y_recv, y_sum, y_piece)
    reduce_stage(y_sum, nh, zi, z_dev, z_recv, z_sum, z_piece)

    s = next_sem()
    c = pltpu.make_async_remote_copy(
        src_ref=z_sum, dst_ref=pair_recv, send_sem=send_sem.at[s], recv_sem=recv_sem.at[s],
        device_id=pair_dev, device_id_type=MESH)
    c.start()
    c.wait()
    z_full[...] = z_sum[...] + pair_recv[...]

    gather_stage(z_full, nh, zi, z_dev, y_out, z_piece)
    gather_stage(y_out, ny, yi, y_dev, x_out, y_piece)
    gather_stage(x_out, nx, xi, x_dev, core_out, x_piece)
    gather_stage(core_out, 2, core, core_dev, out_ref, core_piece)


def allreduce(x, nx, ny, nz):
    rows, cols = x.shape
    nh = nz // 2
    rc = rows // 2
    rx = rc // nx
    ry = rx // ny
    cz = cols // nh
    n_sems = 2 * (1 + (nx - 1) + (ny - 1) + (nh - 1)) + 1
    f32 = jnp.float32
    return pl.pallas_call(
        functools.partial(_allreduce_kernel, nx, ny, nz),
        out_shape=jax.ShapeDtypeStruct((rows, cols), f32),
        in_specs=[pl.BlockSpec(memory_space=pltpu.VMEM)],
        out_specs=pl.BlockSpec(memory_space=pltpu.VMEM),
        scratch_shapes=[
            pltpu.VMEM((1, rc, cols), f32),
            pltpu.VMEM((rc, cols), f32),
            pltpu.VMEM((nx - 1, rx, cols), f32),
            pltpu.VMEM((rx, cols), f32),
            pltpu.VMEM((ny - 1, ry, cols), f32),
            pltpu.VMEM((ry, cols), f32),
            pltpu.VMEM((nh - 1, ry, cz), f32),
            pltpu.VMEM((ry, cz), f32),
            pltpu.VMEM((ry, cz), f32),
            pltpu.VMEM((ry, cz), f32),
            pltpu.VMEM((ry, cols), f32),
            pltpu.VMEM((rx, cols), f32),
            pltpu.VMEM((rc, cols), f32),
            pltpu.SemaphoreType.DMA((n_sems,)),
            pltpu.SemaphoreType.DMA((n_sems,)),
        ],
        compiler_params=pltpu.CompilerParams(
            collective_id=0, has_side_effects=True, vmem_limit_bytes=48 * 1024 * 1024),
    )(x)


def per_device(nx, ny, grads, vec_grads, weight, basis, moment, second, vectors, vec_moment, vec_second):
    shards = lax.axis_size("shard")
    width = grads.shape[-1]
    rows = weight.shape[0]
    cols = vectors.shape[1]
    vec_n = vectors.shape[0]
    me = lax.axis_index("shard")
    summed = grads[0, 0, 0].astype(jnp.float32) + grads[1, 0, 0].astype(jnp.float32)
    vec_local = vec_grads[0, 0, 0].astype(jnp.float32) + vec_grads[1, 0, 0].astype(jnp.float32)
    lanes = 128 * (shards // 2)
    padded = lanes * ((width + vec_n + lanes - 1) // lanes)
    pad = jnp.zeros((width, padded - width - vec_n), jnp.float32)
    packed = jnp.concatenate([summed, vec_local.T, pad], axis=1)
    packed = allreduce(packed, nx, ny, shards)
    total = packed[:, :width]
    vec_total = packed[:, width:width + vec_n].T
    projected_all = matmul(total, basis)
    subspace = lax.dot_general(
        total,
        projected_all,
        (((0,), (0,)), ((), ())),
        precision=HIGH,
        preferred_element_type=jnp.float32,
    )
    squares = jnp.sum(total * total) + jnp.sum(vec_total * vec_total)
    iterate = subspace / jnp.sqrt(jnp.sum(subspace * subspace) + 1e-06)
    for step in range(NS_STEPS):
        gram = matmul(iterate.T, iterate)
        iterate = 1.5 * iterate - 0.5 * matmul(iterate, gram)
    factor = 1.0 / jnp.maximum(jnp.sqrt(squares / (width * width + vec_total.size)), 1.0)
    projected = lax.dynamic_slice_in_dim(projected_all, me * rows, rows, axis=0)
    vec_sum = lax.dynamic_slice_in_dim(vec_total, me * cols, cols, axis=1)
    first_fix = 1.0 - 0.9**STEP
    second_fix = 1.0 - 0.999**STEP
    grad_low = factor * projected
    new_moment = 0.9 * moment + 0.1 * grad_low
    new_second = 0.999 * second + 0.001 * grad_low * grad_low
    normalized = new_moment / first_fix / (jnp.sqrt(new_second / second_fix) + 1e-08)
    full = lax.dot_general(
        normalized,
        basis,
        (((1,), (1,)), ((), ())),
        precision=HIGH,
        preferred_element_type=jnp.float32,
    )
    new_weight = weight - 0.001 * (0.25 * full + 0.01 * weight)
    vec_grad = factor * vec_sum
    new_vec_moment = 0.9 * vec_moment + 0.1 * vec_grad
    new_vec_second = 0.999 * vec_second + 0.001 * vec_grad * vec_grad
    vec_step = new_vec_moment / first_fix / (jnp.sqrt(new_vec_second / second_fix) + 1e-08)
    new_vectors = vectors - 0.001 * (vec_step + 0.01 * vectors)
    return (
        new_weight,
        full.astype(jnp.bfloat16),
        new_moment,
        new_second,
        iterate,
        new_vectors,
        new_vec_moment,
        new_vec_second,
    )


def solution(mesh, nx=None):
    if nx is None:
        nx = math.isqrt(mesh.shape["grp"] // 2)
    ny = mesh.shape["grp"] // 2 // nx
    return jax.shard_map(
        functools.partial(per_device, nx, ny),
        mesh=mesh,
        in_specs=(
            P(None, "grp", "shard", None, None),
            P(None, "grp", "shard", None, None),
            P("shard", None),
            P(),
            P("shard", None),
            P("shard", None),
            P(None, "shard"),
            P(None, "shard"),
            P(None, "shard"),
        ),
        out_specs=(
            P("shard", None),
            P("shard", None),
            P("shard", None),
            P("shard", None),
            P(),
            P(None, "shard"),
            P(None, "shard"),
            P(None, "shard"),
        ),
        check_vma=False,
    )
```

```python
import functools
import math

import jax
import jax.numpy as jnp
from jax import lax
from jax.experimental import pallas as pl
from jax.experimental.pallas import tpu as pltpu
from jax.sharding import PartitionSpec as P

NS_STEPS = 5
STEP = 100
MESH = pl.DeviceIdType.MESH


HIGH = lax.Precision.HIGH


def matmul(left, right):
    return jnp.dot(left, right, precision=HIGH, preferred_element_type=jnp.float32)


def _allreduce_kernel(nx, ny, nz, g_ref, tail_ref, out_ref, sq_ref, x_ref, core_recv, core_sum, x_recv, x_sum, y_recv, y_sum,
                      z_recv, z_sum, pair_recv, z_full, y_out, x_out, core_out, send_sem, recv_sem):
    rows, cols = x_ref.shape
    width = g_ref.shape[-1]
    x_ref[:, :width] = g_ref[0].astype(jnp.float32) + g_ref[1].astype(jnp.float32)
    x_ref[:, width:] = tail_ref[...]
    nh = nz // 2
    rc, rx, ry, cz = rows // 2, rows // 2 // nx, rows // 2 // nx // ny, cols // nh
    g = lax.axis_index("grp")
    z = lax.axis_index("shard")
    core = g % 2
    xi = (g // 2) % nx
    yi = g // (2 * nx)
    zp = z % 2
    zi = z // 2

    def core_dev(_):
        return (g + 1 - 2 * core, z)

    stride_a = 2 + (2 * nx - 2) * core
    pos_a = xi + (yi - xi) * core
    stride_b = 2 * nx - (2 * nx - 2) * core
    pos_b = yi + (xi - yi) * core

    def x_dev(j):
        return (g + stride_a * (j - pos_a), z)

    def y_dev(j):
        return (g + stride_b * (j - pos_b), z)

    def z_dev(j):
        return (g, zp + 2 * j)

    pair_dev = (g, z + 1 - 2 * zp)

    barrier = pltpu.get_barrier_semaphore()
    peers = [core_dev(0), pair_dev]
    peers += [x_dev((pos_a + k) % nx) for k in range(1, nx)]
    peers += [y_dev((pos_b + k) % ny) for k in range(1, ny)]
    peers += [z_dev((zi + k) % nh) for k in range(1, nh)]
    for dev in peers:
        pl.semaphore_signal(barrier, inc=1, device_id=dev, device_id_type=MESH)
    pl.semaphore_wait(barrier, len(peers))

    counter = [0]

    def next_sem():
        s = counter[0]
        counter[0] += 1
        return s

    def row_slice(j, size):
        return pl.ds(pl.multiple_of(j * size, 8), size)

    def col_slice(j, size):
        return (slice(None), pl.ds(pl.multiple_of(j * size, 128), size))

    def reduce_stage(src, n, me, dev_of, recv, dst, piece):
        copies = []
        for k in range(1, n):
            j = (me + k) % n
            s = next_sem()
            c = pltpu.make_async_remote_copy(
                src_ref=src.at[piece(j)], dst_ref=recv.at[k - 1], send_sem=send_sem.at[s],
                recv_sem=recv_sem.at[s], device_id=dev_of(j), device_id_type=MESH)
            c.start()
            copies.append(c)
        for c in copies:
            c.wait()
        acc = src[piece(me)]
        for k in range(1, n):
            acc = acc + recv[k - 1]
        dst[...] = acc

    def gather_stage(src, n, me, dev_of, dst, piece):
        copies = []
        for k in range(1, n):
            j = (me + k) % n
            s = next_sem()
            c = pltpu.make_async_remote_copy(
                src_ref=src, dst_ref=dst.at[piece(me)], send_sem=send_sem.at[s],
                recv_sem=recv_sem.at[s], device_id=dev_of(j), device_id_type=MESH)
            c.start()
            copies.append((c, s, k))
        dst[piece(me)] = src[...]
        for c, s, k in copies:
            c.wait_send()
            j = (me + n - k) % n
            pltpu.make_async_remote_copy(
                src_ref=src, dst_ref=dst.at[piece(j)], send_sem=send_sem.at[s],
                recv_sem=recv_sem.at[s], device_id=dev_of(j), device_id_type=MESH).wait_recv()

    core_piece = lambda j: row_slice(j, rc)
    x_piece = lambda j: row_slice(j, rx)
    y_piece = lambda j: row_slice(j, ry)
    z_piece = lambda j: col_slice(j, cz)

    reduce_stage(x_ref, 2, core, core_dev, core_recv, core_sum, core_piece)
    reduce_stage(core_sum, nx, pos_a, x_dev, x_recv, x_sum, x_piece)
    reduce_stage(x_sum, ny, pos_b, y_dev, y_recv, y_sum, y_piece)
    reduce_stage(y_sum, nh, zi, z_dev, z_recv, z_sum, z_piece)

    s = next_sem()
    c = pltpu.make_async_remote_copy(
        src_ref=z_sum, dst_ref=pair_recv, send_sem=send_sem.at[s], recv_sem=recv_sem.at[s],
        device_id=pair_dev, device_id_type=MESH)
    c.start()
    c.wait()
    z_full[...] = z_sum[...] + pair_recv[...]

    gather_stage(z_full, nh, zi, z_dev, y_out, z_piece)
    gather_stage(y_out, ny, pos_b, y_dev, x_out, y_piece)
    gather_stage(x_out, nx, pos_a, x_dev, core_out, x_piece)
    gather_stage(core_out, 2, core, core_dev, out_ref, core_piece)
    full = out_ref[...]
    part = jnp.sum(full * full, axis=0, keepdims=True)
    sq_ref[...] = jnp.broadcast_to(jnp.sum(part, axis=1, keepdims=True), sq_ref.shape)


def allreduce(g, tail, nx, ny, nz):
    assert nx == ny
    rows = g.shape[1]
    cols = g.shape[2] + tail.shape[1]
    nh = nz // 2
    rc = rows // 2
    rx = rc // nx
    ry = rx // ny
    cz = cols // nh
    n_sems = 2 * (1 + (nx - 1) + (ny - 1) + (nh - 1)) + 1
    f32 = jnp.float32
    return pl.pallas_call(
        functools.partial(_allreduce_kernel, nx, ny, nz),
        out_shape=(jax.ShapeDtypeStruct((rows, cols), f32), jax.ShapeDtypeStruct((8, 128), f32)),
        in_specs=[pl.BlockSpec(memory_space=pltpu.VMEM)] * 2,
        out_specs=(pl.BlockSpec(memory_space=pltpu.VMEM),) * 2,
        scratch_shapes=[
            pltpu.VMEM((rows, cols), f32),
            pltpu.VMEM((1, rc, cols), f32),
            pltpu.VMEM((rc, cols), f32),
            pltpu.VMEM((nx - 1, rx, cols), f32),
            pltpu.VMEM((rx, cols), f32),
            pltpu.VMEM((ny - 1, ry, cols), f32),
            pltpu.VMEM((ry, cols), f32),
            pltpu.VMEM((nh - 1, ry, cz), f32),
            pltpu.VMEM((ry, cz), f32),
            pltpu.VMEM((ry, cz), f32),
            pltpu.VMEM((ry, cz), f32),
            pltpu.VMEM((ry, cols), f32),
            pltpu.VMEM((rx, cols), f32),
            pltpu.VMEM((rc, cols), f32),
            pltpu.SemaphoreType.DMA((n_sems,)),
            pltpu.SemaphoreType.DMA((n_sems,)),
        ],
        compiler_params=pltpu.CompilerParams(
            collective_id=0, has_side_effects=True, vmem_limit_bytes=48 * 1024 * 1024),
    )(g, tail)


def per_device(nx, ny, grads, vec_grads, weight, basis, moment, second, vectors, vec_moment, vec_second):
    shards = lax.axis_size("shard")
    width = grads.shape[-1]
    rows = weight.shape[0]
    cols = vectors.shape[1]
    vec_n = vectors.shape[0]
    me = lax.axis_index("shard")
    vec_local = vec_grads[0, 0, 0].astype(jnp.float32) + vec_grads[1, 0, 0].astype(jnp.float32)
    lanes = 128 * (shards // 2)
    padded = lanes * ((width + vec_n + lanes - 1) // lanes)
    pad = jnp.zeros((width, padded - width - vec_n), jnp.float32)
    tail = jnp.concatenate([vec_local.T, pad], axis=1)
    packed, sq = allreduce(grads[:, 0, 0], tail, nx, ny, shards)
    total = packed[:, :width]
    vec_total = packed[:, width:width + vec_n].T
    projected_all = matmul(total, basis)
    subspace = lax.dot_general(
        total,
        projected_all,
        (((0,), (0,)), ((), ())),
        precision=HIGH,
        preferred_element_type=jnp.float32,
    )
    squares = sq[0, 0]
    iterate = subspace / jnp.sqrt(jnp.sum(subspace * subspace) + 1e-06)
    for step in range(NS_STEPS):
        gram = matmul(iterate.T, iterate)
        iterate = 1.5 * iterate - 0.5 * matmul(iterate, gram)
    factor = 1.0 / jnp.maximum(jnp.sqrt(squares / (width * width + vec_total.size)), 1.0)
    projected = lax.dynamic_slice_in_dim(projected_all, me * rows, rows, axis=0)
    vec_sum = lax.dynamic_slice_in_dim(vec_total, me * cols, cols, axis=1)
    first_fix = 1.0 - 0.9**STEP
    second_fix = 1.0 - 0.999**STEP
    grad_low = factor * projected
    new_moment = 0.9 * moment + 0.1 * grad_low
    new_second = 0.999 * second + 0.001 * grad_low * grad_low
    normalized = new_moment / first_fix / (jnp.sqrt(new_second / second_fix) + 1e-08)
    full = lax.dot_general(
        normalized,
        basis,
        (((1,), (1,)), ((), ())),
        precision=HIGH,
        preferred_element_type=jnp.float32,
    )
    new_weight = weight - 0.001 * (0.25 * full + 0.01 * weight)
    vec_grad = factor * vec_sum
    new_vec_moment = 0.9 * vec_moment + 0.1 * vec_grad
    new_vec_second = 0.999 * vec_second + 0.001 * vec_grad * vec_grad
    vec_step = new_vec_moment / first_fix / (jnp.sqrt(new_vec_second / second_fix) + 1e-08)
    new_vectors = vectors - 0.001 * (vec_step + 0.01 * vectors)
    return (
        new_weight,
        full.astype(jnp.bfloat16),
        new_moment,
        new_second,
        iterate,
        new_vectors,
        new_vec_moment,
        new_vec_second,
    )


def solution(mesh, nx=None):
    if nx is None:
        nx = math.isqrt(mesh.shape["grp"] // 2)
    ny = mesh.shape["grp"] // 2 // nx
    return jax.shard_map(
        functools.partial(per_device, nx, ny),
        mesh=mesh,
        in_specs=(
            P(None, "grp", "shard", None, None),
            P(None, "grp", "shard", None, None),
            P("shard", None),
            P(),
            P("shard", None),
            P("shard", None),
            P(None, "shard"),
            P(None, "shard"),
            P(None, "shard"),
        ),
        out_specs=(
            P("shard", None),
            P("shard", None),
            P("shard", None),
            P("shard", None),
            P(),
            P(None, "shard"),
            P(None, "shard"),
            P(None, "shard"),
        ),
        check_vma=False,
    )
```

```python
import functools
import math

import jax
import jax.numpy as jnp
from jax import lax
from jax.experimental import pallas as pl
from jax.experimental.pallas import tpu as pltpu
from jax.sharding import PartitionSpec as P

NS_STEPS = 5
STEP = 100
MESH = pl.DeviceIdType.MESH


HIGH = lax.Precision.HIGH


def matmul(left, right):
    return jnp.dot(left, right, precision=HIGH, preferred_element_type=jnp.float32)


def _allreduce_kernel(nx, ny, nz, g_ref, tail_ref, out_ref, sq_ref, x_ref, core_recv, core_sum, x_recv, x_sum, y_recv,
                      y_pad, z_recv, z_sum, pair_recv, z_full, y_out, x_out, core_out, send_sem, recv_sem):
    rows, cols = x_ref.shape
    zcols = y_pad.shape[1]
    width = g_ref.shape[-1]
    x_ref[:, :width] = g_ref[0].astype(jnp.float32) + g_ref[1].astype(jnp.float32)
    x_ref[:, width:] = tail_ref[...]
    nh = nz // 2
    rc, rx, ry, cz = rows // 2, rows // 2 // nx, rows // 2 // nx // ny, zcols // nh
    g = lax.axis_index("grp")
    z = lax.axis_index("shard")
    core = g % 2
    xi = (g // 2) % nx
    yi = g // (2 * nx)
    zp = z % 2
    zi = z // 2

    def core_dev(_):
        return (g + 1 - 2 * core, z)

    stride_a = 2 + (2 * nx - 2) * core
    pos_a = xi + (yi - xi) * core
    stride_b = 2 * nx - (2 * nx - 2) * core
    pos_b = yi + (xi - yi) * core

    def x_dev(j):
        return (g + stride_a * (j - pos_a), z)

    def y_dev(j):
        return (g + stride_b * (j - pos_b), z)

    def z_dev(j):
        return (g, zp + 2 * j)

    pair_dev = (g, z + 1 - 2 * zp)

    barrier = pltpu.get_barrier_semaphore()
    peers = [core_dev(0), pair_dev]
    peers += [x_dev((pos_a + k) % nx) for k in range(1, nx)]
    peers += [y_dev((pos_b + k) % ny) for k in range(1, ny)]
    peers += [z_dev((zi + k) % nh) for k in range(1, nh)]
    for dev in peers:
        pl.semaphore_signal(barrier, inc=1, device_id=dev, device_id_type=MESH)
    pl.semaphore_wait(barrier, len(peers))

    counter = [0]

    def next_sem():
        s = counter[0]
        counter[0] += 1
        return s

    def row_slice(j, size):
        return pl.ds(pl.multiple_of(j * size, 8), size)

    def col_slice(j, size):
        return (slice(None), pl.ds(pl.multiple_of(j * size, 128), size))

    def reduce_stage(src, n, me, dev_of, recv, dst, piece):
        copies = []
        for k in range(1, n):
            j = (me + k) % n
            s = next_sem()
            c = pltpu.make_async_remote_copy(
                src_ref=src.at[piece(j)], dst_ref=recv.at[k - 1], send_sem=send_sem.at[s],
                recv_sem=recv_sem.at[s], device_id=dev_of(j), device_id_type=MESH)
            c.start()
            copies.append(c)
        for c in copies:
            c.wait()
        acc = src[piece(me)]
        for k in range(1, n):
            acc = acc + recv[k - 1]
        dst[...] = acc

    def gather_stage(src, n, me, dev_of, dst, piece):
        copies = []
        for k in range(1, n):
            j = (me + k) % n
            s = next_sem()
            c = pltpu.make_async_remote_copy(
                src_ref=src, dst_ref=dst.at[piece(me)], send_sem=send_sem.at[s],
                recv_sem=recv_sem.at[s], device_id=dev_of(j), device_id_type=MESH)
            c.start()
            copies.append((c, s, k))
        dst[piece(me)] = src[...]
        for c, s, k in copies:
            c.wait_send()
            j = (me + n - k) % n
            pltpu.make_async_remote_copy(
                src_ref=src, dst_ref=dst.at[piece(j)], send_sem=send_sem.at[s],
                recv_sem=recv_sem.at[s], device_id=dev_of(j), device_id_type=MESH).wait_recv()

    core_piece = lambda j: row_slice(j, rc)
    x_piece = lambda j: row_slice(j, rx)
    y_piece = lambda j: row_slice(j, ry)
    z_piece = lambda j: col_slice(j, cz)

    reduce_stage(x_ref, 2, core, core_dev, core_recv, core_sum, core_piece)
    reduce_stage(core_sum, nx, pos_a, x_dev, x_recv, x_sum, x_piece)
    if zcols > cols:
        y_pad[:, cols:] = jnp.zeros((ry, zcols - cols), jnp.float32)
    reduce_stage(x_sum, ny, pos_b, y_dev, y_recv, y_pad.at[:, pl.ds(0, cols)], y_piece)
    reduce_stage(y_pad, nh, zi, z_dev, z_recv, z_sum, z_piece)

    s = next_sem()
    c = pltpu.make_async_remote_copy(
        src_ref=z_sum, dst_ref=pair_recv, send_sem=send_sem.at[s], recv_sem=recv_sem.at[s],
        device_id=pair_dev, device_id_type=MESH)
    c.start()
    c.wait()
    z_full[...] = z_sum[...] + pair_recv[...]

    gather_stage(z_full, nh, zi, z_dev, y_out, z_piece)
    gather_stage(y_out.at[:, pl.ds(0, cols)], ny, pos_b, y_dev, x_out, y_piece)
    gather_stage(x_out, nx, pos_a, x_dev, core_out, x_piece)
    gather_stage(core_out, 2, core, core_dev, out_ref, core_piece)
    full = out_ref[...]
    part = jnp.sum(full * full, axis=0, keepdims=True)
    sq_ref[...] = jnp.broadcast_to(jnp.sum(part, axis=1, keepdims=True), sq_ref.shape)


def allreduce(g, tail, nx, ny, nz):
    assert nx == ny
    rows = g.shape[1]
    cols = g.shape[2] + tail.shape[1]
    nh = nz // 2
    rc = rows // 2
    rx = rc // nx
    ry = rx // ny
    zcols = 128 * nh * ((cols + 128 * nh - 1) // (128 * nh))
    cz = zcols // nh
    n_sems = 2 * (1 + (nx - 1) + (ny - 1) + (nh - 1)) + 1
    f32 = jnp.float32
    return pl.pallas_call(
        functools.partial(_allreduce_kernel, nx, ny, nz),
        out_shape=(jax.ShapeDtypeStruct((rows, cols), f32), jax.ShapeDtypeStruct((8, 128), f32)),
        in_specs=[pl.BlockSpec(memory_space=pltpu.VMEM)] * 2,
        out_specs=(pl.BlockSpec(memory_space=pltpu.VMEM),) * 2,
        scratch_shapes=[
            pltpu.VMEM((rows, cols), f32),
            pltpu.VMEM((1, rc, cols), f32),
            pltpu.VMEM((rc, cols), f32),
            pltpu.VMEM((nx - 1, rx, cols), f32),
            pltpu.VMEM((rx, cols), f32),
            pltpu.VMEM((ny - 1, ry, cols), f32),
            pltpu.VMEM((ry, zcols), f32),
            pltpu.VMEM((nh - 1, ry, cz), f32),
            pltpu.VMEM((ry, cz), f32),
            pltpu.VMEM((ry, cz), f32),
            pltpu.VMEM((ry, cz), f32),
            pltpu.VMEM((ry, zcols), f32),
            pltpu.VMEM((rx, cols), f32),
            pltpu.VMEM((rc, cols), f32),
            pltpu.SemaphoreType.DMA((n_sems,)),
            pltpu.SemaphoreType.DMA((n_sems,)),
        ],
        compiler_params=pltpu.CompilerParams(
            collective_id=0, has_side_effects=True, vmem_limit_bytes=48 * 1024 * 1024),
    )(g, tail)


def per_device(nx, ny, grads, vec_grads, weight, basis, moment, second, vectors, vec_moment, vec_second):
    shards = lax.axis_size("shard")
    width = grads.shape[-1]
    rows = weight.shape[0]
    cols = vectors.shape[1]
    vec_n = vectors.shape[0]
    me = lax.axis_index("shard")
    vec_local = vec_grads[0, 0, 0].astype(jnp.float32) + vec_grads[1, 0, 0].astype(jnp.float32)
    padded = 128 * ((width + vec_n + 127) // 128)
    pad = jnp.zeros((width, padded - width - vec_n), jnp.float32)
    tail = jnp.concatenate([vec_local.T, pad], axis=1)
    packed, sq = allreduce(grads[:, 0, 0], tail, nx, ny, shards)
    total = packed[:, :width]
    vec_total = packed[:, width:width + vec_n].T
    projected_all = matmul(total, basis)
    subspace = lax.dot_general(
        total,
        projected_all,
        (((0,), (0,)), ((), ())),
        precision=HIGH,
        preferred_element_type=jnp.float32,
    )
    squares = sq[0, 0]
    iterate = subspace / jnp.sqrt(jnp.sum(subspace * subspace) + 1e-06)
    for step in range(NS_STEPS):
        gram = matmul(iterate.T, iterate)
        iterate = 1.5 * iterate - 0.5 * matmul(iterate, gram)
    factor = 1.0 / jnp.maximum(jnp.sqrt(squares / (width * width + vec_total.size)), 1.0)
    projected = lax.dynamic_slice_in_dim(projected_all, me * rows, rows, axis=0)
    vec_sum = lax.dynamic_slice_in_dim(vec_total, me * cols, cols, axis=1)
    first_fix = 1.0 - 0.9**STEP
    second_fix = 1.0 - 0.999**STEP
    grad_low = factor * projected
    new_moment = 0.9 * moment + 0.1 * grad_low
    new_second = 0.999 * second + 0.001 * grad_low * grad_low
    normalized = new_moment / first_fix / (jnp.sqrt(new_second / second_fix) + 1e-08)
    full = lax.dot_general(
        normalized,
        basis,
        (((1,), (1,)), ((), ())),
        precision=HIGH,
        preferred_element_type=jnp.float32,
    )
    new_weight = weight - 0.001 * (0.25 * full + 0.01 * weight)
    vec_grad = factor * vec_sum
    new_vec_moment = 0.9 * vec_moment + 0.1 * vec_grad
    new_vec_second = 0.999 * vec_second + 0.001 * vec_grad * vec_grad
    vec_step = new_vec_moment / first_fix / (jnp.sqrt(new_vec_second / second_fix) + 1e-08)
    new_vectors = vectors - 0.001 * (vec_step + 0.01 * vectors)
    return (
        new_weight,
        full.astype(jnp.bfloat16),
        new_moment,
        new_second,
        iterate,
        new_vectors,
        new_vec_moment,
        new_vec_second,
    )


def solution(mesh, nx=None):
    if nx is None:
        nx = math.isqrt(mesh.shape["grp"] // 2)
    ny = mesh.shape["grp"] // 2 // nx
    return jax.shard_map(
        functools.partial(per_device, nx, ny),
        mesh=mesh,
        in_specs=(
            P(None, "grp", "shard", None, None),
            P(None, "grp", "shard", None, None),
            P("shard", None),
            P(),
            P("shard", None),
            P("shard", None),
            P(None, "shard"),
            P(None, "shard"),
            P(None, "shard"),
        ),
        out_specs=(
            P("shard", None),
            P("shard", None),
            P("shard", None),
            P("shard", None),
            P(),
            P(None, "shard"),
            P(None, "shard"),
            P(None, "shard"),
        ),
        check_vma=False,
    )
```

```python
import functools
import math

import jax
import jax.numpy as jnp
from jax import lax
from jax.experimental import pallas as pl
from jax.experimental.pallas import tpu as pltpu
from jax.sharding import PartitionSpec as P

NS_STEPS = 5
STEP = 100
MESH = pl.DeviceIdType.MESH


HIGH = lax.Precision.HIGH


def matmul(left, right):
    return jnp.dot(left, right, precision=HIGH, preferred_element_type=jnp.float32)


def _allreduce_kernel(nx, ny, nz, g_ref, tail_ref, out_ref, sq_ref, x_ref, core_recv, core_sum, x_recv, x_sum, y_recv,
                      y_pad, z_recv, z_sum, pair_recv, z_full, y_out, x_out, core_out, send_sem, recv_sem):
    rows, cols = x_ref.shape
    zcols = y_pad.shape[1]
    width = g_ref.shape[-1]
    x_ref[:, :width] = g_ref[0].astype(jnp.float32) + g_ref[1].astype(jnp.float32)
    x_ref[:, width:] = tail_ref[...]
    nh = nz // 2
    rc, rx, ry, cz = rows // 2, rows // 2 // nx, rows // 2 // nx // ny, zcols // nh
    g = lax.axis_index("grp")
    z = lax.axis_index("shard")
    core = g % 2
    xi = (g // 2) % nx
    yi = g // (2 * nx)
    zp = z % 2
    zi = z // 2

    def core_dev(_):
        return (g + 1 - 2 * core, z)

    stride_a = 2 + (2 * nx - 2) * core
    pos_a = xi + (yi - xi) * core
    stride_b = 2 * nx - (2 * nx - 2) * core
    pos_b = yi + (xi - yi) * core

    def x_dev(j):
        return (g + stride_a * (j - pos_a), z)

    def y_dev(j):
        return (g + stride_b * (j - pos_b), z)

    def z_dev(j):
        return (g, zp + 2 * j)

    pair_dev = (g, z + 1 - 2 * zp)

    barrier = pltpu.get_barrier_semaphore()
    peers = [core_dev(0), pair_dev]
    peers += [x_dev((pos_a + k) % nx) for k in range(1, nx)]
    peers += [y_dev((pos_b + k) % ny) for k in range(1, ny)]
    peers += [z_dev((zi + k) % nh) for k in range(1, nh)]
    for dev in peers:
        pl.semaphore_signal(barrier, inc=1, device_id=dev, device_id_type=MESH)
    pl.semaphore_wait(barrier, len(peers))

    counter = [0]

    def next_sem():
        s = counter[0]
        counter[0] += 1
        return s

    def row_slice(j, size):
        return pl.ds(pl.multiple_of(j * size, 8), size)

    def col_slice(j, size):
        return (slice(None), pl.ds(pl.multiple_of(j * size, 128), size))

    def reduce_stage(src, n, me, dev_of, recv, dst, piece):
        copies = []
        for k in range(1, n):
            j = (me + k) % n
            s = next_sem()
            c = pltpu.make_async_remote_copy(
                src_ref=src.at[piece(j)], dst_ref=recv.at[k - 1], send_sem=send_sem.at[s],
                recv_sem=recv_sem.at[s], device_id=dev_of(j), device_id_type=MESH)
            c.start()
            copies.append(c)
        for c in copies:
            c.wait()
        acc = src[piece(me)]
        for k in range(1, n):
            acc = acc + recv[k - 1]
        dst[...] = acc

    def gather_stage(src, n, me, dev_of, dst, piece):
        copies = []
        for k in range(1, n):
            j = (me + k) % n
            s = next_sem()
            c = pltpu.make_async_remote_copy(
                src_ref=src, dst_ref=dst.at[piece(me)], send_sem=send_sem.at[s],
                recv_sem=recv_sem.at[s], device_id=dev_of(j), device_id_type=MESH)
            c.start()
            copies.append((c, s, k))
        dst[piece(me)] = src[...]
        for c, s, k in copies:
            c.wait_send()
            j = (me + n - k) % n
            pltpu.make_async_remote_copy(
                src_ref=src, dst_ref=dst.at[piece(j)], send_sem=send_sem.at[s],
                recv_sem=recv_sem.at[s], device_id=dev_of(j), device_id_type=MESH).wait_recv()

    core_piece = lambda j: row_slice(j, rc)
    x_piece = lambda j: row_slice(j, rx)
    y_piece = lambda j: row_slice(j, ry)
    z_piece = lambda j: col_slice(j, cz)

    reduce_stage(x_ref, 2, core, core_dev, core_recv, core_sum, core_piece)
    reduce_stage(core_sum, nx, pos_a, x_dev, x_recv, x_sum, x_piece)
    if zcols > cols:
        y_pad[:, cols:] = jnp.zeros((ry, zcols - cols), jnp.float32)
    reduce_stage(x_sum, ny, pos_b, y_dev, y_recv, y_pad.at[:, pl.ds(0, cols)], y_piece)
    reduce_stage(y_pad, nh, zi, z_dev, z_recv, z_sum, z_piece)

    s = next_sem()
    c = pltpu.make_async_remote_copy(
        src_ref=z_sum, dst_ref=pair_recv, send_sem=send_sem.at[s], recv_sem=recv_sem.at[s],
        device_id=pair_dev, device_id_type=MESH)
    c.start()
    c.wait()
    z_full[...] = z_sum[...] + pair_recv[...]

    gather_stage(z_full, nh, zi, z_dev, y_out, z_piece)
    gather_stage(y_out.at[:, pl.ds(0, cols)], ny, pos_b, y_dev, x_out, y_piece)
    gather_stage(x_out, nx, pos_a, x_dev, core_out, x_piece)
    gather_stage(core_out, 2, core, core_dev, out_ref, core_piece)
    full = out_ref[...]
    part = jnp.sum(full * full, axis=0, keepdims=True)
    sq_ref[...] = jnp.broadcast_to(jnp.sum(part, axis=1, keepdims=True), sq_ref.shape)


def allreduce(g, tail, nx, ny, nz):
    assert nx == ny
    rows = g.shape[1]
    cols = g.shape[2] + tail.shape[1]
    nh = nz // 2
    rc = rows // 2
    rx = rc // nx
    ry = rx // ny
    zcols = 128 * nh * ((cols + 128 * nh - 1) // (128 * nh))
    cz = zcols // nh
    n_sems = 2 * (1 + (nx - 1) + (ny - 1) + (nh - 1)) + 1
    f32 = jnp.float32
    return pl.pallas_call(
        functools.partial(_allreduce_kernel, nx, ny, nz),
        out_shape=(jax.ShapeDtypeStruct((rows, cols), f32), jax.ShapeDtypeStruct((8, 128), f32)),
        in_specs=[pl.BlockSpec(memory_space=pltpu.VMEM)] * 2,
        out_specs=(pl.BlockSpec(memory_space=pltpu.VMEM),) * 2,
        scratch_shapes=[
            pltpu.VMEM((rows, cols), f32),
            pltpu.VMEM((1, rc, cols), f32),
            pltpu.VMEM((rc, cols), f32),
            pltpu.VMEM((nx - 1, rx, cols), f32),
            pltpu.VMEM((rx, cols), f32),
            pltpu.VMEM((ny - 1, ry, cols), f32),
            pltpu.VMEM((ry, zcols), f32),
            pltpu.VMEM((nh - 1, ry, cz), f32),
            pltpu.VMEM((ry, cz), f32),
            pltpu.VMEM((ry, cz), f32),
            pltpu.VMEM((ry, cz), f32),
            pltpu.VMEM((ry, zcols), f32),
            pltpu.VMEM((rx, cols), f32),
            pltpu.VMEM((rc, cols), f32),
            pltpu.SemaphoreType.DMA((n_sems,)),
            pltpu.SemaphoreType.DMA((n_sems,)),
        ],
        compiler_params=pltpu.CompilerParams(
            collective_id=0, has_side_effects=True, vmem_limit_bytes=48 * 1024 * 1024),
    )(g, tail)


def per_device(nx, ny, grads, vec_grads, weight, basis, moment, second, vectors, vec_moment, vec_second):
    shards = lax.axis_size("shard")
    width = grads.shape[-1]
    rows = weight.shape[0]
    cols = vectors.shape[1]
    vec_n = vectors.shape[0]
    me = lax.axis_index("shard")
    vec_local = vec_grads[0, 0, 0].astype(jnp.float32) + vec_grads[1, 0, 0].astype(jnp.float32)
    lanes = 128 * ((cols + 127) // 128)
    placed = vec_local.reshape(vec_n, shards, cols).transpose(1, 0, 2).reshape(shards * vec_n, cols)
    tail = jnp.pad(placed, ((0, width - shards * vec_n), (0, lanes - cols)))
    packed, sq = allreduce(grads[:, 0, 0], tail, nx, ny, shards)
    total = packed[:, :width]
    projected_all = matmul(total, basis)
    subspace = lax.dot_general(
        total,
        projected_all,
        (((0,), (0,)), ((), ())),
        precision=HIGH,
        preferred_element_type=jnp.float32,
    )
    squares = sq[0, 0]
    iterate = subspace / jnp.sqrt(jnp.sum(subspace * subspace) + 1e-06)
    for step in range(NS_STEPS):
        gram = matmul(iterate.T, iterate)
        iterate = 1.5 * iterate - 0.5 * matmul(iterate, gram)
    factor = 1.0 / jnp.maximum(jnp.sqrt(squares / (width * width + vec_n * width)), 1.0)
    projected = lax.dynamic_slice_in_dim(projected_all, me * rows, rows, axis=0)
    vec_sum = lax.dynamic_slice(packed, (me * vec_n, width), (vec_n, cols))
    first_fix = 1.0 - 0.9**STEP
    second_fix = 1.0 - 0.999**STEP
    grad_low = factor * projected
    new_moment = 0.9 * moment + 0.1 * grad_low
    new_second = 0.999 * second + 0.001 * grad_low * grad_low
    normalized = new_moment / first_fix / (jnp.sqrt(new_second / second_fix) + 1e-08)
    full = lax.dot_general(
        normalized,
        basis,
        (((1,), (1,)), ((), ())),
        precision=HIGH,
        preferred_element_type=jnp.float32,
    )
    new_weight = weight - 0.001 * (0.25 * full + 0.01 * weight)
    vec_grad = factor * vec_sum
    new_vec_moment = 0.9 * vec_moment + 0.1 * vec_grad
    new_vec_second = 0.999 * vec_second + 0.001 * vec_grad * vec_grad
    vec_step = new_vec_moment / first_fix / (jnp.sqrt(new_vec_second / second_fix) + 1e-08)
    new_vectors = vectors - 0.001 * (vec_step + 0.01 * vectors)
    return (
        new_weight,
        full.astype(jnp.bfloat16),
        new_moment,
        new_second,
        iterate,
        new_vectors,
        new_vec_moment,
        new_vec_second,
    )


def solution(mesh, nx=None):
    if nx is None:
        nx = math.isqrt(mesh.shape["grp"] // 2)
    ny = mesh.shape["grp"] // 2 // nx
    return jax.shard_map(
        functools.partial(per_device, nx, ny),
        mesh=mesh,
        in_specs=(
            P(None, "grp", "shard", None, None),
            P(None, "grp", "shard", None, None),
            P("shard", None),
            P(),
            P("shard", None),
            P("shard", None),
            P(None, "shard"),
            P(None, "shard"),
            P(None, "shard"),
        ),
        out_specs=(
            P("shard", None),
            P("shard", None),
            P("shard", None),
            P("shard", None),
            P(),
            P(None, "shard"),
            P(None, "shard"),
            P(None, "shard"),
        ),
        check_vma=False,
    )
```

```python
import functools
import math

import jax
import jax.numpy as jnp
from jax import lax
from jax.experimental import pallas as pl
from jax.experimental.pallas import tpu as pltpu
from jax.sharding import PartitionSpec as P

NS_STEPS = 5
STEP = 100
MESH = pl.DeviceIdType.MESH


HIGH = lax.Precision.HIGH


def matmul(left, right):
    return jnp.dot(left, right, precision=HIGH, preferred_element_type=jnp.float32)


def _allreduce_kernel(nx, ny, nz, g_ref, tail_ref, out_ref, sq_ref, x_ref, core_recv, core_sum, x_recv, x_sum, y_recv,
                      y_pad, z_recv, z_sum, pair_recv, z_full, y_out, x_out, core_out, send_sem, recv_sem):
    rows, cols = x_ref.shape
    zcols = y_pad.shape[1]
    width = g_ref.shape[-1]
    nh = nz // 2
    rc, rx, ry, cz = rows // 2, rows // 2 // nx, rows // 2 // nx // ny, zcols // nh
    g = lax.axis_index("grp")
    z = lax.axis_index("shard")
    core = g % 2
    xi = (g // 2) % nx
    yi = g // (2 * nx)
    zp = z % 2
    zi = z // 2

    def core_dev(_):
        return (g + 1 - 2 * core, z)

    stride_a = 2 + (2 * nx - 2) * core
    pos_a = xi + (yi - xi) * core
    stride_b = 2 * nx - (2 * nx - 2) * core
    pos_b = yi + (xi - yi) * core

    def x_dev(j):
        return (g + stride_a * (j - pos_a), z)

    def y_dev(j):
        return (g + stride_b * (j - pos_b), z)

    def z_dev(j):
        return (g, zp + 2 * j)

    pair_dev = (g, z + 1 - 2 * zp)

    barrier = pltpu.get_barrier_semaphore()
    peers = [core_dev(0), pair_dev]
    peers += [x_dev((pos_a + k) % nx) for k in range(1, nx)]
    peers += [y_dev((pos_b + k) % ny) for k in range(1, ny)]
    peers += [z_dev((zi + k) % nh) for k in range(1, nh)]
    for dev in peers:
        pl.semaphore_signal(barrier, inc=1, device_id=dev, device_id_type=MESH)

    def pack(j):
        r = pl.ds(pl.multiple_of(j * (rows // 2), 8), rows // 2)
        x_ref[r, :width] = g_ref[0, r, :].astype(jnp.float32) + g_ref[1, r, :].astype(jnp.float32)
        x_ref[r, width:] = tail_ref[r, :]


    counter = [0]

    def next_sem():
        s = counter[0]
        counter[0] += 1
        return s

    def row_slice(j, size):
        return pl.ds(pl.multiple_of(j * size, 8), size)

    def col_slice(j, size):
        return (slice(None), pl.ds(pl.multiple_of(j * size, 128), size))

    def reduce_stage(src, n, me, dev_of, recv, dst, piece):
        copies = []
        for k in range(1, n):
            j = (me + k) % n
            s = next_sem()
            c = pltpu.make_async_remote_copy(
                src_ref=src.at[piece(j)], dst_ref=recv.at[k - 1], send_sem=send_sem.at[s],
                recv_sem=recv_sem.at[s], device_id=dev_of(j), device_id_type=MESH)
            c.start()
            copies.append(c)
        for c in copies:
            c.wait()
        acc = src[piece(me)]
        for k in range(1, n):
            acc = acc + recv[k - 1]
        dst[...] = acc

    def gather_stage(src, n, me, dev_of, dst, piece):
        copies = []
        for k in range(1, n):
            j = (me + k) % n
            s = next_sem()
            c = pltpu.make_async_remote_copy(
                src_ref=src, dst_ref=dst.at[piece(me)], send_sem=send_sem.at[s],
                recv_sem=recv_sem.at[s], device_id=dev_of(j), device_id_type=MESH)
            c.start()
            copies.append((c, s, k))
        dst[piece(me)] = src[...]
        for c, s, k in copies:
            c.wait_send()
            j = (me + n - k) % n
            pltpu.make_async_remote_copy(
                src_ref=src, dst_ref=dst.at[piece(j)], send_sem=send_sem.at[s],
                recv_sem=recv_sem.at[s], device_id=dev_of(j), device_id_type=MESH).wait_recv()

    core_piece = lambda j: row_slice(j, rc)
    x_piece = lambda j: row_slice(j, rx)
    y_piece = lambda j: row_slice(j, ry)
    z_piece = lambda j: col_slice(j, cz)

    pack(1 - core)
    pl.semaphore_wait(barrier, len(peers))
    s = next_sem()
    c = pltpu.make_async_remote_copy(
        src_ref=x_ref.at[core_piece(1 - core)], dst_ref=core_recv.at[0], send_sem=send_sem.at[s],
        recv_sem=recv_sem.at[s], device_id=core_dev(0), device_id_type=MESH)
    c.start()
    pack(core)
    c.wait()
    core_sum[...] = x_ref[core_piece(core)] + core_recv[0]
    reduce_stage(core_sum, nx, pos_a, x_dev, x_recv, x_sum, x_piece)
    if zcols > cols:
        y_pad[:, cols:] = jnp.zeros((ry, zcols - cols), jnp.float32)
    reduce_stage(x_sum, ny, pos_b, y_dev, y_recv, y_pad.at[:, pl.ds(0, cols)], y_piece)
    reduce_stage(y_pad, nh, zi, z_dev, z_recv, z_sum, z_piece)

    s = next_sem()
    c = pltpu.make_async_remote_copy(
        src_ref=z_sum, dst_ref=pair_recv, send_sem=send_sem.at[s], recv_sem=recv_sem.at[s],
        device_id=pair_dev, device_id_type=MESH)
    c.start()
    c.wait()
    z_full[...] = z_sum[...] + pair_recv[...]

    gather_stage(z_full, nh, zi, z_dev, y_out, z_piece)
    gather_stage(y_out.at[:, pl.ds(0, cols)], ny, pos_b, y_dev, x_out, y_piece)
    gather_stage(x_out, nx, pos_a, x_dev, core_out, x_piece)
    s = next_sem()
    c = pltpu.make_async_remote_copy(
        src_ref=core_out, dst_ref=out_ref.at[core_piece(core)], send_sem=send_sem.at[s],
        recv_sem=recv_sem.at[s], device_id=core_dev(0), device_id_type=MESH)
    c.start()
    mine = core_out[...]
    out_ref[core_piece(core)] = mine
    own = jnp.sum(jnp.sum(mine * mine, axis=0, keepdims=True), axis=1, keepdims=True)
    c.wait_send()
    pltpu.make_async_remote_copy(
        src_ref=core_out, dst_ref=out_ref.at[core_piece(1 - core)], send_sem=send_sem.at[s],
        recv_sem=recv_sem.at[s], device_id=core_dev(0), device_id_type=MESH).wait_recv()
    other = out_ref[core_piece(1 - core)]
    rest = jnp.sum(jnp.sum(other * other, axis=0, keepdims=True), axis=1, keepdims=True)
    sq_ref[...] = jnp.broadcast_to(own + rest, sq_ref.shape)


def allreduce(g, tail, nx, ny, nz):
    assert nx == ny
    rows = g.shape[1]
    cols = g.shape[2] + tail.shape[1]
    nh = nz // 2
    rc = rows // 2
    rx = rc // nx
    ry = rx // ny
    zcols = 128 * nh * ((cols + 128 * nh - 1) // (128 * nh))
    cz = zcols // nh
    n_sems = 2 * (1 + (nx - 1) + (ny - 1) + (nh - 1)) + 1
    f32 = jnp.float32
    return pl.pallas_call(
        functools.partial(_allreduce_kernel, nx, ny, nz),
        out_shape=(jax.ShapeDtypeStruct((rows, cols), f32), jax.ShapeDtypeStruct((8, 128), f32)),
        in_specs=[pl.BlockSpec(memory_space=pltpu.VMEM)] * 2,
        out_specs=(pl.BlockSpec(memory_space=pltpu.VMEM),) * 2,
        scratch_shapes=[
            pltpu.VMEM((rows, cols), f32),
            pltpu.VMEM((1, rc, cols), f32),
            pltpu.VMEM((rc, cols), f32),
            pltpu.VMEM((nx - 1, rx, cols), f32),
            pltpu.VMEM((rx, cols), f32),
            pltpu.VMEM((ny - 1, ry, cols), f32),
            pltpu.VMEM((ry, zcols), f32),
            pltpu.VMEM((nh - 1, ry, cz), f32),
            pltpu.VMEM((ry, cz), f32),
            pltpu.VMEM((ry, cz), f32),
            pltpu.VMEM((ry, cz), f32),
            pltpu.VMEM((ry, zcols), f32),
            pltpu.VMEM((rx, cols), f32),
            pltpu.VMEM((rc, cols), f32),
            pltpu.SemaphoreType.DMA((n_sems,)),
            pltpu.SemaphoreType.DMA((n_sems,)),
        ],
        compiler_params=pltpu.CompilerParams(
            collective_id=0, has_side_effects=True, vmem_limit_bytes=48 * 1024 * 1024),
    )(g, tail)


def per_device(nx, ny, grads, vec_grads, weight, basis, moment, second, vectors, vec_moment, vec_second):
    shards = lax.axis_size("shard")
    width = grads.shape[-1]
    rows = weight.shape[0]
    cols = vectors.shape[1]
    vec_n = vectors.shape[0]
    me = lax.axis_index("shard")
    vec_local = vec_grads[0, 0, 0].astype(jnp.float32) + vec_grads[1, 0, 0].astype(jnp.float32)
    lanes = 128 * ((cols + 127) // 128)
    placed = vec_local.reshape(vec_n, shards, cols).transpose(1, 0, 2).reshape(shards * vec_n, cols)
    tail = jnp.pad(placed, ((0, width - shards * vec_n), (0, lanes - cols)))
    packed, sq = allreduce(grads[:, 0, 0], tail, nx, ny, shards)
    total = packed[:, :width]
    projected_all = matmul(total, basis)
    subspace = lax.dot_general(
        total,
        projected_all,
        (((0,), (0,)), ((), ())),
        precision=HIGH,
        preferred_element_type=jnp.float32,
    )
    squares = sq[0, 0]
    iterate = subspace / jnp.sqrt(jnp.sum(subspace * subspace) + 1e-06)
    for step in range(NS_STEPS):
        gram = matmul(iterate.T, iterate)
        iterate = 1.5 * iterate - 0.5 * matmul(iterate, gram)
    factor = 1.0 / jnp.maximum(jnp.sqrt(squares / (width * width + vec_n * width)), 1.0)
    projected = lax.dynamic_slice_in_dim(projected_all, me * rows, rows, axis=0)
    vec_sum = lax.dynamic_slice(packed, (me * vec_n, width), (vec_n, cols))
    first_fix = 1.0 - 0.9**STEP
    second_fix = 1.0 - 0.999**STEP
    grad_low = factor * projected
    new_moment = 0.9 * moment + 0.1 * grad_low
    new_second = 0.999 * second + 0.001 * grad_low * grad_low
    normalized = new_moment / first_fix / (jnp.sqrt(new_second / second_fix) + 1e-08)
    full = lax.dot_general(
        normalized,
        basis,
        (((1,), (1,)), ((), ())),
        precision=HIGH,
        preferred_element_type=jnp.float32,
    )
    new_weight = weight - 0.001 * (0.25 * full + 0.01 * weight)
    vec_grad = factor * vec_sum
    new_vec_moment = 0.9 * vec_moment + 0.1 * vec_grad
    new_vec_second = 0.999 * vec_second + 0.001 * vec_grad * vec_grad
    vec_step = new_vec_moment / first_fix / (jnp.sqrt(new_vec_second / second_fix) + 1e-08)
    new_vectors = vectors - 0.001 * (vec_step + 0.01 * vectors)
    return (
        new_weight,
        full.astype(jnp.bfloat16),
        new_moment,
        new_second,
        iterate,
        new_vectors,
        new_vec_moment,
        new_vec_second,
    )


def solution(mesh, nx=None):
    if nx is None:
        nx = math.isqrt(mesh.shape["grp"] // 2)
    ny = mesh.shape["grp"] // 2 // nx
    return jax.shard_map(
        functools.partial(per_device, nx, ny),
        mesh=mesh,
        in_specs=(
            P(None, "grp", "shard", None, None),
            P(None, "grp", "shard", None, None),
            P("shard", None),
            P(),
            P("shard", None),
            P("shard", None),
            P(None, "shard"),
            P(None, "shard"),
            P(None, "shard"),
        ),
        out_specs=(
            P("shard", None),
            P("shard", None),
            P("shard", None),
            P("shard", None),
            P(),
            P(None, "shard"),
            P(None, "shard"),
            P(None, "shard"),
        ),
        check_vma=False,
    )
```

```python
import functools
import math

import jax
import jax.numpy as jnp
from jax import lax
from jax.experimental import pallas as pl
from jax.experimental.pallas import tpu as pltpu
from jax.sharding import PartitionSpec as P

NS_STEPS = 5
STEP = 100
MESH = pl.DeviceIdType.MESH


HIGH = lax.Precision.HIGH


def matmul(left, right):
    return jnp.dot(left, right, precision=HIGH, preferred_element_type=jnp.float32)


def _allreduce_kernel(nx, ny, nz, g_hbm, tail_ref, out_ref, sq_ref, g_ref, in_sem, x_ref, core_recv, core_sum, x_recv, x_sum, y_recv,
                      y_pad, z_recv, z_sum, pair_recv, z_full, y_out, x_out, core_out, send_sem, recv_sem):
    rows, cols = x_ref.shape
    zcols = y_pad.shape[1]
    width = g_ref.shape[-1]
    nh = nz // 2
    rc, rx, ry, cz = rows // 2, rows // 2 // nx, rows // 2 // nx // ny, zcols // nh
    g = lax.axis_index("grp")
    z = lax.axis_index("shard")
    core = g % 2
    xi = (g // 2) % nx
    yi = g // (2 * nx)
    zp = z % 2
    zi = z // 2

    def core_dev(_):
        return (g + 1 - 2 * core, z)

    stride_a = 2 + (2 * nx - 2) * core
    pos_a = xi + (yi - xi) * core
    stride_b = 2 * nx - (2 * nx - 2) * core
    pos_b = yi + (xi - yi) * core

    def x_dev(j):
        return (g + stride_a * (j - pos_a), z)

    def y_dev(j):
        return (g + stride_b * (j - pos_b), z)

    def z_dev(j):
        return (g, zp + 2 * j)

    pair_dev = (g, z + 1 - 2 * zp)

    half = rows // 2
    loads = []
    for j in (1 - core, core):
        r = pl.ds(pl.multiple_of(j * half, 8), half)
        load = pltpu.make_async_copy(g_hbm.at[:, r, :], g_ref.at[:, r, :], in_sem.at[len(loads)])
        load.start()
        loads.append(load)

    barrier = pltpu.get_barrier_semaphore()
    peers = [core_dev(0), pair_dev]
    peers += [x_dev((pos_a + k) % nx) for k in range(1, nx)]
    peers += [y_dev((pos_b + k) % ny) for k in range(1, ny)]
    peers += [z_dev((zi + k) % nh) for k in range(1, nh)]
    for dev in peers:
        pl.semaphore_signal(barrier, inc=1, device_id=dev, device_id_type=MESH)

    def pack(j):
        r = pl.ds(pl.multiple_of(j * (rows // 2), 8), rows // 2)
        x_ref[r, :width] = g_ref[0, r, :].astype(jnp.float32) + g_ref[1, r, :].astype(jnp.float32)
        x_ref[r, width:] = tail_ref[r, :]


    counter = [0]

    def next_sem():
        s = counter[0]
        counter[0] += 1
        return s

    def row_slice(j, size):
        return pl.ds(pl.multiple_of(j * size, 8), size)

    def col_slice(j, size):
        return (slice(None), pl.ds(pl.multiple_of(j * size, 128), size))

    def reduce_stage(src, n, me, dev_of, recv, dst, piece):
        copies = []
        for k in range(1, n):
            j = (me + k) % n
            s = next_sem()
            c = pltpu.make_async_remote_copy(
                src_ref=src.at[piece(j)], dst_ref=recv.at[k - 1], send_sem=send_sem.at[s],
                recv_sem=recv_sem.at[s], device_id=dev_of(j), device_id_type=MESH)
            c.start()
            copies.append(c)
        for c in copies:
            c.wait()
        acc = src[piece(me)]
        for k in range(1, n):
            acc = acc + recv[k - 1]
        dst[...] = acc

    def gather_stage(src, n, me, dev_of, dst, piece):
        copies = []
        for k in range(1, n):
            j = (me + k) % n
            s = next_sem()
            c = pltpu.make_async_remote_copy(
                src_ref=src, dst_ref=dst.at[piece(me)], send_sem=send_sem.at[s],
                recv_sem=recv_sem.at[s], device_id=dev_of(j), device_id_type=MESH)
            c.start()
            copies.append((c, s, k))
        dst[piece(me)] = src[...]
        for c, s, k in copies:
            c.wait_send()
            j = (me + n - k) % n
            pltpu.make_async_remote_copy(
                src_ref=src, dst_ref=dst.at[piece(j)], send_sem=send_sem.at[s],
                recv_sem=recv_sem.at[s], device_id=dev_of(j), device_id_type=MESH).wait_recv()

    core_piece = lambda j: row_slice(j, rc)
    x_piece = lambda j: row_slice(j, rx)
    y_piece = lambda j: row_slice(j, ry)
    z_piece = lambda j: col_slice(j, cz)

    loads[0].wait()
    pack(1 - core)
    pl.semaphore_wait(barrier, len(peers))
    s = next_sem()
    c = pltpu.make_async_remote_copy(
        src_ref=x_ref.at[core_piece(1 - core)], dst_ref=core_recv.at[0], send_sem=send_sem.at[s],
        recv_sem=recv_sem.at[s], device_id=core_dev(0), device_id_type=MESH)
    c.start()
    loads[1].wait()
    pack(core)
    c.wait()
    core_sum[...] = x_ref[core_piece(core)] + core_recv[0]
    reduce_stage(core_sum, nx, pos_a, x_dev, x_recv, x_sum, x_piece)
    if zcols > cols:
        y_pad[:, cols:] = jnp.zeros((ry, zcols - cols), jnp.float32)
    reduce_stage(x_sum, ny, pos_b, y_dev, y_recv, y_pad.at[:, pl.ds(0, cols)], y_piece)
    reduce_stage(y_pad, nh, zi, z_dev, z_recv, z_sum, z_piece)

    s = next_sem()
    c = pltpu.make_async_remote_copy(
        src_ref=z_sum, dst_ref=pair_recv, send_sem=send_sem.at[s], recv_sem=recv_sem.at[s],
        device_id=pair_dev, device_id_type=MESH)
    c.start()
    c.wait()
    z_full[...] = z_sum[...] + pair_recv[...]

    gather_stage(z_full, nh, zi, z_dev, y_out, z_piece)
    gather_stage(y_out.at[:, pl.ds(0, cols)], ny, pos_b, y_dev, x_out, y_piece)
    gather_stage(x_out, nx, pos_a, x_dev, core_out, x_piece)
    s = next_sem()
    c = pltpu.make_async_remote_copy(
        src_ref=core_out, dst_ref=out_ref.at[core_piece(core)], send_sem=send_sem.at[s],
        recv_sem=recv_sem.at[s], device_id=core_dev(0), device_id_type=MESH)
    c.start()
    mine = core_out[...]
    out_ref[core_piece(core)] = mine
    own = jnp.sum(jnp.sum(mine * mine, axis=0, keepdims=True), axis=1, keepdims=True)
    c.wait_send()
    pltpu.make_async_remote_copy(
        src_ref=core_out, dst_ref=out_ref.at[core_piece(1 - core)], send_sem=send_sem.at[s],
        recv_sem=recv_sem.at[s], device_id=core_dev(0), device_id_type=MESH).wait_recv()
    other = out_ref[core_piece(1 - core)]
    rest = jnp.sum(jnp.sum(other * other, axis=0, keepdims=True), axis=1, keepdims=True)
    sq_ref[...] = jnp.broadcast_to(own + rest, sq_ref.shape)


def allreduce(g, tail, nx, ny, nz):
    assert nx == ny
    rows = g.shape[1]
    cols = g.shape[2] + tail.shape[1]
    nh = nz // 2
    rc = rows // 2
    rx = rc // nx
    ry = rx // ny
    zcols = 128 * nh * ((cols + 128 * nh - 1) // (128 * nh))
    cz = zcols // nh
    n_sems = 2 * (1 + (nx - 1) + (ny - 1) + (nh - 1)) + 1
    f32 = jnp.float32
    return pl.pallas_call(
        functools.partial(_allreduce_kernel, nx, ny, nz),
        out_shape=(jax.ShapeDtypeStruct((rows, cols), f32), jax.ShapeDtypeStruct((8, 128), f32)),
        in_specs=[pl.BlockSpec(memory_space=pl.ANY), pl.BlockSpec(memory_space=pltpu.VMEM)],
        out_specs=(pl.BlockSpec(memory_space=pltpu.VMEM),) * 2,
        scratch_shapes=[
            pltpu.VMEM(g.shape, g.dtype),
            pltpu.SemaphoreType.DMA((2,)),
            pltpu.VMEM((rows, cols), f32),
            pltpu.VMEM((1, rc, cols), f32),
            pltpu.VMEM((rc, cols), f32),
            pltpu.VMEM((nx - 1, rx, cols), f32),
            pltpu.VMEM((rx, cols), f32),
            pltpu.VMEM((ny - 1, ry, cols), f32),
            pltpu.VMEM((ry, zcols), f32),
            pltpu.VMEM((nh - 1, ry, cz), f32),
            pltpu.VMEM((ry, cz), f32),
            pltpu.VMEM((ry, cz), f32),
            pltpu.VMEM((ry, cz), f32),
            pltpu.VMEM((ry, zcols), f32),
            pltpu.VMEM((rx, cols), f32),
            pltpu.VMEM((rc, cols), f32),
            pltpu.SemaphoreType.DMA((n_sems,)),
            pltpu.SemaphoreType.DMA((n_sems,)),
        ],
        compiler_params=pltpu.CompilerParams(
            collective_id=0, has_side_effects=True, vmem_limit_bytes=48 * 1024 * 1024),
    )(g, tail)


def per_device(nx, ny, grads, vec_grads, weight, basis, moment, second, vectors, vec_moment, vec_second):
    shards = lax.axis_size("shard")
    width = grads.shape[-1]
    rows = weight.shape[0]
    cols = vectors.shape[1]
    vec_n = vectors.shape[0]
    me = lax.axis_index("shard")
    vec_local = vec_grads[0, 0, 0].astype(jnp.float32) + vec_grads[1, 0, 0].astype(jnp.float32)
    lanes = 128 * ((cols + 127) // 128)
    placed = vec_local.reshape(vec_n, shards, cols).transpose(1, 0, 2).reshape(shards * vec_n, cols)
    tail = jnp.pad(placed, ((0, width - shards * vec_n), (0, lanes - cols)))
    packed, sq = allreduce(grads[:, 0, 0], tail, nx, ny, shards)
    total = packed[:, :width]
    projected_all = matmul(total, basis)
    subspace = lax.dot_general(
        total,
        projected_all,
        (((0,), (0,)), ((), ())),
        precision=HIGH,
        preferred_element_type=jnp.float32,
    )
    squares = sq[0, 0]
    iterate = subspace / jnp.sqrt(jnp.sum(subspace * subspace) + 1e-06)
    for step in range(NS_STEPS):
        gram = matmul(iterate.T, iterate)
        iterate = 1.5 * iterate - 0.5 * matmul(iterate, gram)
    factor = 1.0 / jnp.maximum(jnp.sqrt(squares / (width * width + vec_n * width)), 1.0)
    projected = lax.dynamic_slice_in_dim(projected_all, me * rows, rows, axis=0)
    vec_sum = lax.dynamic_slice(packed, (me * vec_n, width), (vec_n, cols))
    first_fix = 1.0 - 0.9**STEP
    second_fix = 1.0 - 0.999**STEP
    grad_low = factor * projected
    new_moment = 0.9 * moment + 0.1 * grad_low
    new_second = 0.999 * second + 0.001 * grad_low * grad_low
    normalized = new_moment / first_fix / (jnp.sqrt(new_second / second_fix) + 1e-08)
    full = lax.dot_general(
        normalized,
        basis,
        (((1,), (1,)), ((), ())),
        precision=HIGH,
        preferred_element_type=jnp.float32,
    )
    new_weight = weight - 0.001 * (0.25 * full + 0.01 * weight)
    vec_grad = factor * vec_sum
    new_vec_moment = 0.9 * vec_moment + 0.1 * vec_grad
    new_vec_second = 0.999 * vec_second + 0.001 * vec_grad * vec_grad
    vec_step = new_vec_moment / first_fix / (jnp.sqrt(new_vec_second / second_fix) + 1e-08)
    new_vectors = vectors - 0.001 * (vec_step + 0.01 * vectors)
    return (
        new_weight,
        full.astype(jnp.bfloat16),
        new_moment,
        new_second,
        iterate,
        new_vectors,
        new_vec_moment,
        new_vec_second,
    )


def solution(mesh, nx=None):
    if nx is None:
        nx = math.isqrt(mesh.shape["grp"] // 2)
    ny = mesh.shape["grp"] // 2 // nx
    return jax.shard_map(
        functools.partial(per_device, nx, ny),
        mesh=mesh,
        in_specs=(
            P(None, "grp", "shard", None, None),
            P(None, "grp", "shard", None, None),
            P("shard", None),
            P(),
            P("shard", None),
            P("shard", None),
            P(None, "shard"),
            P(None, "shard"),
            P(None, "shard"),
        ),
        out_specs=(
            P("shard", None),
            P("shard", None),
            P("shard", None),
            P("shard", None),
            P(),
            P(None, "shard"),
            P(None, "shard"),
            P(None, "shard"),
        ),
        check_vma=False,
    )
```

```python
import functools
import math

import jax
import jax.numpy as jnp
from jax import lax
from jax.experimental import pallas as pl
from jax.experimental.pallas import tpu as pltpu
from jax.sharding import PartitionSpec as P

NS_STEPS = 5
STEP = 100
MESH = pl.DeviceIdType.MESH


HIGH = lax.Precision.HIGH


def matmul(left, right):
    return jnp.dot(left, right, precision=HIGH, preferred_element_type=jnp.float32)


def _allreduce_kernel(nx, ny, nz, g_hbm, tail_ref, out_ref, sq_ref, g_ref, in_sem, x_ref, core_recv, core_sum, x_recv, x_sum, y_recv,
                      y_pad, z_recv, z_sum, pair_recv, z_full, y_out, x_out, core_out, send_sem, recv_sem):
    rows, cols = x_ref.shape
    zcols = y_pad.shape[1]
    width = g_ref.shape[-1]
    nh = nz // 2
    rc, rx, ry, cz = rows // 2, rows // 2 // nx, rows // 2 // nx // ny, zcols // nh
    g = lax.axis_index("grp")
    z = lax.axis_index("shard")
    core = g % 2
    xi = (g // 2) % nx
    yi = g // (2 * nx)
    zp = z % 2
    zi = z // 2

    def core_dev(_):
        return (g + 1 - 2 * core, z)

    stride_a = 2 + (2 * nx - 2) * core
    pos_a = xi + (yi - xi) * core
    stride_b = 2 * nx - (2 * nx - 2) * core
    pos_b = yi + (xi - yi) * core

    def x_dev(j):
        return (g + stride_a * (j - pos_a), z)

    def y_dev(j):
        return (g + stride_b * (j - pos_b), z)

    def z_dev(j):
        return (g, zp + 2 * j)

    pair_dev = (g, z + 1 - 2 * zp)

    half = rows // 2
    loads = []
    for j in (1 - core, core):
        r = pl.ds(pl.multiple_of(j * half, 8), half)
        load = pltpu.make_async_copy(g_hbm.at[:, r, :], g_ref.at[:, r, :], in_sem.at[len(loads)])
        load.start()
        loads.append(load)

    barrier = pltpu.get_barrier_semaphore()
    peers = [core_dev(0), pair_dev]
    peers += [x_dev((pos_a + k) % nx) for k in range(1, nx)]
    peers += [y_dev((pos_b + k) % ny) for k in range(1, ny)]
    peers += [z_dev((zi + k) % nh) for k in range(1, nh)]
    for dev in peers:
        pl.semaphore_signal(barrier, inc=1, device_id=dev, device_id_type=MESH)

    def pack(j):
        r = pl.ds(pl.multiple_of(j * (rows // 2), 8), rows // 2)
        x_ref[r, :width] = g_ref[0, r, :].astype(jnp.float32) + g_ref[1, r, :].astype(jnp.float32)
        x_ref[r, width:] = tail_ref[r, :]


    counter = [0]

    def next_sem():
        s = counter[0]
        counter[0] += 1
        return s

    def row_slice(j, size):
        return pl.ds(pl.multiple_of(j * size, 8), size)

    def col_slice(j, size):
        return (slice(None), pl.ds(pl.multiple_of(j * size, 128), size))

    def reduce_stage(src, n, me, dev_of, recv, dst, piece):
        copies = []
        for k in range(1, n):
            j = (me + k) % n
            s = next_sem()
            c = pltpu.make_async_remote_copy(
                src_ref=src.at[piece(j)], dst_ref=recv.at[k - 1], send_sem=send_sem.at[s],
                recv_sem=recv_sem.at[s], device_id=dev_of(j), device_id_type=MESH)
            c.start()
            copies.append(c)
        for c in copies:
            c.wait()
        acc = src[piece(me)]
        for k in range(1, n):
            acc = acc + recv[k - 1]
        dst[...] = acc

    def gather_stage(src, n, me, dev_of, dst, piece):
        copies = []
        for k in range(1, n):
            j = (me + k) % n
            s = next_sem()
            c = pltpu.make_async_remote_copy(
                src_ref=src, dst_ref=dst.at[piece(me)], send_sem=send_sem.at[s],
                recv_sem=recv_sem.at[s], device_id=dev_of(j), device_id_type=MESH)
            c.start()
            copies.append((c, s, k))
        dst[piece(me)] = src[...]
        for c, s, k in copies:
            c.wait_send()
            j = (me + n - k) % n
            pltpu.make_async_remote_copy(
                src_ref=src, dst_ref=dst.at[piece(j)], send_sem=send_sem.at[s],
                recv_sem=recv_sem.at[s], device_id=dev_of(j), device_id_type=MESH).wait_recv()

    core_piece = lambda j: row_slice(j, rc)
    x_piece = lambda j: row_slice(j, rx)
    y_piece = lambda j: row_slice(j, ry)
    z_piece = lambda j: col_slice(j, cz)

    loads[0].wait()
    pack(1 - core)
    pl.semaphore_wait(barrier, len(peers))
    s = next_sem()
    c = pltpu.make_async_remote_copy(
        src_ref=x_ref.at[core_piece(1 - core)], dst_ref=core_recv.at[0], send_sem=send_sem.at[s],
        recv_sem=recv_sem.at[s], device_id=core_dev(0), device_id_type=MESH)
    c.start()
    loads[1].wait()
    pack(core)
    c.wait()
    core_sum[...] = x_ref[core_piece(core)] + core_recv[0]
    reduce_stage(core_sum, nx, pos_a, x_dev, x_recv, x_sum, x_piece)
    if zcols > cols:
        y_pad[:, cols:] = jnp.zeros((ry, zcols - cols), jnp.float32)
    reduce_stage(x_sum, ny, pos_b, y_dev, y_recv, y_pad.at[:, pl.ds(0, cols)], y_piece)
    reduce_stage(y_pad, nh, zi, z_dev, z_recv, z_sum, z_piece)

    s = next_sem()
    c = pltpu.make_async_remote_copy(
        src_ref=z_sum, dst_ref=pair_recv, send_sem=send_sem.at[s], recv_sem=recv_sem.at[s],
        device_id=pair_dev, device_id_type=MESH)
    c.start()
    c.wait()
    z_full[...] = z_sum[...] + pair_recv[...]

    gather_stage(z_full, nh, zi, z_dev, y_out, z_piece)
    gather_stage(y_out.at[:, pl.ds(0, cols)], ny, pos_b, y_dev, x_out, y_piece)
    gather_stage(x_out, nx, pos_a, x_dev, core_out, x_piece)
    s = next_sem()
    c = pltpu.make_async_remote_copy(
        src_ref=core_out, dst_ref=out_ref.at[core_piece(core)], send_sem=send_sem.at[s],
        recv_sem=recv_sem.at[s], device_id=core_dev(0), device_id_type=MESH)
    c.start()
    mine = core_out[...]
    out_ref[core_piece(core)] = mine
    own = jnp.sum(jnp.sum(mine * mine, axis=0, keepdims=True), axis=1, keepdims=True)
    c.wait_send()
    pltpu.make_async_remote_copy(
        src_ref=core_out, dst_ref=out_ref.at[core_piece(1 - core)], send_sem=send_sem.at[s],
        recv_sem=recv_sem.at[s], device_id=core_dev(0), device_id_type=MESH).wait_recv()
    other = out_ref[core_piece(1 - core)]
    rest = jnp.sum(jnp.sum(other * other, axis=0, keepdims=True), axis=1, keepdims=True)
    sq_ref[...] = jnp.broadcast_to(own + rest, sq_ref.shape)


def allreduce(g, tail, nx, ny, nz):
    assert nx == ny
    rows = g.shape[1]
    cols = g.shape[2] + tail.shape[1]
    nh = nz // 2
    rc = rows // 2
    rx = rc // nx
    ry = rx // ny
    zcols = 128 * nh * ((cols + 128 * nh - 1) // (128 * nh))
    cz = zcols // nh
    n_sems = 2 * (1 + (nx - 1) + (ny - 1) + (nh - 1)) + 1
    f32 = jnp.float32
    return pl.pallas_call(
        functools.partial(_allreduce_kernel, nx, ny, nz),
        out_shape=(jax.ShapeDtypeStruct((rows, cols), f32), jax.ShapeDtypeStruct((8, 128), f32)),
        in_specs=[pl.BlockSpec(memory_space=pltpu.HBM), pl.BlockSpec(memory_space=pltpu.VMEM)],
        out_specs=(pl.BlockSpec(memory_space=pltpu.VMEM),) * 2,
        scratch_shapes=[
            pltpu.VMEM(g.shape, g.dtype),
            pltpu.SemaphoreType.DMA((2,)),
            pltpu.VMEM((rows, cols), f32),
            pltpu.VMEM((1, rc, cols), f32),
            pltpu.VMEM((rc, cols), f32),
            pltpu.VMEM((nx - 1, rx, cols), f32),
            pltpu.VMEM((rx, cols), f32),
            pltpu.VMEM((ny - 1, ry, cols), f32),
            pltpu.VMEM((ry, zcols), f32),
            pltpu.VMEM((nh - 1, ry, cz), f32),
            pltpu.VMEM((ry, cz), f32),
            pltpu.VMEM((ry, cz), f32),
            pltpu.VMEM((ry, cz), f32),
            pltpu.VMEM((ry, zcols), f32),
            pltpu.VMEM((rx, cols), f32),
            pltpu.VMEM((rc, cols), f32),
            pltpu.SemaphoreType.DMA((n_sems,)),
            pltpu.SemaphoreType.DMA((n_sems,)),
        ],
        compiler_params=pltpu.CompilerParams(
            collective_id=0, has_side_effects=True),
    )(g, tail)


def per_device(nx, ny, grads, vec_grads, weight, basis, moment, second, vectors, vec_moment, vec_second):
    shards = lax.axis_size("shard")
    width = grads.shape[-1]
    rows = weight.shape[0]
    cols = vectors.shape[1]
    vec_n = vectors.shape[0]
    me = lax.axis_index("shard")
    vec_local = vec_grads[0, 0, 0].astype(jnp.float32) + vec_grads[1, 0, 0].astype(jnp.float32)
    lanes = 128 * ((cols + 127) // 128)
    placed = vec_local.reshape(vec_n, shards, cols).transpose(1, 0, 2).reshape(shards * vec_n, cols)
    tail = jnp.pad(placed, ((0, width - shards * vec_n), (0, lanes - cols)))
    packed, sq = allreduce(grads[:, 0, 0], tail, nx, ny, shards)
    total = packed[:, :width]
    projected_all = matmul(total, basis)
    subspace = lax.dot_general(
        total,
        projected_all,
        (((0,), (0,)), ((), ())),
        precision=HIGH,
        preferred_element_type=jnp.float32,
    )
    squares = sq[0, 0]
    iterate = subspace / jnp.sqrt(jnp.sum(subspace * subspace) + 1e-06)
    for step in range(NS_STEPS):
        gram = matmul(iterate.T, iterate)
        iterate = 1.5 * iterate - 0.5 * matmul(iterate, gram)
    factor = 1.0 / jnp.maximum(jnp.sqrt(squares / (width * width + vec_n * width)), 1.0)
    projected = lax.dynamic_slice_in_dim(projected_all, me * rows, rows, axis=0)
    vec_sum = lax.dynamic_slice(packed, (me * vec_n, width), (vec_n, cols))
    first_fix = 1.0 - 0.9**STEP
    second_fix = 1.0 - 0.999**STEP
    grad_low = factor * projected
    new_moment = 0.9 * moment + 0.1 * grad_low
    new_second = 0.999 * second + 0.001 * grad_low * grad_low
    normalized = new_moment / first_fix / (jnp.sqrt(new_second / second_fix) + 1e-08)
    full = lax.dot_general(
        normalized,
        basis,
        (((1,), (1,)), ((), ())),
        precision=HIGH,
        preferred_element_type=jnp.float32,
    )
    new_weight = weight - 0.001 * (0.25 * full + 0.01 * weight)
    vec_grad = factor * vec_sum
    new_vec_moment = 0.9 * vec_moment + 0.1 * vec_grad
    new_vec_second = 0.999 * vec_second + 0.001 * vec_grad * vec_grad
    vec_step = new_vec_moment / first_fix / (jnp.sqrt(new_vec_second / second_fix) + 1e-08)
    new_vectors = vectors - 0.001 * (vec_step + 0.01 * vectors)
    return (
        new_weight,
        full.astype(jnp.bfloat16),
        new_moment,
        new_second,
        iterate,
        new_vectors,
        new_vec_moment,
        new_vec_second,
    )


def solution(mesh, nx=None):
    if nx is None:
        nx = math.isqrt(mesh.shape["grp"] // 2)
    ny = mesh.shape["grp"] // 2 // nx
    return jax.shard_map(
        functools.partial(per_device, nx, ny),
        mesh=mesh,
        in_specs=(
            P(None, "grp", "shard", None, None),
            P(None, "grp", "shard", None, None),
            P("shard", None),
            P(),
            P("shard", None),
            P("shard", None),
            P(None, "shard"),
            P(None, "shard"),
            P(None, "shard"),
        ),
        out_specs=(
            P("shard", None),
            P("shard", None),
            P("shard", None),
            P("shard", None),
            P(),
            P(None, "shard"),
            P(None, "shard"),
            P(None, "shard"),
        ),
        check_vma=False,
    )
```

```python
import functools
import math

import jax
import jax.numpy as jnp
from jax import lax
from jax.experimental import pallas as pl
from jax.experimental.pallas import tpu as pltpu
from jax.sharding import PartitionSpec as P

NS_STEPS = 5
STEP = 100
MESH = pl.DeviceIdType.MESH


HIGH = lax.Precision.HIGH


def matmul(left, right):
    return jnp.dot(left, right, precision=HIGH, preferred_element_type=jnp.float32)


def _allreduce_kernel(nx, ny, nz, g_ref, tail_ref, out_ref, sq_ref, x_ref, core_recv, core_sum, x_recv, x_sum, y_recv,
                      y_pad, z_recv, z_sum, pair_recv, z_full, y_out, x_out, core_out, send_sem, recv_sem):
    rows, cols = x_ref.shape
    zcols = y_pad.shape[1]
    width = g_ref.shape[-1]
    nh = nz // 2
    rc, rx, ry, cz = rows // 2, rows // 2 // nx, rows // 2 // nx // ny, zcols // nh
    g = lax.axis_index("grp")
    z = lax.axis_index("shard")
    core = g % 2
    xi = (g // 2) % nx
    yi = g // (2 * nx)
    zp = z % 2
    zi = z // 2

    def core_dev(_):
        return (g + 1 - 2 * core, z)

    stride_a = 2 + (2 * nx - 2) * core
    pos_a = xi + (yi - xi) * core
    stride_b = 2 * nx - (2 * nx - 2) * core
    pos_b = yi + (xi - yi) * core

    def x_dev(j):
        return (g + stride_a * (j - pos_a), z)

    def y_dev(j):
        return (g + stride_b * (j - pos_b), z)

    def z_dev(j):
        return (g, zp + 2 * j)

    pair_dev = (g, z + 1 - 2 * zp)

    barrier = pltpu.get_barrier_semaphore()
    peers = [core_dev(0), pair_dev]
    peers += [x_dev((pos_a + k) % nx) for k in range(1, nx)]
    peers += [y_dev((pos_b + k) % ny) for k in range(1, ny)]
    peers += [z_dev((zi + k) % nh) for k in range(1, nh)]
    for dev in peers:
        pl.semaphore_signal(barrier, inc=1, device_id=dev, device_id_type=MESH)

    def pack(j):
        r = pl.ds(pl.multiple_of(j * (rows // 2), 8), rows // 2)
        x_ref[r, :width] = g_ref[0, r, :].astype(jnp.float32) + g_ref[1, r, :].astype(jnp.float32)
        x_ref[r, width:] = tail_ref[r, :]


    counter = [0]

    def next_sem():
        s = counter[0]
        counter[0] += 1
        return s

    def row_slice(j, size):
        return pl.ds(pl.multiple_of(j * size, 8), size)

    def col_slice(j, size):
        return (slice(None), pl.ds(pl.multiple_of(j * size, 128), size))

    def reduce_stage(src, n, me, dev_of, recv, dst, piece):
        copies = []
        for k in range(1, n):
            j = (me + k) % n
            s = next_sem()
            c = pltpu.make_async_remote_copy(
                src_ref=src.at[piece(j)], dst_ref=recv.at[k - 1], send_sem=send_sem.at[s],
                recv_sem=recv_sem.at[s], device_id=dev_of(j), device_id_type=MESH)
            c.start()
            copies.append(c)
        for c in copies:
            c.wait()
        acc = src[piece(me)]
        for k in range(1, n):
            acc = acc + recv[k - 1]
        dst[...] = acc

    def gather_stage(src, n, me, dev_of, dst, piece):
        copies = []
        for k in range(1, n):
            j = (me + k) % n
            s = next_sem()
            c = pltpu.make_async_remote_copy(
                src_ref=src, dst_ref=dst.at[piece(me)], send_sem=send_sem.at[s],
                recv_sem=recv_sem.at[s], device_id=dev_of(j), device_id_type=MESH)
            c.start()
            copies.append((c, s, k))
        dst[piece(me)] = src[...]
        for c, s, k in copies:
            c.wait_send()
            j = (me + n - k) % n
            pltpu.make_async_remote_copy(
                src_ref=src, dst_ref=dst.at[piece(j)], send_sem=send_sem.at[s],
                recv_sem=recv_sem.at[s], device_id=dev_of(j), device_id_type=MESH).wait_recv()

    core_piece = lambda j: row_slice(j, rc)
    x_piece = lambda j: row_slice(j, rx)
    y_piece = lambda j: row_slice(j, ry)
    z_piece = lambda j: col_slice(j, cz)

    pack(1 - core)
    pl.semaphore_wait(barrier, len(peers))
    s = next_sem()
    c = pltpu.make_async_remote_copy(
        src_ref=x_ref.at[core_piece(1 - core)], dst_ref=core_recv.at[0], send_sem=send_sem.at[s],
        recv_sem=recv_sem.at[s], device_id=core_dev(0), device_id_type=MESH)
    c.start()
    pack(core)
    c.wait()
    core_sum[...] = x_ref[core_piece(core)] + core_recv[0]
    reduce_stage(core_sum, nx, pos_a, x_dev, x_recv, x_sum, x_piece)
    if zcols > cols:
        y_pad[:, cols:] = jnp.zeros((ry, zcols - cols), jnp.float32)
    reduce_stage(x_sum, ny, pos_b, y_dev, y_recv, y_pad.at[:, pl.ds(0, cols)], y_piece)
    reduce_stage(y_pad, nh, zi, z_dev, z_recv, z_sum, z_piece)

    s = next_sem()
    c = pltpu.make_async_remote_copy(
        src_ref=z_sum, dst_ref=pair_recv, send_sem=send_sem.at[s], recv_sem=recv_sem.at[s],
        device_id=pair_dev, device_id_type=MESH)
    c.start()
    c.wait()
    z_full[...] = z_sum[...] + pair_recv[...]

    gather_stage(z_full, nh, zi, z_dev, y_out, z_piece)
    gather_stage(y_out.at[:, pl.ds(0, cols)], ny, pos_b, y_dev, x_out, y_piece)
    half_off = core * rc
    other_off = (1 - core) * rc

    def out_rows(off, j):
        return pl.ds(pl.multiple_of(off + j * rx, 8), rx)

    a_sends = []
    for k in range(1, nx):
        j = (pos_a + k) % nx
        s = next_sem()
        c = pltpu.make_async_remote_copy(
            src_ref=x_out, dst_ref=core_out.at[x_piece(pos_a)], send_sem=send_sem.at[s],
            recv_sem=recv_sem.at[s], device_id=x_dev(j), device_id_type=MESH)
        c.start()
        a_sends.append((c, s, k))
    fwd = []
    s = next_sem()
    c = pltpu.make_async_remote_copy(
        src_ref=x_out, dst_ref=out_ref.at[out_rows(half_off, pos_a)], send_sem=send_sem.at[s],
        recv_sem=recv_sem.at[s], device_id=core_dev(0), device_id_type=MESH)
    c.start()
    fwd.append((c, s, pos_a))
    core_out[x_piece(pos_a)] = x_out[...]
    for c, s, k in a_sends:
        j = (pos_a + nx - k) % nx
        pltpu.make_async_remote_copy(
            src_ref=x_out, dst_ref=core_out.at[x_piece(j)], send_sem=send_sem.at[s],
            recv_sem=recv_sem.at[s], device_id=x_dev(j), device_id_type=MESH).wait_recv()
        s2 = next_sem()
        c2 = pltpu.make_async_remote_copy(
            src_ref=core_out.at[x_piece(j)], dst_ref=out_ref.at[out_rows(half_off, j)], send_sem=send_sem.at[s2],
            recv_sem=recv_sem.at[s2], device_id=core_dev(0), device_id_type=MESH)
        c2.start()
        fwd.append((c2, s2, j))
    for c, s, k in a_sends:
        c.wait_send()
    mine = core_out[...]
    out_ref[core_piece(core)] = mine
    own = jnp.sum(jnp.sum(mine * mine, axis=0, keepdims=True), axis=1, keepdims=True)
    for c, s, j in fwd:
        c.wait_send()
    partner_pos = xi + (yi - xi) * (1 - core)
    for idx, (c, s, j) in enumerate(fwd):
        jp = (partner_pos + nx - idx) % nx
        pltpu.make_async_remote_copy(
            src_ref=x_out, dst_ref=out_ref.at[out_rows(other_off, jp)], send_sem=send_sem.at[s],
            recv_sem=recv_sem.at[s], device_id=core_dev(0), device_id_type=MESH).wait_recv()
    other = out_ref[core_piece(1 - core)]
    rest = jnp.sum(jnp.sum(other * other, axis=0, keepdims=True), axis=1, keepdims=True)
    sq_ref[...] = jnp.broadcast_to(own + rest, sq_ref.shape)


def allreduce(g, tail, nx, ny, nz):
    assert nx == ny
    rows = g.shape[1]
    cols = g.shape[2] + tail.shape[1]
    nh = nz // 2
    rc = rows // 2
    rx = rc // nx
    ry = rx // ny
    zcols = 128 * nh * ((cols + 128 * nh - 1) // (128 * nh))
    cz = zcols // nh
    n_sems = 2 * (1 + (nx - 1) + (ny - 1) + (nh - 1)) + 1 + (nx - 1)
    f32 = jnp.float32
    return pl.pallas_call(
        functools.partial(_allreduce_kernel, nx, ny, nz),
        out_shape=(jax.ShapeDtypeStruct((rows, cols), f32), jax.ShapeDtypeStruct((8, 128), f32)),
        in_specs=[pl.BlockSpec(memory_space=pltpu.VMEM)] * 2,
        out_specs=(pl.BlockSpec(memory_space=pltpu.VMEM),) * 2,
        scratch_shapes=[
            pltpu.VMEM((rows, cols), f32),
            pltpu.VMEM((1, rc, cols), f32),
            pltpu.VMEM((rc, cols), f32),
            pltpu.VMEM((nx - 1, rx, cols), f32),
            pltpu.VMEM((rx, cols), f32),
            pltpu.VMEM((ny - 1, ry, cols), f32),
            pltpu.VMEM((ry, zcols), f32),
            pltpu.VMEM((nh - 1, ry, cz), f32),
            pltpu.VMEM((ry, cz), f32),
            pltpu.VMEM((ry, cz), f32),
            pltpu.VMEM((ry, cz), f32),
            pltpu.VMEM((ry, zcols), f32),
            pltpu.VMEM((rx, cols), f32),
            pltpu.VMEM((rc, cols), f32),
            pltpu.SemaphoreType.DMA((n_sems,)),
            pltpu.SemaphoreType.DMA((n_sems,)),
        ],
        compiler_params=pltpu.CompilerParams(
            collective_id=0, has_side_effects=True, vmem_limit_bytes=48 * 1024 * 1024),
    )(g, tail)


def per_device(nx, ny, grads, vec_grads, weight, basis, moment, second, vectors, vec_moment, vec_second):
    shards = lax.axis_size("shard")
    width = grads.shape[-1]
    rows = weight.shape[0]
    cols = vectors.shape[1]
    vec_n = vectors.shape[0]
    me = lax.axis_index("shard")
    vec_local = vec_grads[0, 0, 0].astype(jnp.float32) + vec_grads[1, 0, 0].astype(jnp.float32)
    lanes = 128 * ((cols + 127) // 128)
    placed = vec_local.reshape(vec_n, shards, cols).transpose(1, 0, 2).reshape(shards * vec_n, cols)
    tail = jnp.pad(placed, ((0, width - shards * vec_n), (0, lanes - cols)))
    packed, sq = allreduce(grads[:, 0, 0], tail, nx, ny, shards)
    total = packed[:, :width]
    projected_all = matmul(total, basis)
    subspace = lax.dot_general(
        total,
        projected_all,
        (((0,), (0,)), ((), ())),
        precision=HIGH,
        preferred_element_type=jnp.float32,
    )
    squares = sq[0, 0]
    iterate = subspace / jnp.sqrt(jnp.sum(subspace * subspace) + 1e-06)
    for step in range(NS_STEPS):
        gram = matmul(iterate.T, iterate)
        iterate = 1.5 * iterate - 0.5 * matmul(iterate, gram)
    factor = 1.0 / jnp.maximum(jnp.sqrt(squares / (width * width + vec_n * width)), 1.0)
    projected = lax.dynamic_slice_in_dim(projected_all, me * rows, rows, axis=0)
    vec_sum = lax.dynamic_slice(packed, (me * vec_n, width), (vec_n, cols))
    first_fix = 1.0 - 0.9**STEP
    second_fix = 1.0 - 0.999**STEP
    grad_low = factor * projected
    new_moment = 0.9 * moment + 0.1 * grad_low
    new_second = 0.999 * second + 0.001 * grad_low * grad_low
    normalized = new_moment / first_fix / (jnp.sqrt(new_second / second_fix) + 1e-08)
    full = lax.dot_general(
        normalized,
        basis,
        (((1,), (1,)), ((), ())),
        precision=HIGH,
        preferred_element_type=jnp.float32,
    )
    new_weight = weight - 0.001 * (0.25 * full + 0.01 * weight)
    vec_grad = factor * vec_sum
    new_vec_moment = 0.9 * vec_moment + 0.1 * vec_grad
    new_vec_second = 0.999 * vec_second + 0.001 * vec_grad * vec_grad
    vec_step = new_vec_moment / first_fix / (jnp.sqrt(new_vec_second / second_fix) + 1e-08)
    new_vectors = vectors - 0.001 * (vec_step + 0.01 * vectors)
    return (
        new_weight,
        full.astype(jnp.bfloat16),
        new_moment,
        new_second,
        iterate,
        new_vectors,
        new_vec_moment,
        new_vec_second,
    )


def solution(mesh, nx=None):
    if nx is None:
        nx = math.isqrt(mesh.shape["grp"] // 2)
    ny = mesh.shape["grp"] // 2 // nx
    return jax.shard_map(
        functools.partial(per_device, nx, ny),
        mesh=mesh,
        in_specs=(
            P(None, "grp", "shard", None, None),
            P(None, "grp", "shard", None, None),
            P("shard", None),
            P(),
            P("shard", None),
            P("shard", None),
            P(None, "shard"),
            P(None, "shard"),
            P(None, "shard"),
        ),
        out_specs=(
            P("shard", None),
            P("shard", None),
            P("shard", None),
            P("shard", None),
            P(),
            P(None, "shard"),
            P(None, "shard"),
            P(None, "shard"),
        ),
        check_vma=False,
    )
```

```python
import functools
import math

import jax
import jax.numpy as jnp
from jax import lax
from jax.experimental import pallas as pl
from jax.experimental.pallas import tpu as pltpu
from jax.sharding import PartitionSpec as P

NS_STEPS = 5
STEP = 100
MESH = pl.DeviceIdType.MESH


HIGH = lax.Precision.HIGH


def matmul(left, right):
    return jnp.dot(left, right, precision=HIGH, preferred_element_type=jnp.float32)


def _allreduce_kernel(nx, ny, nz, g_ref, tail_ref, out_ref, sq_ref, x_ref, core_recv, core_sum, x_recv, x_sum, y_recv,
                      y_pad, z_recv, z_sum, pair_recv, z_full, y_out, x_out, core_out, send_sem, recv_sem):
    rows, cols = x_ref.shape
    zcols = y_pad.shape[1]
    width = g_ref.shape[-1]
    nh = nz // 2
    rc, rx, ry, cz = rows // 2, rows // 2 // nx, rows // 2 // nx // ny, zcols // nh
    g = lax.axis_index("grp")
    z = lax.axis_index("shard")
    core = g % 2
    xi = (g // 2) % nx
    yi = g // (2 * nx)
    zp = z % 2
    zi = z // 2

    def core_dev(_):
        return (g + 1 - 2 * core, z)

    stride_a = 2 + (2 * nx - 2) * core
    pos_a = xi + (yi - xi) * core
    stride_b = 2 * nx - (2 * nx - 2) * core
    pos_b = yi + (xi - yi) * core

    def x_dev(j):
        return (g + stride_a * (j - pos_a), z)

    def y_dev(j):
        return (g + stride_b * (j - pos_b), z)

    def z_dev(j):
        return (g, zp + 2 * j)

    pair_dev = (g, z + 1 - 2 * zp)

    barrier = pltpu.get_barrier_semaphore()
    peers = [core_dev(0), pair_dev]
    peers += [x_dev((pos_a + k) % nx) for k in range(1, nx)]
    peers += [y_dev((pos_b + k) % ny) for k in range(1, ny)]
    peers += [z_dev((zi + k) % nh) for k in range(1, nh)]
    for dev in peers:
        pl.semaphore_signal(barrier, inc=1, device_id=dev, device_id_type=MESH)

    def pack(j):
        r = pl.ds(pl.multiple_of(j * (rows // 2), 8), rows // 2)
        x_ref[r, :width] = g_ref[0, r, :].astype(jnp.float32) + g_ref[1, r, :].astype(jnp.float32)
        x_ref[r, width:] = tail_ref[r, :]


    counter = [0]

    def next_sem():
        s = counter[0]
        counter[0] += 1
        return s

    def row_slice(j, size):
        return pl.ds(pl.multiple_of(j * size, 8), size)

    def col_slice(j, size):
        return (slice(None), pl.ds(pl.multiple_of(j * size, 128), size))

    def far_first(n):
        return sorted(range(1, n), key=lambda k: (-min(k, n - k), k))

    def reduce_stage(src, n, me, dev_of, recv, dst, piece):
        copies = []
        for k in far_first(n):
            j = (me + k) % n
            s = next_sem()
            c = pltpu.make_async_remote_copy(
                src_ref=src.at[piece(j)], dst_ref=recv.at[k - 1], send_sem=send_sem.at[s],
                recv_sem=recv_sem.at[s], device_id=dev_of(j), device_id_type=MESH)
            c.start()
            copies.append(c)
        for c in copies:
            c.wait()
        acc = src[piece(me)]
        for k in range(1, n):
            acc = acc + recv[k - 1]
        dst[...] = acc

    def gather_stage(src, n, me, dev_of, dst, piece):
        copies = []
        for k in far_first(n):
            j = (me + k) % n
            s = next_sem()
            c = pltpu.make_async_remote_copy(
                src_ref=src, dst_ref=dst.at[piece(me)], send_sem=send_sem.at[s],
                recv_sem=recv_sem.at[s], device_id=dev_of(j), device_id_type=MESH)
            c.start()
            copies.append((c, s, k))
        dst[piece(me)] = src[...]
        for c, s, k in copies:
            c.wait_send()
            j = (me + n - k) % n
            pltpu.make_async_remote_copy(
                src_ref=src, dst_ref=dst.at[piece(j)], send_sem=send_sem.at[s],
                recv_sem=recv_sem.at[s], device_id=dev_of(j), device_id_type=MESH).wait_recv()

    core_piece = lambda j: row_slice(j, rc)
    x_piece = lambda j: row_slice(j, rx)
    y_piece = lambda j: row_slice(j, ry)
    z_piece = lambda j: col_slice(j, cz)

    pack(1 - core)
    pl.semaphore_wait(barrier, len(peers))
    s = next_sem()
    c = pltpu.make_async_remote_copy(
        src_ref=x_ref.at[core_piece(1 - core)], dst_ref=core_recv.at[0], send_sem=send_sem.at[s],
        recv_sem=recv_sem.at[s], device_id=core_dev(0), device_id_type=MESH)
    c.start()
    pack(core)
    c.wait()
    core_sum[...] = x_ref[core_piece(core)] + core_recv[0]
    reduce_stage(core_sum, nx, pos_a, x_dev, x_recv, x_sum, x_piece)
    if zcols > cols:
        y_pad[:, cols:] = jnp.zeros((ry, zcols - cols), jnp.float32)
    reduce_stage(x_sum, ny, pos_b, y_dev, y_recv, y_pad.at[:, pl.ds(0, cols)], y_piece)
    reduce_stage(y_pad, nh, zi, z_dev, z_recv, z_sum, z_piece)

    s = next_sem()
    c = pltpu.make_async_remote_copy(
        src_ref=z_sum, dst_ref=pair_recv, send_sem=send_sem.at[s], recv_sem=recv_sem.at[s],
        device_id=pair_dev, device_id_type=MESH)
    c.start()
    c.wait()
    z_full[...] = z_sum[...] + pair_recv[...]

    gather_stage(z_full, nh, zi, z_dev, y_out, z_piece)
    gather_stage(y_out.at[:, pl.ds(0, cols)], ny, pos_b, y_dev, x_out, y_piece)
    half_off = core * rc
    other_off = (1 - core) * rc

    def out_rows(off, j):
        return pl.ds(pl.multiple_of(off + j * rx, 8), rx)

    a_sends = []
    for k in range(1, nx):
        j = (pos_a + k) % nx
        s = next_sem()
        c = pltpu.make_async_remote_copy(
            src_ref=x_out, dst_ref=core_out.at[x_piece(pos_a)], send_sem=send_sem.at[s],
            recv_sem=recv_sem.at[s], device_id=x_dev(j), device_id_type=MESH)
        c.start()
        a_sends.append((c, s, k))
    fwd = []
    s = next_sem()
    c = pltpu.make_async_remote_copy(
        src_ref=x_out, dst_ref=out_ref.at[out_rows(half_off, pos_a)], send_sem=send_sem.at[s],
        recv_sem=recv_sem.at[s], device_id=core_dev(0), device_id_type=MESH)
    c.start()
    fwd.append((c, s, pos_a))
    core_out[x_piece(pos_a)] = x_out[...]
    for c, s, k in a_sends:
        j = (pos_a + nx - k) % nx
        pltpu.make_async_remote_copy(
            src_ref=x_out, dst_ref=core_out.at[x_piece(j)], send_sem=send_sem.at[s],
            recv_sem=recv_sem.at[s], device_id=x_dev(j), device_id_type=MESH).wait_recv()
        s2 = next_sem()
        c2 = pltpu.make_async_remote_copy(
            src_ref=core_out.at[x_piece(j)], dst_ref=out_ref.at[out_rows(half_off, j)], send_sem=send_sem.at[s2],
            recv_sem=recv_sem.at[s2], device_id=core_dev(0), device_id_type=MESH)
        c2.start()
        fwd.append((c2, s2, j))
    for c, s, k in a_sends:
        c.wait_send()
    mine = core_out[...]
    out_ref[core_piece(core)] = mine
    own = jnp.sum(jnp.sum(mine * mine, axis=0, keepdims=True), axis=1, keepdims=True)
    for c, s, j in fwd:
        c.wait_send()
    partner_pos = xi + (yi - xi) * (1 - core)
    for idx, (c, s, j) in enumerate(fwd):
        jp = (partner_pos + nx - idx) % nx
        pltpu.make_async_remote_copy(
            src_ref=x_out, dst_ref=out_ref.at[out_rows(other_off, jp)], send_sem=send_sem.at[s],
            recv_sem=recv_sem.at[s], device_id=core_dev(0), device_id_type=MESH).wait_recv()
    other = out_ref[core_piece(1 - core)]
    rest = jnp.sum(jnp.sum(other * other, axis=0, keepdims=True), axis=1, keepdims=True)
    sq_ref[...] = jnp.broadcast_to(own + rest, sq_ref.shape)


def allreduce(g, tail, nx, ny, nz):
    assert nx == ny
    rows = g.shape[1]
    cols = g.shape[2] + tail.shape[1]
    nh = nz // 2
    rc = rows // 2
    rx = rc // nx
    ry = rx // ny
    zcols = 128 * nh * ((cols + 128 * nh - 1) // (128 * nh))
    cz = zcols // nh
    n_sems = 2 * (1 + (nx - 1) + (ny - 1) + (nh - 1)) + 1 + (nx - 1)
    f32 = jnp.float32
    return pl.pallas_call(
        functools.partial(_allreduce_kernel, nx, ny, nz),
        out_shape=(jax.ShapeDtypeStruct((rows, cols), f32), jax.ShapeDtypeStruct((8, 128), f32)),
        in_specs=[pl.BlockSpec(memory_space=pltpu.VMEM)] * 2,
        out_specs=(pl.BlockSpec(memory_space=pltpu.VMEM),) * 2,
        scratch_shapes=[
            pltpu.VMEM((rows, cols), f32),
            pltpu.VMEM((1, rc, cols), f32),
            pltpu.VMEM((rc, cols), f32),
            pltpu.VMEM((nx - 1, rx, cols), f32),
            pltpu.VMEM((rx, cols), f32),
            pltpu.VMEM((ny - 1, ry, cols), f32),
            pltpu.VMEM((ry, zcols), f32),
            pltpu.VMEM((nh - 1, ry, cz), f32),
            pltpu.VMEM((ry, cz), f32),
            pltpu.VMEM((ry, cz), f32),
            pltpu.VMEM((ry, cz), f32),
            pltpu.VMEM((ry, zcols), f32),
            pltpu.VMEM((rx, cols), f32),
            pltpu.VMEM((rc, cols), f32),
            pltpu.SemaphoreType.DMA((n_sems,)),
            pltpu.SemaphoreType.DMA((n_sems,)),
        ],
        compiler_params=pltpu.CompilerParams(
            collective_id=0, has_side_effects=True, vmem_limit_bytes=48 * 1024 * 1024),
    )(g, tail)


def per_device(nx, ny, grads, vec_grads, weight, basis, moment, second, vectors, vec_moment, vec_second):
    shards = lax.axis_size("shard")
    width = grads.shape[-1]
    rows = weight.shape[0]
    cols = vectors.shape[1]
    vec_n = vectors.shape[0]
    me = lax.axis_index("shard")
    vec_local = vec_grads[0, 0, 0].astype(jnp.float32) + vec_grads[1, 0, 0].astype(jnp.float32)
    lanes = 128 * ((cols + 127) // 128)
    placed = vec_local.reshape(vec_n, shards, cols).transpose(1, 0, 2).reshape(shards * vec_n, cols)
    tail = jnp.pad(placed, ((0, width - shards * vec_n), (0, lanes - cols)))
    packed, sq = allreduce(grads[:, 0, 0], tail, nx, ny, shards)
    total = packed[:, :width]
    projected_all = matmul(total, basis)
    subspace = lax.dot_general(
        total,
        projected_all,
        (((0,), (0,)), ((), ())),
        precision=HIGH,
        preferred_element_type=jnp.float32,
    )
    squares = sq[0, 0]
    iterate = subspace / jnp.sqrt(jnp.sum(subspace * subspace) + 1e-06)
    for step in range(NS_STEPS):
        gram = matmul(iterate.T, iterate)
        iterate = 1.5 * iterate - 0.5 * matmul(iterate, gram)
    factor = 1.0 / jnp.maximum(jnp.sqrt(squares / (width * width + vec_n * width)), 1.0)
    projected = lax.dynamic_slice_in_dim(projected_all, me * rows, rows, axis=0)
    vec_sum = lax.dynamic_slice(packed, (me * vec_n, width), (vec_n, cols))
    first_fix = 1.0 - 0.9**STEP
    second_fix = 1.0 - 0.999**STEP
    grad_low = factor * projected
    new_moment = 0.9 * moment + 0.1 * grad_low
    new_second = 0.999 * second + 0.001 * grad_low * grad_low
    normalized = new_moment / first_fix / (jnp.sqrt(new_second / second_fix) + 1e-08)
    full = lax.dot_general(
        normalized,
        basis,
        (((1,), (1,)), ((), ())),
        precision=HIGH,
        preferred_element_type=jnp.float32,
    )
    new_weight = weight - 0.001 * (0.25 * full + 0.01 * weight)
    vec_grad = factor * vec_sum
    new_vec_moment = 0.9 * vec_moment + 0.1 * vec_grad
    new_vec_second = 0.999 * vec_second + 0.001 * vec_grad * vec_grad
    vec_step = new_vec_moment / first_fix / (jnp.sqrt(new_vec_second / second_fix) + 1e-08)
    new_vectors = vectors - 0.001 * (vec_step + 0.01 * vectors)
    return (
        new_weight,
        full.astype(jnp.bfloat16),
        new_moment,
        new_second,
        iterate,
        new_vectors,
        new_vec_moment,
        new_vec_second,
    )


def solution(mesh, nx=None):
    if nx is None:
        nx = math.isqrt(mesh.shape["grp"] // 2)
    ny = mesh.shape["grp"] // 2 // nx
    return jax.shard_map(
        functools.partial(per_device, nx, ny),
        mesh=mesh,
        in_specs=(
            P(None, "grp", "shard", None, None),
            P(None, "grp", "shard", None, None),
            P("shard", None),
            P(),
            P("shard", None),
            P("shard", None),
            P(None, "shard"),
            P(None, "shard"),
            P(None, "shard"),
        ),
        out_specs=(
            P("shard", None),
            P("shard", None),
            P("shard", None),
            P("shard", None),
            P(),
            P(None, "shard"),
            P(None, "shard"),
            P(None, "shard"),
        ),
        check_vma=False,
    )
```

```python
import functools
import math

import jax
import jax.numpy as jnp
from jax import lax
from jax.experimental import pallas as pl
from jax.experimental.pallas import tpu as pltpu
from jax.sharding import PartitionSpec as P

NS_STEPS = 5
STEP = 100
MESH = pl.DeviceIdType.MESH


HIGH = lax.Precision.HIGH


def matmul(left, right):
    return jnp.dot(left, right, precision=HIGH, preferred_element_type=jnp.float32)


def _allreduce_kernel(nx, ny, nz, g_ref, tail_ref, out_ref, sq_ref, x_ref, core_recv, core_sum, x_recv, x_sum, y_recv,
                      y_pad, z_recv, z_sum, pair_recv, z_full, y_out, x_out, core_out, send_sem, recv_sem):
    rows, cols = x_ref.shape
    zcols = y_pad.shape[1]
    width = g_ref.shape[-1]
    nh = nz // 2
    rc, rx, ry, cz = rows // 2, rows // 2 // nx, rows // 2 // nx // ny, zcols // nh
    g = lax.axis_index("grp")
    z = lax.axis_index("shard")
    core = g % 2
    xi = (g // 2) % nx
    yi = g // (2 * nx)
    zp = z % 2
    zi = z // 2

    def core_dev(_):
        return (g + 1 - 2 * core, z)

    stride_a = 2 + (2 * nx - 2) * core
    pos_a = xi + (yi - xi) * core
    stride_b = 2 * nx - (2 * nx - 2) * core
    pos_b = yi + (xi - yi) * core

    def x_dev(j):
        return (g + stride_a * (j - pos_a), z)

    def y_dev(j):
        return (g + stride_b * (j - pos_b), z)

    def z_dev(j):
        return (g, zp + 2 * j)

    pair_dev = (g, z + 1 - 2 * zp)

    barrier = pltpu.get_barrier_semaphore()
    peers = [core_dev(0), pair_dev]
    peers += [x_dev((pos_a + k) % nx) for k in range(1, nx)]
    peers += [y_dev((pos_b + k) % ny) for k in range(1, ny)]
    peers += [z_dev((zi + k) % nh) for k in range(1, nh)]
    for dev in peers:
        pl.semaphore_signal(barrier, inc=1, device_id=dev, device_id_type=MESH)

    def pack(j):
        r = pl.ds(pl.multiple_of(j * (rows // 2), 8), rows // 2)
        x_ref[r, :width] = g_ref[0, r, :].astype(jnp.float32) + g_ref[1, r, :].astype(jnp.float32)
        x_ref[r, width:] = tail_ref[r, :]


    counter = [0]

    def next_sem():
        s = counter[0]
        counter[0] += 1
        return s

    def row_slice(j, size):
        return pl.ds(pl.multiple_of(j * size, 8), size)

    def col_slice(j, size):
        return (slice(None), pl.ds(pl.multiple_of(j * size, 128), size))

    def far_first(n):
        return sorted(range(1, n), key=lambda k: (-min(k, n - k), k))

    def reduce_stage(src, n, me, dev_of, recv, dst, piece):
        copies = []
        for k in far_first(n):
            j = (me + k) % n
            s = next_sem()
            c = pltpu.make_async_remote_copy(
                src_ref=src.at[piece(j)], dst_ref=recv.at[k - 1], send_sem=send_sem.at[s],
                recv_sem=recv_sem.at[s], device_id=dev_of(j), device_id_type=MESH)
            c.start()
            copies.append(c)
        for c in copies:
            c.wait()
        acc = src[piece(me)]
        for k in range(1, n):
            acc = acc + recv[k - 1]
        dst[...] = acc

    def gather_stage(src, n, me, dev_of, dst, piece):
        copies = []
        for k in far_first(n):
            j = (me + k) % n
            s = next_sem()
            c = pltpu.make_async_remote_copy(
                src_ref=src, dst_ref=dst.at[piece(me)], send_sem=send_sem.at[s],
                recv_sem=recv_sem.at[s], device_id=dev_of(j), device_id_type=MESH)
            c.start()
            copies.append((c, s, k))
        dst[piece(me)] = src[...]
        for c, s, k in copies:
            c.wait_send()
            j = (me + n - k) % n
            pltpu.make_async_remote_copy(
                src_ref=src, dst_ref=dst.at[piece(j)], send_sem=send_sem.at[s],
                recv_sem=recv_sem.at[s], device_id=dev_of(j), device_id_type=MESH).wait_recv()

    core_piece = lambda j: row_slice(j, rc)
    x_piece = lambda j: row_slice(j, rx)
    y_piece = lambda j: row_slice(j, ry)
    z_piece = lambda j: col_slice(j, cz)

    pack(1 - core)
    pl.semaphore_wait(barrier, len(peers))
    s = next_sem()
    c = pltpu.make_async_remote_copy(
        src_ref=x_ref.at[core_piece(1 - core)], dst_ref=core_recv.at[0], send_sem=send_sem.at[s],
        recv_sem=recv_sem.at[s], device_id=core_dev(0), device_id_type=MESH)
    c.start()
    pack(core)
    c.wait()
    core_sum[...] = x_ref[core_piece(core)] + core_recv[0]
    reduce_stage(core_sum, nx, pos_a, x_dev, x_recv, x_sum, x_piece)
    if zcols > cols:
        y_pad[:, cols:] = jnp.zeros((ry, zcols - cols), jnp.float32)
    reduce_stage(x_sum, ny, pos_b, y_dev, y_recv, y_pad.at[:, pl.ds(0, cols)], y_piece)
    reduce_stage(y_pad, nh, zi, z_dev, z_recv, z_sum, z_piece)

    s = next_sem()
    c = pltpu.make_async_remote_copy(
        src_ref=z_sum, dst_ref=pair_recv, send_sem=send_sem.at[s], recv_sem=recv_sem.at[s],
        device_id=pair_dev, device_id_type=MESH)
    c.start()
    c.wait()
    z_full[...] = z_sum[...] + pair_recv[...]

    gather_stage(z_full, nh, zi, z_dev, y_out, z_piece)
    gather_stage(y_out.at[:, pl.ds(0, cols)], ny, pos_b, y_dev, x_out, y_piece)
    half_off = core * rc
    other_off = (1 - core) * rc

    def out_rows(off, j):
        return pl.ds(pl.multiple_of(off + j * rx, 8), rx)

    a_sends = []
    for k in far_first(nx):
        j = (pos_a + k) % nx
        s = next_sem()
        c = pltpu.make_async_remote_copy(
            src_ref=x_out, dst_ref=core_out.at[x_piece(pos_a)], send_sem=send_sem.at[s],
            recv_sem=recv_sem.at[s], device_id=x_dev(j), device_id_type=MESH)
        c.start()
        a_sends.append((c, s, k))
    fwd = []
    s = next_sem()
    c = pltpu.make_async_remote_copy(
        src_ref=x_out, dst_ref=out_ref.at[out_rows(half_off, pos_a)], send_sem=send_sem.at[s],
        recv_sem=recv_sem.at[s], device_id=core_dev(0), device_id_type=MESH)
    c.start()
    fwd.append((c, s, pos_a))
    core_out[x_piece(pos_a)] = x_out[...]
    near_first = sorted(a_sends, key=lambda t: (min(t[2], nx - t[2]), t[2]))
    for c, s, k in near_first:
        j = (pos_a + nx - k) % nx
        pltpu.make_async_remote_copy(
            src_ref=x_out, dst_ref=core_out.at[x_piece(j)], send_sem=send_sem.at[s],
            recv_sem=recv_sem.at[s], device_id=x_dev(j), device_id_type=MESH).wait_recv()
        s2 = next_sem()
        c2 = pltpu.make_async_remote_copy(
            src_ref=core_out.at[x_piece(j)], dst_ref=out_ref.at[out_rows(half_off, j)], send_sem=send_sem.at[s2],
            recv_sem=recv_sem.at[s2], device_id=core_dev(0), device_id_type=MESH)
        c2.start()
        fwd.append((c2, s2, j))
    for c, s, k in a_sends:
        c.wait_send()
    mine = core_out[...]
    out_ref[core_piece(core)] = mine
    own = jnp.sum(jnp.sum(mine * mine, axis=0, keepdims=True), axis=1, keepdims=True)
    for c, s, j in fwd:
        c.wait_send()
    partner_pos = xi + (yi - xi) * (1 - core)
    fwd_k = [0] + [t[2] for t in near_first]
    for idx, (c, s, j) in enumerate(fwd):
        jp = (partner_pos + nx - fwd_k[idx]) % nx
        pltpu.make_async_remote_copy(
            src_ref=x_out, dst_ref=out_ref.at[out_rows(other_off, jp)], send_sem=send_sem.at[s],
            recv_sem=recv_sem.at[s], device_id=core_dev(0), device_id_type=MESH).wait_recv()
    other = out_ref[core_piece(1 - core)]
    rest = jnp.sum(jnp.sum(other * other, axis=0, keepdims=True), axis=1, keepdims=True)
    sq_ref[...] = jnp.broadcast_to(own + rest, sq_ref.shape)


def allreduce(g, tail, nx, ny, nz):
    assert nx == ny
    rows = g.shape[1]
    cols = g.shape[2] + tail.shape[1]
    nh = nz // 2
    rc = rows // 2
    rx = rc // nx
    ry = rx // ny
    zcols = 128 * nh * ((cols + 128 * nh - 1) // (128 * nh))
    cz = zcols // nh
    n_sems = 2 * (1 + (nx - 1) + (ny - 1) + (nh - 1)) + 1 + (nx - 1)
    f32 = jnp.float32
    return pl.pallas_call(
        functools.partial(_allreduce_kernel, nx, ny, nz),
        out_shape=(jax.ShapeDtypeStruct((rows, cols), f32), jax.ShapeDtypeStruct((8, 128), f32)),
        in_specs=[pl.BlockSpec(memory_space=pltpu.VMEM)] * 2,
        out_specs=(pl.BlockSpec(memory_space=pltpu.VMEM),) * 2,
        scratch_shapes=[
            pltpu.VMEM((rows, cols), f32),
            pltpu.VMEM((1, rc, cols), f32),
            pltpu.VMEM((rc, cols), f32),
            pltpu.VMEM((nx - 1, rx, cols), f32),
            pltpu.VMEM((rx, cols), f32),
            pltpu.VMEM((ny - 1, ry, cols), f32),
            pltpu.VMEM((ry, zcols), f32),
            pltpu.VMEM((nh - 1, ry, cz), f32),
            pltpu.VMEM((ry, cz), f32),
            pltpu.VMEM((ry, cz), f32),
            pltpu.VMEM((ry, cz), f32),
            pltpu.VMEM((ry, zcols), f32),
            pltpu.VMEM((rx, cols), f32),
            pltpu.VMEM((rc, cols), f32),
            pltpu.SemaphoreType.DMA((n_sems,)),
            pltpu.SemaphoreType.DMA((n_sems,)),
        ],
        compiler_params=pltpu.CompilerParams(
            collective_id=0, has_side_effects=True, vmem_limit_bytes=48 * 1024 * 1024),
    )(g, tail)


def per_device(nx, ny, grads, vec_grads, weight, basis, moment, second, vectors, vec_moment, vec_second):
    shards = lax.axis_size("shard")
    width = grads.shape[-1]
    rows = weight.shape[0]
    cols = vectors.shape[1]
    vec_n = vectors.shape[0]
    me = lax.axis_index("shard")
    vec_local = vec_grads[0, 0, 0].astype(jnp.float32) + vec_grads[1, 0, 0].astype(jnp.float32)
    lanes = 128 * ((cols + 127) // 128)
    placed = vec_local.reshape(vec_n, shards, cols).transpose(1, 0, 2).reshape(shards * vec_n, cols)
    tail = jnp.pad(placed, ((0, width - shards * vec_n), (0, lanes - cols)))
    packed, sq = allreduce(grads[:, 0, 0], tail, nx, ny, shards)
    total = packed[:, :width]
    projected_all = matmul(total, basis)
    subspace = lax.dot_general(
        total,
        projected_all,
        (((0,), (0,)), ((), ())),
        precision=HIGH,
        preferred_element_type=jnp.float32,
    )
    squares = sq[0, 0]
    iterate = subspace / jnp.sqrt(jnp.sum(subspace * subspace) + 1e-06)
    for step in range(NS_STEPS):
        gram = matmul(iterate.T, iterate)
        iterate = 1.5 * iterate - 0.5 * matmul(iterate, gram)
    factor = 1.0 / jnp.maximum(jnp.sqrt(squares / (width * width + vec_n * width)), 1.0)
    projected = lax.dynamic_slice_in_dim(projected_all, me * rows, rows, axis=0)
    vec_sum = lax.dynamic_slice(packed, (me * vec_n, width), (vec_n, cols))
    first_fix = 1.0 - 0.9**STEP
    second_fix = 1.0 - 0.999**STEP
    grad_low = factor * projected
    new_moment = 0.9 * moment + 0.1 * grad_low
    new_second = 0.999 * second + 0.001 * grad_low * grad_low
    normalized = new_moment / first_fix / (jnp.sqrt(new_second / second_fix) + 1e-08)
    full = lax.dot_general(
        normalized,
        basis,
        (((1,), (1,)), ((), ())),
        precision=HIGH,
        preferred_element_type=jnp.float32,
    )
    new_weight = weight - 0.001 * (0.25 * full + 0.01 * weight)
    vec_grad = factor * vec_sum
    new_vec_moment = 0.9 * vec_moment + 0.1 * vec_grad
    new_vec_second = 0.999 * vec_second + 0.001 * vec_grad * vec_grad
    vec_step = new_vec_moment / first_fix / (jnp.sqrt(new_vec_second / second_fix) + 1e-08)
    new_vectors = vectors - 0.001 * (vec_step + 0.01 * vectors)
    return (
        new_weight,
        full.astype(jnp.bfloat16),
        new_moment,
        new_second,
        iterate,
        new_vectors,
        new_vec_moment,
        new_vec_second,
    )


def solution(mesh, nx=None):
    if nx is None:
        nx = math.isqrt(mesh.shape["grp"] // 2)
    ny = mesh.shape["grp"] // 2 // nx
    return jax.shard_map(
        functools.partial(per_device, nx, ny),
        mesh=mesh,
        in_specs=(
            P(None, "grp", "shard", None, None),
            P(None, "grp", "shard", None, None),
            P("shard", None),
            P(),
            P("shard", None),
            P("shard", None),
            P(None, "shard"),
            P(None, "shard"),
            P(None, "shard"),
        ),
        out_specs=(
            P("shard", None),
            P("shard", None),
            P("shard", None),
            P("shard", None),
            P(),
            P(None, "shard"),
            P(None, "shard"),
            P(None, "shard"),
        ),
        check_vma=False,
    )
```

```python
import functools
import math

import jax
import jax.numpy as jnp
from jax import lax
from jax.experimental import pallas as pl
from jax.experimental.pallas import tpu as pltpu
from jax.sharding import PartitionSpec as P

NS_STEPS = 5
STEP = 100
MESH = pl.DeviceIdType.MESH


HIGH = lax.Precision.HIGH


def matmul(left, right):
    return jnp.dot(left, right, precision=HIGH, preferred_element_type=jnp.float32)


def _allreduce_kernel(nx, ny, nz, g_ref, tail_ref, out_ref, sq_ref, x_ref, core_recv, core_sum, x_recv, x_sum, y_recv,
                      y_pad, z_recv, z_sum, pair_recv, z_full, y_out, x_out, core_out, send_sem, recv_sem):
    rows, cols = x_ref.shape
    zcols = y_pad.shape[1]
    width = g_ref.shape[-1]
    nh = nz // 2
    rc, rx, ry, cz = rows // 2, rows // 2 // nx, rows // 2 // nx // ny, zcols // nh
    g = lax.axis_index("grp")
    z = lax.axis_index("shard")
    core = g % 2
    xi = (g // 2) % nx
    yi = g // (2 * nx)
    zp = z % 2
    zi = z // 2

    def core_dev(_):
        return (g + 1 - 2 * core, z)

    stride_a = 2 + (2 * nx - 2) * core
    pos_a = xi + (yi - xi) * core
    stride_b = 2 * nx - (2 * nx - 2) * core
    pos_b = yi + (xi - yi) * core

    def x_dev(j):
        return (g + stride_a * (j - pos_a), z)

    def y_dev(j):
        return (g + stride_b * (j - pos_b), z)

    def z_dev(j):
        return (g, zp + 2 * j)

    pair_dev = (g, z + 1 - 2 * zp)

    barrier = pltpu.get_barrier_semaphore()
    peers = [core_dev(0), pair_dev]
    peers += [x_dev((pos_a + k) % nx) for k in range(1, nx)]
    peers += [y_dev((pos_b + k) % ny) for k in range(1, ny)]
    peers += [z_dev((zi + k) % nh) for k in range(1, nh)]
    for dev in peers:
        pl.semaphore_signal(barrier, inc=1, device_id=dev, device_id_type=MESH)

    def pack(j):
        r = pl.ds(pl.multiple_of(j * (rows // 2), 8), rows // 2)
        x_ref[r, :width] = g_ref[0, r, :].astype(jnp.float32) + g_ref[1, r, :].astype(jnp.float32)
        x_ref[r, width:] = tail_ref[r, :]


    counter = [0]

    def next_sem():
        s = counter[0]
        counter[0] += 1
        return s

    def row_slice(j, size):
        return pl.ds(pl.multiple_of(j * size, 8), size)

    def col_slice(j, size):
        return (slice(None), pl.ds(pl.multiple_of(j * size, 128), size))

    def far_first(n):
        return sorted(range(1, n), key=lambda k: (-min(k, n - k), k))

    def reduce_stage(src, n, me, dev_of, recv, dst, piece):
        copies = []
        for k in far_first(n):
            j = (me + k) % n
            s = next_sem()
            c = pltpu.make_async_remote_copy(
                src_ref=src.at[piece(j)], dst_ref=recv.at[k - 1], send_sem=send_sem.at[s],
                recv_sem=recv_sem.at[s], device_id=dev_of(j), device_id_type=MESH)
            c.start()
            copies.append(c)
        for c in copies:
            c.wait()
        acc = src[piece(me)]
        for k in range(1, n):
            acc = acc + recv[k - 1]
        dst[...] = acc

    def gather_stage(src, n, me, dev_of, dst, piece):
        copies = []
        for k in far_first(n):
            j = (me + k) % n
            s = next_sem()
            c = pltpu.make_async_remote_copy(
                src_ref=src, dst_ref=dst.at[piece(me)], send_sem=send_sem.at[s],
                recv_sem=recv_sem.at[s], device_id=dev_of(j), device_id_type=MESH)
            c.start()
            copies.append((c, s, k))
        dst[piece(me)] = src[...]
        for c, s, k in copies:
            c.wait_send()
            j = (me + n - k) % n
            pltpu.make_async_remote_copy(
                src_ref=src, dst_ref=dst.at[piece(j)], send_sem=send_sem.at[s],
                recv_sem=recv_sem.at[s], device_id=dev_of(j), device_id_type=MESH).wait_recv()

    core_piece = lambda j: row_slice(j, rc)
    x_piece = lambda j: row_slice(j, rx)
    y_piece = lambda j: row_slice(j, ry)
    z_piece = lambda j: col_slice(j, cz)

    pack(1 - core)
    pl.semaphore_wait(barrier, len(peers))
    order = far_first(nx) + [0]
    partner_pos = xi + (yi - xi) * (1 - core)

    def half_rows(h, q):
        return pl.ds(pl.multiple_of(h * rc + q * rx, 8), rx)

    core_copies = []
    for k in order:
        q = (partner_pos + k) % nx
        s = next_sem()
        c = pltpu.make_async_remote_copy(
            src_ref=x_ref.at[half_rows(1 - core, q)], dst_ref=core_recv.at[0].at[x_piece(q)],
            send_sem=send_sem.at[s], recv_sem=recv_sem.at[s], device_id=core_dev(0), device_id_type=MESH)
        c.start()
        core_copies.append((c, s))
    pack(core)
    a_copies = []
    for (c, s), k in zip(core_copies, order):
        q = (pos_a + k) % nx
        pltpu.make_async_remote_copy(
            src_ref=x_ref.at[half_rows(1 - core, q)], dst_ref=core_recv.at[0].at[x_piece(q)],
            send_sem=send_sem.at[s], recv_sem=recv_sem.at[s], device_id=core_dev(0),
            device_id_type=MESH).wait_recv()
        core_sum[x_piece(q)] = x_ref[half_rows(core, q)] + core_recv[0, x_piece(q)]
        if k != 0:
            s2 = next_sem()
            c2 = pltpu.make_async_remote_copy(
                src_ref=core_sum.at[x_piece(q)], dst_ref=x_recv.at[k - 1], send_sem=send_sem.at[s2],
                recv_sem=recv_sem.at[s2], device_id=x_dev(q), device_id_type=MESH)
            c2.start()
            a_copies.append(c2)
    for c, s in core_copies:
        c.wait_send()
    for c2 in a_copies:
        c2.wait()
    acc = core_sum[x_piece(pos_a)]
    for k in range(1, nx):
        acc = acc + x_recv[k - 1]
    x_sum[...] = acc
    if zcols > cols:
        y_pad[:, cols:] = jnp.zeros((ry, zcols - cols), jnp.float32)
    reduce_stage(x_sum, ny, pos_b, y_dev, y_recv, y_pad.at[:, pl.ds(0, cols)], y_piece)
    reduce_stage(y_pad, nh, zi, z_dev, z_recv, z_sum, z_piece)

    s = next_sem()
    c = pltpu.make_async_remote_copy(
        src_ref=z_sum, dst_ref=pair_recv, send_sem=send_sem.at[s], recv_sem=recv_sem.at[s],
        device_id=pair_dev, device_id_type=MESH)
    c.start()
    c.wait()
    z_full[...] = z_sum[...] + pair_recv[...]

    gather_stage(z_full, nh, zi, z_dev, y_out, z_piece)
    gather_stage(y_out.at[:, pl.ds(0, cols)], ny, pos_b, y_dev, x_out, y_piece)
    half_off = core * rc
    other_off = (1 - core) * rc

    def out_rows(off, j):
        return pl.ds(pl.multiple_of(off + j * rx, 8), rx)

    a_sends = []
    for k in range(1, nx):
        j = (pos_a + k) % nx
        s = next_sem()
        c = pltpu.make_async_remote_copy(
            src_ref=x_out, dst_ref=core_out.at[x_piece(pos_a)], send_sem=send_sem.at[s],
            recv_sem=recv_sem.at[s], device_id=x_dev(j), device_id_type=MESH)
        c.start()
        a_sends.append((c, s, k))
    fwd = []
    s = next_sem()
    c = pltpu.make_async_remote_copy(
        src_ref=x_out, dst_ref=out_ref.at[out_rows(half_off, pos_a)], send_sem=send_sem.at[s],
        recv_sem=recv_sem.at[s], device_id=core_dev(0), device_id_type=MESH)
    c.start()
    fwd.append((c, s, pos_a))
    core_out[x_piece(pos_a)] = x_out[...]
    for c, s, k in a_sends:
        j = (pos_a + nx - k) % nx
        pltpu.make_async_remote_copy(
            src_ref=x_out, dst_ref=core_out.at[x_piece(j)], send_sem=send_sem.at[s],
            recv_sem=recv_sem.at[s], device_id=x_dev(j), device_id_type=MESH).wait_recv()
        s2 = next_sem()
        c2 = pltpu.make_async_remote_copy(
            src_ref=core_out.at[x_piece(j)], dst_ref=out_ref.at[out_rows(half_off, j)], send_sem=send_sem.at[s2],
            recv_sem=recv_sem.at[s2], device_id=core_dev(0), device_id_type=MESH)
        c2.start()
        fwd.append((c2, s2, j))
    for c, s, k in a_sends:
        c.wait_send()
    mine = core_out[...]
    out_ref[core_piece(core)] = mine
    own = jnp.sum(jnp.sum(mine * mine, axis=0, keepdims=True), axis=1, keepdims=True)
    for c, s, j in fwd:
        c.wait_send()
    partner_pos = xi + (yi - xi) * (1 - core)
    for idx, (c, s, j) in enumerate(fwd):
        jp = (partner_pos + nx - idx) % nx
        pltpu.make_async_remote_copy(
            src_ref=x_out, dst_ref=out_ref.at[out_rows(other_off, jp)], send_sem=send_sem.at[s],
            recv_sem=recv_sem.at[s], device_id=core_dev(0), device_id_type=MESH).wait_recv()
    other = out_ref[core_piece(1 - core)]
    rest = jnp.sum(jnp.sum(other * other, axis=0, keepdims=True), axis=1, keepdims=True)
    sq_ref[...] = jnp.broadcast_to(own + rest, sq_ref.shape)


def allreduce(g, tail, nx, ny, nz):
    assert nx == ny
    rows = g.shape[1]
    cols = g.shape[2] + tail.shape[1]
    nh = nz // 2
    rc = rows // 2
    rx = rc // nx
    ry = rx // ny
    zcols = 128 * nh * ((cols + 128 * nh - 1) // (128 * nh))
    cz = zcols // nh
    n_sems = 2 * (1 + (nx - 1) + (ny - 1) + (nh - 1)) + 1 + 2 * (nx - 1)
    f32 = jnp.float32
    return pl.pallas_call(
        functools.partial(_allreduce_kernel, nx, ny, nz),
        out_shape=(jax.ShapeDtypeStruct((rows, cols), f32), jax.ShapeDtypeStruct((8, 128), f32)),
        in_specs=[pl.BlockSpec(memory_space=pltpu.VMEM)] * 2,
        out_specs=(pl.BlockSpec(memory_space=pltpu.VMEM),) * 2,
        scratch_shapes=[
            pltpu.VMEM((rows, cols), f32),
            pltpu.VMEM((1, rc, cols), f32),
            pltpu.VMEM((rc, cols), f32),
            pltpu.VMEM((nx - 1, rx, cols), f32),
            pltpu.VMEM((rx, cols), f32),
            pltpu.VMEM((ny - 1, ry, cols), f32),
            pltpu.VMEM((ry, zcols), f32),
            pltpu.VMEM((nh - 1, ry, cz), f32),
            pltpu.VMEM((ry, cz), f32),
            pltpu.VMEM((ry, cz), f32),
            pltpu.VMEM((ry, cz), f32),
            pltpu.VMEM((ry, zcols), f32),
            pltpu.VMEM((rx, cols), f32),
            pltpu.VMEM((rc, cols), f32),
            pltpu.SemaphoreType.DMA((n_sems,)),
            pltpu.SemaphoreType.DMA((n_sems,)),
        ],
        compiler_params=pltpu.CompilerParams(
            collective_id=0, has_side_effects=True, vmem_limit_bytes=48 * 1024 * 1024),
    )(g, tail)


def per_device(nx, ny, grads, vec_grads, weight, basis, moment, second, vectors, vec_moment, vec_second):
    shards = lax.axis_size("shard")
    width = grads.shape[-1]
    rows = weight.shape[0]
    cols = vectors.shape[1]
    vec_n = vectors.shape[0]
    me = lax.axis_index("shard")
    vec_local = vec_grads[0, 0, 0].astype(jnp.float32) + vec_grads[1, 0, 0].astype(jnp.float32)
    lanes = 128 * ((cols + 127) // 128)
    placed = vec_local.reshape(vec_n, shards, cols).transpose(1, 0, 2).reshape(shards * vec_n, cols)
    tail = jnp.pad(placed, ((0, width - shards * vec_n), (0, lanes - cols)))
    packed, sq = allreduce(grads[:, 0, 0], tail, nx, ny, shards)
    total = packed[:, :width]
    projected_all = matmul(total, basis)
    subspace = lax.dot_general(
        total,
        projected_all,
        (((0,), (0,)), ((), ())),
        precision=HIGH,
        preferred_element_type=jnp.float32,
    )
    squares = sq[0, 0]
    iterate = subspace / jnp.sqrt(jnp.sum(subspace * subspace) + 1e-06)
    for step in range(NS_STEPS):
        gram = matmul(iterate.T, iterate)
        iterate = 1.5 * iterate - 0.5 * matmul(iterate, gram)
    factor = 1.0 / jnp.maximum(jnp.sqrt(squares / (width * width + vec_n * width)), 1.0)
    projected = lax.dynamic_slice_in_dim(projected_all, me * rows, rows, axis=0)
    vec_sum = lax.dynamic_slice(packed, (me * vec_n, width), (vec_n, cols))
    first_fix = 1.0 - 0.9**STEP
    second_fix = 1.0 - 0.999**STEP
    grad_low = factor * projected
    new_moment = 0.9 * moment + 0.1 * grad_low
    new_second = 0.999 * second + 0.001 * grad_low * grad_low
    normalized = new_moment / first_fix / (jnp.sqrt(new_second / second_fix) + 1e-08)
    full = lax.dot_general(
        normalized,
        basis,
        (((1,), (1,)), ((), ())),
        precision=HIGH,
        preferred_element_type=jnp.float32,
    )
    new_weight = weight - 0.001 * (0.25 * full + 0.01 * weight)
    vec_grad = factor * vec_sum
    new_vec_moment = 0.9 * vec_moment + 0.1 * vec_grad
    new_vec_second = 0.999 * vec_second + 0.001 * vec_grad * vec_grad
    vec_step = new_vec_moment / first_fix / (jnp.sqrt(new_vec_second / second_fix) + 1e-08)
    new_vectors = vectors - 0.001 * (vec_step + 0.01 * vectors)
    return (
        new_weight,
        full.astype(jnp.bfloat16),
        new_moment,
        new_second,
        iterate,
        new_vectors,
        new_vec_moment,
        new_vec_second,
    )


def solution(mesh, nx=None):
    if nx is None:
        nx = math.isqrt(mesh.shape["grp"] // 2)
    ny = mesh.shape["grp"] // 2 // nx
    return jax.shard_map(
        functools.partial(per_device, nx, ny),
        mesh=mesh,
        in_specs=(
            P(None, "grp", "shard", None, None),
            P(None, "grp", "shard", None, None),
            P("shard", None),
            P(),
            P("shard", None),
            P("shard", None),
            P(None, "shard"),
            P(None, "shard"),
            P(None, "shard"),
        ),
        out_specs=(
            P("shard", None),
            P("shard", None),
            P("shard", None),
            P("shard", None),
            P(),
            P(None, "shard"),
            P(None, "shard"),
            P(None, "shard"),
        ),
        check_vma=False,
    )
```

```python
import functools
import math

import jax
import jax.numpy as jnp
from jax import lax
from jax.experimental import pallas as pl
from jax.experimental.pallas import tpu as pltpu
from jax.sharding import PartitionSpec as P

NS_STEPS = 5
STEP = 100
MESH = pl.DeviceIdType.MESH


HIGH = lax.Precision.HIGH


def matmul(left, right):
    return jnp.dot(left, right, precision=HIGH, preferred_element_type=jnp.float32)


def _allreduce_kernel(nx, ny, nz, g_ref, tail_ref, out_ref, sq_ref, x_ref, core_recv, core_sum, x_recv, x_sum, y_recv,
                      y_pad, z_recv, z_sum, pair_recv, z_full, y_out, x_wide, core_out, send_sem, recv_sem):
    rows, cols = x_ref.shape
    zcols = y_pad.shape[1]
    width = g_ref.shape[-1]
    nh = nz // 2
    rc, rx, ry, cz = rows // 2, rows // 2 // nx, rows // 2 // nx // ny, zcols // nh
    g = lax.axis_index("grp")
    z = lax.axis_index("shard")
    core = g % 2
    xi = (g // 2) % nx
    yi = g // (2 * nx)
    zp = z % 2
    zi = z // 2

    def core_dev(_):
        return (g + 1 - 2 * core, z)

    stride_a = 2 + (2 * nx - 2) * core
    pos_a = xi + (yi - xi) * core
    stride_b = 2 * nx - (2 * nx - 2) * core
    pos_b = yi + (xi - yi) * core

    def x_dev(j):
        return (g + stride_a * (j - pos_a), z)

    def y_dev(j):
        return (g + stride_b * (j - pos_b), z)

    def z_dev(j):
        return (g, zp + 2 * j)

    pair_dev = (g, z + 1 - 2 * zp)

    barrier = pltpu.get_barrier_semaphore()
    peers = [core_dev(0), pair_dev]
    peers += [x_dev((pos_a + k) % nx) for k in range(1, nx)]
    peers += [y_dev((pos_b + k) % ny) for k in range(1, ny)]
    peers += [z_dev((zi + k) % nh) for k in range(1, nh)]
    for dev in peers:
        pl.semaphore_signal(barrier, inc=1, device_id=dev, device_id_type=MESH)

    def pack(j):
        r = pl.ds(pl.multiple_of(j * (rows // 2), 8), rows // 2)
        x_ref[r, :width] = g_ref[0, r, :].astype(jnp.float32) + g_ref[1, r, :].astype(jnp.float32)
        x_ref[r, width:] = tail_ref[r, :]


    counter = [0]

    def next_sem():
        s = counter[0]
        counter[0] += 1
        return s

    def row_slice(j, size):
        return pl.ds(pl.multiple_of(j * size, 8), size)

    def col_slice(j, size):
        return (slice(None), pl.ds(pl.multiple_of(j * size, 128), size))

    def far_first(n):
        return sorted(range(1, n), key=lambda k: (-min(k, n - k), k))

    def reduce_stage(src, n, me, dev_of, recv, dst, piece):
        copies = []
        for k in far_first(n):
            j = (me + k) % n
            s = next_sem()
            c = pltpu.make_async_remote_copy(
                src_ref=src.at[piece(j)], dst_ref=recv.at[k - 1], send_sem=send_sem.at[s],
                recv_sem=recv_sem.at[s], device_id=dev_of(j), device_id_type=MESH)
            c.start()
            copies.append(c)
        for c in copies:
            c.wait()
        acc = src[piece(me)]
        for k in range(1, n):
            acc = acc + recv[k - 1]
        dst[...] = acc

    def gather_stage(src, n, me, dev_of, dst, piece):
        copies = []
        for k in far_first(n):
            j = (me + k) % n
            s = next_sem()
            c = pltpu.make_async_remote_copy(
                src_ref=src, dst_ref=dst.at[piece(me)], send_sem=send_sem.at[s],
                recv_sem=recv_sem.at[s], device_id=dev_of(j), device_id_type=MESH)
            c.start()
            copies.append((c, s, k))
        dst[piece(me)] = src[...]
        for c, s, k in copies:
            c.wait_send()
            j = (me + n - k) % n
            pltpu.make_async_remote_copy(
                src_ref=src, dst_ref=dst.at[piece(j)], send_sem=send_sem.at[s],
                recv_sem=recv_sem.at[s], device_id=dev_of(j), device_id_type=MESH).wait_recv()

    core_piece = lambda j: row_slice(j, rc)
    x_piece = lambda j: row_slice(j, rx)
    y_piece = lambda j: row_slice(j, ry)
    z_piece = lambda j: col_slice(j, cz)

    pack(1 - core)
    pl.semaphore_wait(barrier, len(peers))
    order = far_first(nx) + [0]
    partner_pos = xi + (yi - xi) * (1 - core)

    def half_rows(h, q):
        return pl.ds(pl.multiple_of(h * rc + q * rx, 8), rx)

    core_copies = []
    for k in order:
        q = (partner_pos + k) % nx
        s = next_sem()
        c = pltpu.make_async_remote_copy(
            src_ref=x_ref.at[half_rows(1 - core, q)], dst_ref=core_recv.at[0].at[x_piece(q)],
            send_sem=send_sem.at[s], recv_sem=recv_sem.at[s], device_id=core_dev(0), device_id_type=MESH)
        c.start()
        core_copies.append((c, s))
    pack(core)
    a_copies = []
    for (c, s), k in zip(core_copies, order):
        q = (pos_a + k) % nx
        pltpu.make_async_remote_copy(
            src_ref=x_ref.at[half_rows(1 - core, q)], dst_ref=core_recv.at[0].at[x_piece(q)],
            send_sem=send_sem.at[s], recv_sem=recv_sem.at[s], device_id=core_dev(0),
            device_id_type=MESH).wait_recv()
        core_sum[x_piece(q)] = x_ref[half_rows(core, q)] + core_recv[0, x_piece(q)]
        if k != 0:
            s2 = next_sem()
            c2 = pltpu.make_async_remote_copy(
                src_ref=core_sum.at[x_piece(q)], dst_ref=x_recv.at[k - 1], send_sem=send_sem.at[s2],
                recv_sem=recv_sem.at[s2], device_id=x_dev(q), device_id_type=MESH)
            c2.start()
            a_copies.append(c2)
    for c, s in core_copies:
        c.wait_send()
    for c2 in a_copies:
        c2.wait()
    acc = core_sum[x_piece(pos_a)]
    for k in range(1, nx):
        acc = acc + x_recv[k - 1]
    x_sum[...] = acc
    if zcols > cols:
        y_pad[:, cols:] = jnp.zeros((ry, zcols - cols), jnp.float32)
    reduce_stage(x_sum, ny, pos_b, y_dev, y_recv, y_pad.at[:, pl.ds(0, cols)], y_piece)
    reduce_stage(y_pad, nh, zi, z_dev, z_recv, z_sum, z_piece)

    s = next_sem()
    c = pltpu.make_async_remote_copy(
        src_ref=z_sum, dst_ref=pair_recv, send_sem=send_sem.at[s], recv_sem=recv_sem.at[s],
        device_id=pair_dev, device_id_type=MESH)
    c.start()
    c.wait()
    z_full[...] = z_sum[...] + pair_recv[...]

    x_out = x_wide.at[:, pl.ds(0, cols)]

    def slab(q):
        return pl.ds(pl.multiple_of(q * cz, 128), cz)

    z_sends = []
    for k in far_first(nh):
        j = (zi + k) % nh
        s = next_sem()
        c = pltpu.make_async_remote_copy(
            src_ref=z_full, dst_ref=y_out.at[:, slab(zi)], send_sem=send_sem.at[s],
            recv_sem=recv_sem.at[s], device_id=z_dev(j), device_id_type=MESH)
        c.start()
        z_sends.append((c, s, k))
    y_out[:, slab(zi)] = z_full[...]
    fwd_base = counter[0]
    counter[0] += nh * (ny - 1)
    slab_order = [0] + sorted(range(1, nh), key=lambda k: (min(k, nh - k), k))
    b_copies = []

    def forward(t, k):
        q = (zi + nh - k) % nh
        src_slab = z_full if k == 0 else y_out.at[:, slab(q)]
        for kb in range(1, ny):
            jb = (pos_b + kb) % ny
            sb = fwd_base + t * (ny - 1) + kb - 1
            cb = pltpu.make_async_remote_copy(
                src_ref=src_slab, dst_ref=x_wide.at[y_piece(pos_b), slab(q)], send_sem=send_sem.at[sb],
                recv_sem=recv_sem.at[sb], device_id=y_dev(jb), device_id_type=MESH)
            cb.start()
            b_copies.append(cb)

    forward(0, 0)
    z_by_k = {k: (c, s) for c, s, k in z_sends}
    for t, k in enumerate(slab_order):
        if k == 0:
            continue
        c, s = z_by_k[k]
        q = (zi + nh - k) % nh
        pltpu.make_async_remote_copy(
            src_ref=z_full, dst_ref=y_out.at[:, slab(q)], send_sem=send_sem.at[s],
            recv_sem=recv_sem.at[s], device_id=z_dev(q), device_id_type=MESH).wait_recv()
        forward(t, k)
    x_wide[y_piece(pos_b), :] = y_out[...]
    for c, s, k in z_sends:
        c.wait_send()
    for cb in b_copies:
        cb.wait_send()
    for t, k in enumerate(slab_order):
        q = (zi + nh - k) % nh
        for kb in range(1, ny):
            jb = (pos_b + ny - kb) % ny
            sb = fwd_base + t * (ny - 1) + kb - 1
            pltpu.make_async_remote_copy(
                src_ref=z_full, dst_ref=x_wide.at[y_piece(jb), slab(q)], send_sem=send_sem.at[sb],
                recv_sem=recv_sem.at[sb], device_id=y_dev(jb), device_id_type=MESH).wait_recv()
    half_off = core * rc
    other_off = (1 - core) * rc

    def out_rows(off, j):
        return pl.ds(pl.multiple_of(off + j * rx, 8), rx)

    a_sends = []
    for k in range(1, nx):
        j = (pos_a + k) % nx
        s = next_sem()
        c = pltpu.make_async_remote_copy(
            src_ref=x_out, dst_ref=core_out.at[x_piece(pos_a)], send_sem=send_sem.at[s],
            recv_sem=recv_sem.at[s], device_id=x_dev(j), device_id_type=MESH)
        c.start()
        a_sends.append((c, s, k))
    fwd = []
    s = next_sem()
    c = pltpu.make_async_remote_copy(
        src_ref=x_out, dst_ref=out_ref.at[out_rows(half_off, pos_a)], send_sem=send_sem.at[s],
        recv_sem=recv_sem.at[s], device_id=core_dev(0), device_id_type=MESH)
    c.start()
    fwd.append((c, s, pos_a))
    core_out[x_piece(pos_a)] = x_out[...]
    for c, s, k in a_sends:
        j = (pos_a + nx - k) % nx
        pltpu.make_async_remote_copy(
            src_ref=x_out, dst_ref=core_out.at[x_piece(j)], send_sem=send_sem.at[s],
            recv_sem=recv_sem.at[s], device_id=x_dev(j), device_id_type=MESH).wait_recv()
        s2 = next_sem()
        c2 = pltpu.make_async_remote_copy(
            src_ref=core_out.at[x_piece(j)], dst_ref=out_ref.at[out_rows(half_off, j)], send_sem=send_sem.at[s2],
            recv_sem=recv_sem.at[s2], device_id=core_dev(0), device_id_type=MESH)
        c2.start()
        fwd.append((c2, s2, j))
    for c, s, k in a_sends:
        c.wait_send()
    mine = core_out[...]
    out_ref[core_piece(core)] = mine
    own = jnp.sum(jnp.sum(mine * mine, axis=0, keepdims=True), axis=1, keepdims=True)
    for c, s, j in fwd:
        c.wait_send()
    partner_pos = xi + (yi - xi) * (1 - core)
    for idx, (c, s, j) in enumerate(fwd):
        jp = (partner_pos + nx - idx) % nx
        pltpu.make_async_remote_copy(
            src_ref=x_out, dst_ref=out_ref.at[out_rows(other_off, jp)], send_sem=send_sem.at[s],
            recv_sem=recv_sem.at[s], device_id=core_dev(0), device_id_type=MESH).wait_recv()
    other = out_ref[core_piece(1 - core)]
    rest = jnp.sum(jnp.sum(other * other, axis=0, keepdims=True), axis=1, keepdims=True)
    sq_ref[...] = jnp.broadcast_to(own + rest, sq_ref.shape)


def allreduce(g, tail, nx, ny, nz):
    assert nx == ny
    rows = g.shape[1]
    cols = g.shape[2] + tail.shape[1]
    nh = nz // 2
    rc = rows // 2
    rx = rc // nx
    ry = rx // ny
    zcols = 128 * nh * ((cols + 128 * nh - 1) // (128 * nh))
    cz = zcols // nh
    n_sems = 2 * (1 + (nx - 1) + (ny - 1) + (nh - 1)) + 1 + 2 * (nx - 1) + (nh - 1) * (ny - 1)
    f32 = jnp.float32
    return pl.pallas_call(
        functools.partial(_allreduce_kernel, nx, ny, nz),
        out_shape=(jax.ShapeDtypeStruct((rows, cols), f32), jax.ShapeDtypeStruct((8, 128), f32)),
        in_specs=[pl.BlockSpec(memory_space=pltpu.VMEM)] * 2,
        out_specs=(pl.BlockSpec(memory_space=pltpu.VMEM),) * 2,
        scratch_shapes=[
            pltpu.VMEM((rows, cols), f32),
            pltpu.VMEM((1, rc, cols), f32),
            pltpu.VMEM((rc, cols), f32),
            pltpu.VMEM((nx - 1, rx, cols), f32),
            pltpu.VMEM((rx, cols), f32),
            pltpu.VMEM((ny - 1, ry, cols), f32),
            pltpu.VMEM((ry, zcols), f32),
            pltpu.VMEM((nh - 1, ry, cz), f32),
            pltpu.VMEM((ry, cz), f32),
            pltpu.VMEM((ry, cz), f32),
            pltpu.VMEM((ry, cz), f32),
            pltpu.VMEM((ry, zcols), f32),
            pltpu.VMEM((rx, zcols), f32),
            pltpu.VMEM((rc, cols), f32),
            pltpu.SemaphoreType.DMA((n_sems,)),
            pltpu.SemaphoreType.DMA((n_sems,)),
        ],
        compiler_params=pltpu.CompilerParams(
            collective_id=0, has_side_effects=True, vmem_limit_bytes=48 * 1024 * 1024),
    )(g, tail)


def per_device(nx, ny, grads, vec_grads, weight, basis, moment, second, vectors, vec_moment, vec_second):
    shards = lax.axis_size("shard")
    width = grads.shape[-1]
    rows = weight.shape[0]
    cols = vectors.shape[1]
    vec_n = vectors.shape[0]
    me = lax.axis_index("shard")
    vec_local = vec_grads[0, 0, 0].astype(jnp.float32) + vec_grads[1, 0, 0].astype(jnp.float32)
    lanes = 128 * ((cols + 127) // 128)
    placed = vec_local.reshape(vec_n, shards, cols).transpose(1, 0, 2).reshape(shards * vec_n, cols)
    tail = jnp.pad(placed, ((0, width - shards * vec_n), (0, lanes - cols)))
    packed, sq = allreduce(grads[:, 0, 0], tail, nx, ny, shards)
    total = packed[:, :width]
    projected_all = matmul(total, basis)
    subspace = lax.dot_general(
        total,
        projected_all,
        (((0,), (0,)), ((), ())),
        precision=HIGH,
        preferred_element_type=jnp.float32,
    )
    squares = sq[0, 0]
    iterate = subspace / jnp.sqrt(jnp.sum(subspace * subspace) + 1e-06)
    for step in range(NS_STEPS):
        gram = matmul(iterate.T, iterate)
        iterate = 1.5 * iterate - 0.5 * matmul(iterate, gram)
    factor = 1.0 / jnp.maximum(jnp.sqrt(squares / (width * width + vec_n * width)), 1.0)
    projected = lax.dynamic_slice_in_dim(projected_all, me * rows, rows, axis=0)
    vec_sum = lax.dynamic_slice(packed, (me * vec_n, width), (vec_n, cols))
    first_fix = 1.0 - 0.9**STEP
    second_fix = 1.0 - 0.999**STEP
    grad_low = factor * projected
    new_moment = 0.9 * moment + 0.1 * grad_low
    new_second = 0.999 * second + 0.001 * grad_low * grad_low
    normalized = new_moment / first_fix / (jnp.sqrt(new_second / second_fix) + 1e-08)
    full = lax.dot_general(
        normalized,
        basis,
        (((1,), (1,)), ((), ())),
        precision=HIGH,
        preferred_element_type=jnp.float32,
    )
    new_weight = weight - 0.001 * (0.25 * full + 0.01 * weight)
    vec_grad = factor * vec_sum
    new_vec_moment = 0.9 * vec_moment + 0.1 * vec_grad
    new_vec_second = 0.999 * vec_second + 0.001 * vec_grad * vec_grad
    vec_step = new_vec_moment / first_fix / (jnp.sqrt(new_vec_second / second_fix) + 1e-08)
    new_vectors = vectors - 0.001 * (vec_step + 0.01 * vectors)
    return (
        new_weight,
        full.astype(jnp.bfloat16),
        new_moment,
        new_second,
        iterate,
        new_vectors,
        new_vec_moment,
        new_vec_second,
    )


def solution(mesh, nx=None):
    if nx is None:
        nx = math.isqrt(mesh.shape["grp"] // 2)
    ny = mesh.shape["grp"] // 2 // nx
    return jax.shard_map(
        functools.partial(per_device, nx, ny),
        mesh=mesh,
        in_specs=(
            P(None, "grp", "shard", None, None),
            P(None, "grp", "shard", None, None),
            P("shard", None),
            P(),
            P("shard", None),
            P("shard", None),
            P(None, "shard"),
            P(None, "shard"),
            P(None, "shard"),
        ),
        out_specs=(
            P("shard", None),
            P("shard", None),
            P("shard", None),
            P("shard", None),
            P(),
            P(None, "shard"),
            P(None, "shard"),
            P(None, "shard"),
        ),
        check_vma=False,
    )
```

```python
import functools
import math

import jax
import jax.numpy as jnp
from jax import lax
from jax.experimental import pallas as pl
from jax.experimental.pallas import tpu as pltpu
from jax.sharding import PartitionSpec as P

NS_STEPS = 5
STEP = 100
MESH = pl.DeviceIdType.MESH


HIGH = lax.Precision.HIGH


def matmul(left, right):
    return jnp.dot(left, right, precision=HIGH, preferred_element_type=jnp.float32)


def _allreduce_kernel(nx, ny, nz, g_ref, tail_ref, out_ref, sq_ref, x_ref, core_recv, core_sum, x_recv, x_sum, y_recv,
                      y_pad, z_recv, z_sum, pair_recv, z_full, y_out, x_wide, core_out, send_sem, recv_sem):
    rows, cols = x_ref.shape
    zcols = y_pad.shape[1]
    width = g_ref.shape[-1]
    nh = nz // 2
    rc, rx, ry, cz = rows // 2, rows // 2 // nx, rows // 2 // nx // ny, zcols // nh
    g = lax.axis_index("grp")
    z = lax.axis_index("shard")
    core = g % 2
    xi = (g // 2) % nx
    yi = g // (2 * nx)
    zp = z % 2
    zi = z // 2

    def core_dev(_):
        return (g + 1 - 2 * core, z)

    stride_a = 2 + (2 * nx - 2) * core
    pos_a = xi + (yi - xi) * core
    stride_b = 2 * nx - (2 * nx - 2) * core
    pos_b = yi + (xi - yi) * core

    def x_dev(j):
        return (g + stride_a * (j - pos_a), z)

    def y_dev(j):
        return (g + stride_b * (j - pos_b), z)

    def z_dev(j):
        return (g, zp + 2 * j)

    pair_dev = (g, z + 1 - 2 * zp)

    barrier = pltpu.get_barrier_semaphore()
    peers = [core_dev(0)] + [(g, 1 - zp + 2 * j) for j in range(nh)]
    peers += [x_dev((pos_a + k) % nx) for k in range(1, nx)]
    peers += [y_dev((pos_b + k) % ny) for k in range(1, ny)]
    peers += [z_dev((zi + k) % nh) for k in range(1, nh)]
    for dev in peers:
        pl.semaphore_signal(barrier, inc=1, device_id=dev, device_id_type=MESH)

    def pack(j):
        r = pl.ds(pl.multiple_of(j * (rows // 2), 8), rows // 2)
        x_ref[r, :width] = g_ref[0, r, :].astype(jnp.float32) + g_ref[1, r, :].astype(jnp.float32)
        x_ref[r, width:] = tail_ref[r, :]


    counter = [0]

    def next_sem():
        s = counter[0]
        counter[0] += 1
        return s

    def row_slice(j, size):
        return pl.ds(pl.multiple_of(j * size, 8), size)

    def col_slice(j, size):
        return (slice(None), pl.ds(pl.multiple_of(j * size, 128), size))

    def far_first(n):
        return sorted(range(1, n), key=lambda k: (-min(k, n - k), k))

    def reduce_stage(src, n, me, dev_of, recv, dst, piece):
        copies = []
        for k in far_first(n):
            j = (me + k) % n
            s = next_sem()
            c = pltpu.make_async_remote_copy(
                src_ref=src.at[piece(j)], dst_ref=recv.at[k - 1], send_sem=send_sem.at[s],
                recv_sem=recv_sem.at[s], device_id=dev_of(j), device_id_type=MESH)
            c.start()
            copies.append(c)
        for c in copies:
            c.wait()
        acc = src[piece(me)]
        for k in range(1, n):
            acc = acc + recv[k - 1]
        dst[...] = acc

    def gather_stage(src, n, me, dev_of, dst, piece):
        copies = []
        for k in far_first(n):
            j = (me + k) % n
            s = next_sem()
            c = pltpu.make_async_remote_copy(
                src_ref=src, dst_ref=dst.at[piece(me)], send_sem=send_sem.at[s],
                recv_sem=recv_sem.at[s], device_id=dev_of(j), device_id_type=MESH)
            c.start()
            copies.append((c, s, k))
        dst[piece(me)] = src[...]
        for c, s, k in copies:
            c.wait_send()
            j = (me + n - k) % n
            pltpu.make_async_remote_copy(
                src_ref=src, dst_ref=dst.at[piece(j)], send_sem=send_sem.at[s],
                recv_sem=recv_sem.at[s], device_id=dev_of(j), device_id_type=MESH).wait_recv()

    core_piece = lambda j: row_slice(j, rc)
    x_piece = lambda j: row_slice(j, rx)
    y_piece = lambda j: row_slice(j, ry)
    z_piece = lambda j: col_slice(j, cz)

    pack(1 - core)
    pl.semaphore_wait(barrier, len(peers))
    order = far_first(nx) + [0]
    partner_pos = xi + (yi - xi) * (1 - core)

    def half_rows(h, q):
        return pl.ds(pl.multiple_of(h * rc + q * rx, 8), rx)

    core_copies = []
    for k in order:
        q = (partner_pos + k) % nx
        s = next_sem()
        c = pltpu.make_async_remote_copy(
            src_ref=x_ref.at[half_rows(1 - core, q)], dst_ref=core_recv.at[0].at[x_piece(q)],
            send_sem=send_sem.at[s], recv_sem=recv_sem.at[s], device_id=core_dev(0), device_id_type=MESH)
        c.start()
        core_copies.append((c, s))
    pack(core)
    a_copies = []
    for (c, s), k in zip(core_copies, order):
        q = (pos_a + k) % nx
        pltpu.make_async_remote_copy(
            src_ref=x_ref.at[half_rows(1 - core, q)], dst_ref=core_recv.at[0].at[x_piece(q)],
            send_sem=send_sem.at[s], recv_sem=recv_sem.at[s], device_id=core_dev(0),
            device_id_type=MESH).wait_recv()
        core_sum[x_piece(q)] = x_ref[half_rows(core, q)] + core_recv[0, x_piece(q)]
        if k != 0:
            s2 = next_sem()
            c2 = pltpu.make_async_remote_copy(
                src_ref=core_sum.at[x_piece(q)], dst_ref=x_recv.at[k - 1], send_sem=send_sem.at[s2],
                recv_sem=recv_sem.at[s2], device_id=x_dev(q), device_id_type=MESH)
            c2.start()
            a_copies.append(c2)
    for c, s in core_copies:
        c.wait_send()
    for c2 in a_copies:
        c2.wait()
    acc = core_sum[x_piece(pos_a)]
    for k in range(1, nx):
        acc = acc + x_recv[k - 1]
    x_sum[...] = acc
    if zcols > cols:
        y_pad[:, cols:] = jnp.zeros((ry, zcols - cols), jnp.float32)
    reduce_stage(x_sum, ny, pos_b, y_dev, y_recv, y_pad.at[:, pl.ds(0, cols)], y_piece)
    reduce_stage(y_pad, nh, zi, z_dev, z_recv, z_sum, z_piece)

    x_out = x_wide.at[:, pl.ds(0, cols)]
    y_parts = pair_recv

    def slab(q):
        return pl.ds(pl.multiple_of(q * cz, 128), cz)

    sbase = counter[0]
    counter[0] += nz - 1
    rbase = counter[0]
    counter[0] += nz
    z_sends = []
    for idx, off in enumerate(far_first(nz)):
        c = pltpu.make_async_remote_copy(
            src_ref=z_sum, dst_ref=y_parts.at[zp, :, slab(zi)], send_sem=send_sem.at[sbase + idx],
            recv_sem=recv_sem.at[rbase + z], device_id=(g, (z + off) % nz), device_id_type=MESH)
        c.start()
        z_sends.append(c)
    y_parts[zp, :, slab(zi)] = z_sum[...]
    fwd_base = counter[0]
    counter[0] += nh * (ny - 1)
    slab_order = [0] + sorted(range(1, nh), key=lambda k: (min(k, nh - k), k))
    b_copies = []

    def forward(t, q):
        for kb in range(1, ny):
            jb = (pos_b + kb) % ny
            sb = fwd_base + t * (ny - 1) + kb - 1
            cb = pltpu.make_async_remote_copy(
                src_ref=y_out.at[:, slab(q)], dst_ref=x_wide.at[y_piece(pos_b), slab(q)],
                send_sem=send_sem.at[sb], recv_sem=recv_sem.at[sb], device_id=y_dev(jb), device_id_type=MESH)
            cb.start()
            b_copies.append(cb)

    def wait_part(p, q):
        zs = 2 * q + p
        pltpu.make_async_remote_copy(
            src_ref=z_sum, dst_ref=y_parts.at[p, :, slab(q)], send_sem=send_sem.at[sbase],
            recv_sem=recv_sem.at[rbase + zs], device_id=(g, zs), device_id_type=MESH).wait_recv()

    for t, k in enumerate(slab_order):
        q = (zi + nh - k) % nh
        if k == 0:
            wait_part(1 - zp, q)
        else:
            wait_part(0, q)
            wait_part(1, q)
        y_out[:, slab(q)] = y_parts[0, :, slab(q)] + y_parts[1, :, slab(q)]
        forward(t, q)
    x_wide[y_piece(pos_b), :] = y_out[...]
    for c in z_sends:
        c.wait_send()
    for cb in b_copies:
        cb.wait_send()
    for t, k in enumerate(slab_order):
        q = (zi + nh - k) % nh
        for kb in range(1, ny):
            jb = (pos_b + ny - kb) % ny
            sb = fwd_base + t * (ny - 1) + kb - 1
            pltpu.make_async_remote_copy(
                src_ref=z_full, dst_ref=x_wide.at[y_piece(jb), slab(q)], send_sem=send_sem.at[sb],
                recv_sem=recv_sem.at[sb], device_id=y_dev(jb), device_id_type=MESH).wait_recv()
    half_off = core * rc
    other_off = (1 - core) * rc

    def out_rows(off, j):
        return pl.ds(pl.multiple_of(off + j * rx, 8), rx)

    a_sends = []
    for k in range(1, nx):
        j = (pos_a + k) % nx
        s = next_sem()
        c = pltpu.make_async_remote_copy(
            src_ref=x_out, dst_ref=core_out.at[x_piece(pos_a)], send_sem=send_sem.at[s],
            recv_sem=recv_sem.at[s], device_id=x_dev(j), device_id_type=MESH)
        c.start()
        a_sends.append((c, s, k))
    fwd = []
    s = next_sem()
    c = pltpu.make_async_remote_copy(
        src_ref=x_out, dst_ref=out_ref.at[out_rows(half_off, pos_a)], send_sem=send_sem.at[s],
        recv_sem=recv_sem.at[s], device_id=core_dev(0), device_id_type=MESH)
    c.start()
    fwd.append((c, s, pos_a))
    core_out[x_piece(pos_a)] = x_out[...]
    for c, s, k in a_sends:
        j = (pos_a + nx - k) % nx
        pltpu.make_async_remote_copy(
            src_ref=x_out, dst_ref=core_out.at[x_piece(j)], send_sem=send_sem.at[s],
            recv_sem=recv_sem.at[s], device_id=x_dev(j), device_id_type=MESH).wait_recv()
        s2 = next_sem()
        c2 = pltpu.make_async_remote_copy(
            src_ref=core_out.at[x_piece(j)], dst_ref=out_ref.at[out_rows(half_off, j)], send_sem=send_sem.at[s2],
            recv_sem=recv_sem.at[s2], device_id=core_dev(0), device_id_type=MESH)
        c2.start()
        fwd.append((c2, s2, j))
    for c, s, k in a_sends:
        c.wait_send()
    mine = core_out[...]
    out_ref[core_piece(core)] = mine
    own = jnp.sum(jnp.sum(mine * mine, axis=0, keepdims=True), axis=1, keepdims=True)
    for c, s, j in fwd:
        c.wait_send()
    partner_pos = xi + (yi - xi) * (1 - core)
    for idx, (c, s, j) in enumerate(fwd):
        jp = (partner_pos + nx - idx) % nx
        pltpu.make_async_remote_copy(
            src_ref=x_out, dst_ref=out_ref.at[out_rows(other_off, jp)], send_sem=send_sem.at[s],
            recv_sem=recv_sem.at[s], device_id=core_dev(0), device_id_type=MESH).wait_recv()
    other = out_ref[core_piece(1 - core)]
    rest = jnp.sum(jnp.sum(other * other, axis=0, keepdims=True), axis=1, keepdims=True)
    sq_ref[...] = jnp.broadcast_to(own + rest, sq_ref.shape)


def allreduce(g, tail, nx, ny, nz):
    assert nx == ny
    rows = g.shape[1]
    cols = g.shape[2] + tail.shape[1]
    nh = nz // 2
    rc = rows // 2
    rx = rc // nx
    ry = rx // ny
    zcols = 128 * nh * ((cols + 128 * nh - 1) // (128 * nh))
    cz = zcols // nh
    n_sems = 2 * (1 + (nx - 1) + (ny - 1) + (nh - 1)) + 1 + 2 * (nx - 1) + (nh - 1) * (ny - 1) + 2 * nz
    f32 = jnp.float32
    return pl.pallas_call(
        functools.partial(_allreduce_kernel, nx, ny, nz),
        out_shape=(jax.ShapeDtypeStruct((rows, cols), f32), jax.ShapeDtypeStruct((8, 128), f32)),
        in_specs=[pl.BlockSpec(memory_space=pltpu.VMEM)] * 2,
        out_specs=(pl.BlockSpec(memory_space=pltpu.VMEM),) * 2,
        scratch_shapes=[
            pltpu.VMEM((rows, cols), f32),
            pltpu.VMEM((1, rc, cols), f32),
            pltpu.VMEM((rc, cols), f32),
            pltpu.VMEM((nx - 1, rx, cols), f32),
            pltpu.VMEM((rx, cols), f32),
            pltpu.VMEM((ny - 1, ry, cols), f32),
            pltpu.VMEM((ry, zcols), f32),
            pltpu.VMEM((nh - 1, ry, cz), f32),
            pltpu.VMEM((ry, cz), f32),
            pltpu.VMEM((2, ry, zcols), f32),
            pltpu.VMEM((ry, cz), f32),
            pltpu.VMEM((ry, zcols), f32),
            pltpu.VMEM((rx, zcols), f32),
            pltpu.VMEM((rc, cols), f32),
            pltpu.SemaphoreType.DMA((n_sems,)),
            pltpu.SemaphoreType.DMA((n_sems,)),
        ],
        compiler_params=pltpu.CompilerParams(
            collective_id=0, has_side_effects=True, vmem_limit_bytes=48 * 1024 * 1024),
    )(g, tail)


def per_device(nx, ny, grads, vec_grads, weight, basis, moment, second, vectors, vec_moment, vec_second):
    shards = lax.axis_size("shard")
    width = grads.shape[-1]
    rows = weight.shape[0]
    cols = vectors.shape[1]
    vec_n = vectors.shape[0]
    me = lax.axis_index("shard")
    vec_local = vec_grads[0, 0, 0].astype(jnp.float32) + vec_grads[1, 0, 0].astype(jnp.float32)
    lanes = 128 * ((cols + 127) // 128)
    placed = vec_local.reshape(vec_n, shards, cols).transpose(1, 0, 2).reshape(shards * vec_n, cols)
    tail = jnp.pad(placed, ((0, width - shards * vec_n), (0, lanes - cols)))
    packed, sq = allreduce(grads[:, 0, 0], tail, nx, ny, shards)
    total = packed[:, :width]
    projected_all = matmul(total, basis)
    subspace = lax.dot_general(
        total,
        projected_all,
        (((0,), (0,)), ((), ())),
        precision=HIGH,
        preferred_element_type=jnp.float32,
    )
    squares = sq[0, 0]
    iterate = subspace / jnp.sqrt(jnp.sum(subspace * subspace) + 1e-06)
    for step in range(NS_STEPS):
        gram = matmul(iterate.T, iterate)
        iterate = 1.5 * iterate - 0.5 * matmul(iterate, gram)
    factor = 1.0 / jnp.maximum(jnp.sqrt(squares / (width * width + vec_n * width)), 1.0)
    projected = lax.dynamic_slice_in_dim(projected_all, me * rows, rows, axis=0)
    vec_sum = lax.dynamic_slice(packed, (me * vec_n, width), (vec_n, cols))
    first_fix = 1.0 - 0.9**STEP
    second_fix = 1.0 - 0.999**STEP
    grad_low = factor * projected
    new_moment = 0.9 * moment + 0.1 * grad_low
    new_second = 0.999 * second + 0.001 * grad_low * grad_low
    normalized = new_moment / first_fix / (jnp.sqrt(new_second / second_fix) + 1e-08)
    full = lax.dot_general(
        normalized,
        basis,
        (((1,), (1,)), ((), ())),
        precision=HIGH,
        preferred_element_type=jnp.float32,
    )
    new_weight = weight - 0.001 * (0.25 * full + 0.01 * weight)
    vec_grad = factor * vec_sum
    new_vec_moment = 0.9 * vec_moment + 0.1 * vec_grad
    new_vec_second = 0.999 * vec_second + 0.001 * vec_grad * vec_grad
    vec_step = new_vec_moment / first_fix / (jnp.sqrt(new_vec_second / second_fix) + 1e-08)
    new_vectors = vectors - 0.001 * (vec_step + 0.01 * vectors)
    return (
        new_weight,
        full.astype(jnp.bfloat16),
        new_moment,
        new_second,
        iterate,
        new_vectors,
        new_vec_moment,
        new_vec_second,
    )


def solution(mesh, nx=None):
    if nx is None:
        nx = math.isqrt(mesh.shape["grp"] // 2)
    ny = mesh.shape["grp"] // 2 // nx
    return jax.shard_map(
        functools.partial(per_device, nx, ny),
        mesh=mesh,
        in_specs=(
            P(None, "grp", "shard", None, None),
            P(None, "grp", "shard", None, None),
            P("shard", None),
            P(),
            P("shard", None),
            P("shard", None),
            P(None, "shard"),
            P(None, "shard"),
            P(None, "shard"),
        ),
        out_specs=(
            P("shard", None),
            P("shard", None),
            P("shard", None),
            P("shard", None),
            P(),
            P(None, "shard"),
            P(None, "shard"),
            P(None, "shard"),
        ),
        check_vma=False,
    )
```

```python
import functools
import math

import jax
import jax.numpy as jnp
from jax import lax
from jax.experimental import pallas as pl
from jax.experimental.pallas import tpu as pltpu
from jax.sharding import PartitionSpec as P

NS_STEPS = 5
STEP = 100
MESH = pl.DeviceIdType.MESH


HIGH = lax.Precision.HIGH


def matmul(left, right):
    return jnp.dot(left, right, precision=HIGH, preferred_element_type=jnp.float32)


def _allreduce_kernel(nx, ny, nz, g_ref, tail_ref, out_ref, sq_ref, x_ref, core_recv, core_sum, x_recv, x_sum, y_recv,
                      y_pad, z_recv, z_sum, pair_recv, z_full, y_out, x_wide, core_out, send_sem, recv_sem):
    rows, cols = x_ref.shape
    zcols = y_pad.shape[1]
    width = g_ref.shape[-1]
    nh = nz // 2
    rc, rx, ry, cz = rows // 2, rows // 2 // nx, rows // 2 // nx // ny, zcols // nh
    g = lax.axis_index("grp")
    z = lax.axis_index("shard")
    core = g % 2
    xi = (g // 2) % nx
    yi = g // (2 * nx)
    zp = z % 2
    zi = z // 2

    def core_dev(_):
        return (g + 1 - 2 * core, z)

    stride_a = 2 + (2 * nx - 2) * core
    pos_a = xi + (yi - xi) * core
    stride_b = 2 * nx - (2 * nx - 2) * core
    pos_b = yi + (xi - yi) * core

    def x_dev(j):
        return (g + stride_a * (j - pos_a), z)

    def y_dev(j):
        return (g + stride_b * (j - pos_b), z)

    def z_dev(j):
        return (g, zp + 2 * j)

    pair_dev = (g, z + 1 - 2 * zp)

    barrier = pltpu.get_barrier_semaphore()
    peers = [core_dev(0)] + [(g, 1 - zp + 2 * j) for j in range(nh)]
    peers += [x_dev((pos_a + k) % nx) for k in range(1, nx)]
    peers += [y_dev((pos_b + k) % ny) for k in range(1, ny)]
    peers += [z_dev((zi + k) % nh) for k in range(1, nh)]
    for dev in peers:
        pl.semaphore_signal(barrier, inc=1, device_id=dev, device_id_type=MESH)

    def pack(j):
        r = pl.ds(pl.multiple_of(j * (rows // 2), 8), rows // 2)
        x_ref[r, :width] = g_ref[0, r, :].astype(jnp.float32) + g_ref[1, r, :].astype(jnp.float32)
        x_ref[r, width:] = tail_ref[r, :]


    counter = [0]

    def next_sem():
        s = counter[0]
        counter[0] += 1
        return s

    def row_slice(j, size):
        return pl.ds(pl.multiple_of(j * size, 8), size)

    def col_slice(j, size):
        return (slice(None), pl.ds(pl.multiple_of(j * size, 128), size))

    def far_first(n):
        return sorted(range(1, n), key=lambda k: (-min(k, n - k), k))

    def reduce_stage(src, n, me, dev_of, recv, dst, piece):
        copies = []
        for k in far_first(n):
            j = (me + k) % n
            s = next_sem()
            c = pltpu.make_async_remote_copy(
                src_ref=src.at[piece(j)], dst_ref=recv.at[k - 1], send_sem=send_sem.at[s],
                recv_sem=recv_sem.at[s], device_id=dev_of(j), device_id_type=MESH)
            c.start()
            copies.append(c)
        for c in copies:
            c.wait()
        acc = src[piece(me)]
        for k in range(1, n):
            acc = acc + recv[k - 1]
        dst[...] = acc

    def gather_stage(src, n, me, dev_of, dst, piece):
        copies = []
        for k in far_first(n):
            j = (me + k) % n
            s = next_sem()
            c = pltpu.make_async_remote_copy(
                src_ref=src, dst_ref=dst.at[piece(me)], send_sem=send_sem.at[s],
                recv_sem=recv_sem.at[s], device_id=dev_of(j), device_id_type=MESH)
            c.start()
            copies.append((c, s, k))
        dst[piece(me)] = src[...]
        for c, s, k in copies:
            c.wait_send()
            j = (me + n - k) % n
            pltpu.make_async_remote_copy(
                src_ref=src, dst_ref=dst.at[piece(j)], send_sem=send_sem.at[s],
                recv_sem=recv_sem.at[s], device_id=dev_of(j), device_id_type=MESH).wait_recv()

    core_piece = lambda j: row_slice(j, rc)
    x_piece = lambda j: row_slice(j, rx)
    y_piece = lambda j: row_slice(j, ry)
    z_piece = lambda j: col_slice(j, cz)

    pack(1 - core)
    pl.semaphore_wait(barrier, len(peers))
    order = far_first(nx) + [0]
    partner_pos = xi + (yi - xi) * (1 - core)

    def half_rows(h, q):
        return pl.ds(pl.multiple_of(h * rc + q * rx, 8), rx)

    core_copies = []
    for k in order:
        q = (partner_pos + k) % nx
        s = next_sem()
        c = pltpu.make_async_remote_copy(
            src_ref=x_ref.at[half_rows(1 - core, q)], dst_ref=core_recv.at[0].at[x_piece(q)],
            send_sem=send_sem.at[s], recv_sem=recv_sem.at[s], device_id=core_dev(0), device_id_type=MESH)
        c.start()
        core_copies.append((c, s))
    pack(core)
    a_copies = []
    for (c, s), k in zip(core_copies, order):
        q = (pos_a + k) % nx
        pltpu.make_async_remote_copy(
            src_ref=x_ref.at[half_rows(1 - core, q)], dst_ref=core_recv.at[0].at[x_piece(q)],
            send_sem=send_sem.at[s], recv_sem=recv_sem.at[s], device_id=core_dev(0),
            device_id_type=MESH).wait_recv()
        core_sum[x_piece(q)] = x_ref[half_rows(core, q)] + core_recv[0, x_piece(q)]
        if k != 0:
            s2 = next_sem()
            c2 = pltpu.make_async_remote_copy(
                src_ref=core_sum.at[x_piece(q)], dst_ref=x_recv.at[k - 1], send_sem=send_sem.at[s2],
                recv_sem=recv_sem.at[s2], device_id=x_dev(q), device_id_type=MESH)
            c2.start()
            a_copies.append(c2)
    for c, s in core_copies:
        c.wait_send()
    for c2 in a_copies:
        c2.wait()
    acc = core_sum[x_piece(pos_a)]
    for k in range(1, nx):
        acc = acc + x_recv[k - 1]
    x_sum[...] = acc
    if zcols > cols:
        y_pad[:, cols:] = jnp.zeros((ry, zcols - cols), jnp.float32)
    reduce_stage(x_sum, ny, pos_b, y_dev, y_recv, y_pad.at[:, pl.ds(0, cols)], y_piece)
    reduce_stage(y_pad, nh, zi, z_dev, z_recv, z_sum, z_piece)

    x_out = x_wide.at[:, pl.ds(0, cols)]
    y_parts = pair_recv

    def slab(q):
        return pl.ds(pl.multiple_of(q * cz, 128), cz)

    sbase = counter[0]
    counter[0] += nz - 1
    rbase = counter[0]
    counter[0] += nz
    z_sends = []
    for idx, off in enumerate(far_first(nz)):
        c = pltpu.make_async_remote_copy(
            src_ref=z_sum, dst_ref=y_parts.at[zp, :, slab(zi)], send_sem=send_sem.at[sbase + idx],
            recv_sem=recv_sem.at[rbase + z], device_id=(g, (z + off) % nz), device_id_type=MESH)
        c.start()
        z_sends.append(c)
    y_parts[zp, :, slab(zi)] = z_sum[...]
    fwd_base = counter[0]
    counter[0] += nh * (ny - 1)
    slab_order = [0] + sorted(range(1, nh), key=lambda k: (min(k, nh - k), k))
    b_copies = []

    def forward(t, q):
        for kb in range(1, ny):
            jb = (pos_b + kb) % ny
            sb = fwd_base + t * (ny - 1) + kb - 1
            cb = pltpu.make_async_remote_copy(
                src_ref=y_out.at[:, slab(q)], dst_ref=x_wide.at[y_piece(pos_b), slab(q)],
                send_sem=send_sem.at[sb], recv_sem=recv_sem.at[sb], device_id=y_dev(jb), device_id_type=MESH)
            cb.start()
            b_copies.append(cb)

    def wait_part(p, q):
        zs = 2 * q + p
        pltpu.make_async_remote_copy(
            src_ref=z_sum, dst_ref=y_parts.at[p, :, slab(q)], send_sem=send_sem.at[sbase],
            recv_sem=recv_sem.at[rbase + zs], device_id=(g, zs), device_id_type=MESH).wait_recv()

    for t, k in enumerate(slab_order):
        q = (zi + nh - k) % nh
        if k == 0:
            wait_part(1 - zp, q)
        else:
            wait_part(0, q)
            wait_part(1, q)
        y_out[:, slab(q)] = y_parts[0, :, slab(q)] + y_parts[1, :, slab(q)]
        forward(t, q)
    x_wide[y_piece(pos_b), :] = y_out[...]
    for c in z_sends:
        c.wait_send()
    for cb in b_copies:
        cb.wait_send()
    for t, k in enumerate(slab_order):
        q = (zi + nh - k) % nh
        for kb in range(1, ny):
            jb = (pos_b + ny - kb) % ny
            sb = fwd_base + t * (ny - 1) + kb - 1
            pltpu.make_async_remote_copy(
                src_ref=z_full, dst_ref=x_wide.at[y_piece(jb), slab(q)], send_sem=send_sem.at[sb],
                recv_sem=recv_sem.at[sb], device_id=y_dev(jb), device_id_type=MESH).wait_recv()
    half_off = core * rc
    other_off = (1 - core) * rc

    def out_rows(off, j):
        return pl.ds(pl.multiple_of(off + j * rx, 8), rx)

    a_sends = []
    for k in range(1, nx):
        j = (pos_a + k) % nx
        s = next_sem()
        c = pltpu.make_async_remote_copy(
            src_ref=x_out, dst_ref=core_out.at[x_piece(pos_a)], send_sem=send_sem.at[s],
            recv_sem=recv_sem.at[s], device_id=x_dev(j), device_id_type=MESH)
        c.start()
        a_sends.append((c, s, k))
    fwd = []
    s = next_sem()
    c = pltpu.make_async_remote_copy(
        src_ref=x_out, dst_ref=out_ref.at[out_rows(half_off, pos_a)], send_sem=send_sem.at[s],
        recv_sem=recv_sem.at[s], device_id=core_dev(0), device_id_type=MESH)
    c.start()
    fwd.append((c, s, pos_a))
    core_out[x_piece(pos_a)] = x_out[...]
    for c, s, k in a_sends:
        j = (pos_a + nx - k) % nx
        pltpu.make_async_remote_copy(
            src_ref=x_out, dst_ref=core_out.at[x_piece(j)], send_sem=send_sem.at[s],
            recv_sem=recv_sem.at[s], device_id=x_dev(j), device_id_type=MESH).wait_recv()
        s2 = next_sem()
        c2 = pltpu.make_async_remote_copy(
            src_ref=core_out.at[x_piece(j)], dst_ref=out_ref.at[out_rows(half_off, j)], send_sem=send_sem.at[s2],
            recv_sem=recv_sem.at[s2], device_id=core_dev(0), device_id_type=MESH)
        c2.start()
        fwd.append((c2, s2, j))
    for c, s, k in a_sends:
        c.wait_send()
    mine = core_out[...]
    out_ref[core_piece(core)] = mine
    own = jnp.sum(jnp.sum(mine * mine, axis=0, keepdims=True), axis=1, keepdims=True)
    for c, s, j in fwd:
        c.wait_send()
    partner_pos = xi + (yi - xi) * (1 - core)
    for idx, (c, s, j) in enumerate(fwd):
        jp = (partner_pos + nx - idx) % nx
        pltpu.make_async_remote_copy(
            src_ref=x_out, dst_ref=out_ref.at[out_rows(other_off, jp)], send_sem=send_sem.at[s],
            recv_sem=recv_sem.at[s], device_id=core_dev(0), device_id_type=MESH).wait_recv()
    other = out_ref[core_piece(1 - core)]
    rest = jnp.sum(jnp.sum(other * other, axis=0, keepdims=True), axis=1, keepdims=True)
    sq_ref[...] = own + rest


def allreduce(g, tail, nx, ny, nz):
    assert nx == ny
    rows = g.shape[1]
    cols = g.shape[2] + tail.shape[1]
    nh = nz // 2
    rc = rows // 2
    rx = rc // nx
    ry = rx // ny
    zcols = 128 * nh * ((cols + 128 * nh - 1) // (128 * nh))
    cz = zcols // nh
    n_sems = 2 * (1 + (nx - 1) + (ny - 1) + (nh - 1)) + 1 + 2 * (nx - 1) + (nh - 1) * (ny - 1) + 2 * nz
    f32 = jnp.float32
    return pl.pallas_call(
        functools.partial(_allreduce_kernel, nx, ny, nz),
        out_shape=(jax.ShapeDtypeStruct((rows, cols), f32), jax.ShapeDtypeStruct((1, 1), f32)),
        in_specs=[pl.BlockSpec(memory_space=pltpu.VMEM)] * 2,
        out_specs=(pl.BlockSpec(memory_space=pltpu.VMEM),) * 2,
        scratch_shapes=[
            pltpu.VMEM((rows, cols), f32),
            pltpu.VMEM((1, rc, cols), f32),
            pltpu.VMEM((rc, cols), f32),
            pltpu.VMEM((nx - 1, rx, cols), f32),
            pltpu.VMEM((rx, cols), f32),
            pltpu.VMEM((ny - 1, ry, cols), f32),
            pltpu.VMEM((ry, zcols), f32),
            pltpu.VMEM((nh - 1, ry, cz), f32),
            pltpu.VMEM((ry, cz), f32),
            pltpu.VMEM((2, ry, zcols), f32),
            pltpu.VMEM((ry, cz), f32),
            pltpu.VMEM((ry, zcols), f32),
            pltpu.VMEM((rx, zcols), f32),
            pltpu.VMEM((rc, cols), f32),
            pltpu.SemaphoreType.DMA((n_sems,)),
            pltpu.SemaphoreType.DMA((n_sems,)),
        ],
        compiler_params=pltpu.CompilerParams(
            collective_id=0, has_side_effects=True, vmem_limit_bytes=48 * 1024 * 1024),
    )(g, tail)


def per_device(nx, ny, grads, vec_grads, weight, basis, moment, second, vectors, vec_moment, vec_second):
    shards = lax.axis_size("shard")
    width = grads.shape[-1]
    rows = weight.shape[0]
    cols = vectors.shape[1]
    vec_n = vectors.shape[0]
    me = lax.axis_index("shard")
    vec_local = vec_grads[0, 0, 0].astype(jnp.float32) + vec_grads[1, 0, 0].astype(jnp.float32)
    lanes = 128 * ((cols + 127) // 128)
    placed = vec_local.reshape(vec_n, shards, cols).transpose(1, 0, 2).reshape(shards * vec_n, cols)
    tail = jnp.pad(placed, ((0, width - shards * vec_n), (0, lanes - cols)))
    packed, sq = allreduce(grads[:, 0, 0], tail, nx, ny, shards)
    total = packed[:, :width]
    projected_all = matmul(total, basis)
    subspace = lax.dot_general(
        total,
        projected_all,
        (((0,), (0,)), ((), ())),
        precision=HIGH,
        preferred_element_type=jnp.float32,
    )
    squares = sq[0, 0]
    iterate = subspace / jnp.sqrt(jnp.sum(subspace * subspace) + 1e-06)
    for step in range(NS_STEPS):
        gram = matmul(iterate.T, iterate)
        iterate = 1.5 * iterate - 0.5 * matmul(iterate, gram)
    factor = 1.0 / jnp.maximum(jnp.sqrt(squares / (width * width + vec_n * width)), 1.0)
    projected = lax.dynamic_slice_in_dim(projected_all, me * rows, rows, axis=0)
    vec_sum = lax.dynamic_slice(packed, (me * vec_n, width), (vec_n, cols))
    first_fix = 1.0 - 0.9**STEP
    second_fix = 1.0 - 0.999**STEP
    grad_low = factor * projected
    new_moment = 0.9 * moment + 0.1 * grad_low
    new_second = 0.999 * second + 0.001 * grad_low * grad_low
    normalized = new_moment / first_fix / (jnp.sqrt(new_second / second_fix) + 1e-08)
    full = lax.dot_general(
        normalized,
        basis,
        (((1,), (1,)), ((), ())),
        precision=HIGH,
        preferred_element_type=jnp.float32,
    )
    new_weight = weight - 0.001 * (0.25 * full + 0.01 * weight)
    vec_grad = factor * vec_sum
    new_vec_moment = 0.9 * vec_moment + 0.1 * vec_grad
    new_vec_second = 0.999 * vec_second + 0.001 * vec_grad * vec_grad
    vec_step = new_vec_moment / first_fix / (jnp.sqrt(new_vec_second / second_fix) + 1e-08)
    new_vectors = vectors - 0.001 * (vec_step + 0.01 * vectors)
    return (
        new_weight,
        full.astype(jnp.bfloat16),
        new_moment,
        new_second,
        iterate,
        new_vectors,
        new_vec_moment,
        new_vec_second,
    )


def solution(mesh, nx=None):
    if nx is None:
        nx = math.isqrt(mesh.shape["grp"] // 2)
    ny = mesh.shape["grp"] // 2 // nx
    return jax.shard_map(
        functools.partial(per_device, nx, ny),
        mesh=mesh,
        in_specs=(
            P(None, "grp", "shard", None, None),
            P(None, "grp", "shard", None, None),
            P("shard", None),
            P(),
            P("shard", None),
            P("shard", None),
            P(None, "shard"),
            P(None, "shard"),
            P(None, "shard"),
        ),
        out_specs=(
            P("shard", None),
            P("shard", None),
            P("shard", None),
            P("shard", None),
            P(),
            P(None, "shard"),
            P(None, "shard"),
            P(None, "shard"),
        ),
        check_vma=False,
    )
```

```python
import functools
import math

import jax
import jax.numpy as jnp
from jax import lax
from jax.experimental import pallas as pl
from jax.experimental.pallas import tpu as pltpu
from jax.sharding import PartitionSpec as P

NS_STEPS = 5
STEP = 100
MESH = pl.DeviceIdType.MESH


HIGH = lax.Precision.HIGH


def matmul(left, right):
    return jnp.dot(left, right, precision=HIGH, preferred_element_type=jnp.float32)


def _allreduce_kernel(nx, ny, nz, g_ref, tail_ref, out_ref, sq_ref, x_ref, core_recv, core_sum, x_recv, x_sum, y_recv,
                      y_pad, z_recv, z_sum, pair_recv, z_full, y_out, x_wide, core_out, send_sem, recv_sem):
    rows, cols = x_ref.shape
    zcols = y_pad.shape[1]
    width = g_ref.shape[-1]
    nh = nz // 2
    rc, rx, ry, cz = rows // 2, rows // 2 // nx, rows // 2 // nx // ny, zcols // nh
    g = lax.axis_index("grp")
    z = lax.axis_index("shard")
    core = g % 2
    xi = (g // 2) % nx
    yi = g // (2 * nx)
    zp = z % 2
    zi = z // 2

    def core_dev(_):
        return (g + 1 - 2 * core, z)

    stride_a = 2 + (2 * nx - 2) * core
    pos_a = xi + (yi - xi) * core
    stride_b = 2 * nx - (2 * nx - 2) * core
    pos_b = yi + (xi - yi) * core

    def x_dev(j):
        return (g + stride_a * (j - pos_a), z)

    def y_dev(j):
        return (g + stride_b * (j - pos_b), z)

    def z_dev(j):
        return (g, zp + 2 * j)

    pair_dev = (g, z + 1 - 2 * zp)

    barrier = pltpu.get_barrier_semaphore()
    peers = [core_dev(0)] + [(g, 1 - zp + 2 * j) for j in range(nh)]
    peers += [x_dev((pos_a + k) % nx) for k in range(1, nx)]
    peers += [y_dev((pos_b + k) % ny) for k in range(1, ny)]
    peers += [z_dev((zi + k) % nh) for k in range(1, nh)]
    for dev in peers:
        pl.semaphore_signal(barrier, inc=1, device_id=dev, device_id_type=MESH)

    def pack(j):
        r = pl.ds(pl.multiple_of(j * (rows // 2), 8), rows // 2)
        x_ref[r, :width] = g_ref[0, r, :].astype(jnp.float32) + g_ref[1, r, :].astype(jnp.float32)
        x_ref[r, width:] = tail_ref[r, :]


    counter = [0]

    def next_sem():
        s = counter[0]
        counter[0] += 1
        return s

    def row_slice(j, size):
        return pl.ds(pl.multiple_of(j * size, 8), size)

    def col_slice(j, size):
        return (slice(None), pl.ds(pl.multiple_of(j * size, 128), size))

    def far_first(n):
        return sorted(range(1, n), key=lambda k: (-min(k, n - k), k))

    def reduce_stage(src, n, me, dev_of, recv, dst, piece):
        copies = []
        for k in far_first(n):
            j = (me + k) % n
            s = next_sem()
            c = pltpu.make_async_remote_copy(
                src_ref=src.at[piece(j)], dst_ref=recv.at[k - 1], send_sem=send_sem.at[s],
                recv_sem=recv_sem.at[s], device_id=dev_of(j), device_id_type=MESH)
            c.start()
            copies.append(c)
        for c in copies:
            c.wait()
        acc = src[piece(me)]
        for k in range(1, n):
            acc = acc + recv[k - 1]
        dst[...] = acc

    def gather_stage(src, n, me, dev_of, dst, piece):
        copies = []
        for k in far_first(n):
            j = (me + k) % n
            s = next_sem()
            c = pltpu.make_async_remote_copy(
                src_ref=src, dst_ref=dst.at[piece(me)], send_sem=send_sem.at[s],
                recv_sem=recv_sem.at[s], device_id=dev_of(j), device_id_type=MESH)
            c.start()
            copies.append((c, s, k))
        dst[piece(me)] = src[...]
        for c, s, k in copies:
            c.wait_send()
            j = (me + n - k) % n
            pltpu.make_async_remote_copy(
                src_ref=src, dst_ref=dst.at[piece(j)], send_sem=send_sem.at[s],
                recv_sem=recv_sem.at[s], device_id=dev_of(j), device_id_type=MESH).wait_recv()

    core_piece = lambda j: row_slice(j, rc)
    x_piece = lambda j: row_slice(j, rx)
    y_piece = lambda j: row_slice(j, ry)
    z_piece = lambda j: col_slice(j, cz)

    pack(1 - core)
    pl.semaphore_wait(barrier, len(peers))
    order = far_first(nx) + [0]
    partner_pos = xi + (yi - xi) * (1 - core)

    def half_rows(h, q):
        return pl.ds(pl.multiple_of(h * rc + q * rx, 8), rx)

    core_copies = []
    for k in order:
        q = (partner_pos + k) % nx
        s = next_sem()
        c = pltpu.make_async_remote_copy(
            src_ref=x_ref.at[half_rows(1 - core, q)], dst_ref=core_recv.at[0].at[x_piece(q)],
            send_sem=send_sem.at[s], recv_sem=recv_sem.at[s], device_id=core_dev(0), device_id_type=MESH)
        c.start()
        core_copies.append((c, s))
    pack(core)
    a_copies = []
    for (c, s), k in zip(core_copies, order):
        q = (pos_a + k) % nx
        pltpu.make_async_remote_copy(
            src_ref=x_ref.at[half_rows(1 - core, q)], dst_ref=core_recv.at[0].at[x_piece(q)],
            send_sem=send_sem.at[s], recv_sem=recv_sem.at[s], device_id=core_dev(0),
            device_id_type=MESH).wait_recv()
        core_sum[x_piece(q)] = x_ref[half_rows(core, q)] + core_recv[0, x_piece(q)]
        if k != 0:
            s2 = next_sem()
            c2 = pltpu.make_async_remote_copy(
                src_ref=core_sum.at[x_piece(q)], dst_ref=x_recv.at[k - 1], send_sem=send_sem.at[s2],
                recv_sem=recv_sem.at[s2], device_id=x_dev(q), device_id_type=MESH)
            c2.start()
            a_copies.append(c2)
    for c, s in core_copies:
        c.wait_send()
    for c2 in a_copies:
        c2.wait()
    acc = core_sum[x_piece(pos_a)]
    for k in range(1, nx):
        acc = acc + x_recv[k - 1]
    x_sum[...] = acc
    if zcols > cols:
        y_pad[:, cols:] = jnp.zeros((ry, zcols - cols), jnp.float32)
    reduce_stage(x_sum, ny, pos_b, y_dev, y_recv, y_pad.at[:, pl.ds(0, cols)], y_piece)
    reduce_stage(y_pad, nh, zi, z_dev, z_recv, z_sum, z_piece)

    x_out = x_wide.at[:, pl.ds(0, cols)]
    y_parts = pair_recv

    def slab(q):
        return pl.ds(pl.multiple_of(q * cz, 128), cz)

    sbase = counter[0]
    counter[0] += nz - 1
    rbase = counter[0]
    counter[0] += nz
    z_sends = []
    for idx, off in enumerate(far_first(nz)):
        c = pltpu.make_async_remote_copy(
            src_ref=z_sum, dst_ref=y_parts.at[zp, :, slab(zi)], send_sem=send_sem.at[sbase + idx],
            recv_sem=recv_sem.at[rbase + z], device_id=(g, (z + off) % nz), device_id_type=MESH)
        c.start()
        z_sends.append(c)
    y_parts[zp, :, slab(zi)] = z_sum[...]
    fwd_base = counter[0]
    counter[0] += nh * (ny - 1)
    slab_order = [0] + sorted(range(1, nh), key=lambda k: (min(k, nh - k), k))
    b_copies = []

    def forward(t, q):
        for kb in range(1, ny):
            jb = (pos_b + kb) % ny
            sb = fwd_base + t * (ny - 1) + kb - 1
            cb = pltpu.make_async_remote_copy(
                src_ref=y_out.at[:, slab(q)], dst_ref=x_wide.at[y_piece(pos_b), slab(q)],
                send_sem=send_sem.at[sb], recv_sem=recv_sem.at[sb], device_id=y_dev(jb), device_id_type=MESH)
            cb.start()
            b_copies.append(cb)

    def wait_part(p, q):
        zs = 2 * q + p
        pltpu.make_async_remote_copy(
            src_ref=z_sum, dst_ref=y_parts.at[p, :, slab(q)], send_sem=send_sem.at[sbase],
            recv_sem=recv_sem.at[rbase + zs], device_id=(g, zs), device_id_type=MESH).wait_recv()

    for t, k in enumerate(slab_order):
        q = (zi + nh - k) % nh
        if k == 0:
            wait_part(1 - zp, q)
        else:
            wait_part(0, q)
            wait_part(1, q)
        y_out[:, slab(q)] = y_parts[0, :, slab(q)] + y_parts[1, :, slab(q)]
        forward(t, q)
    x_wide[y_piece(pos_b), :] = y_out[...]
    for c in z_sends:
        c.wait_send()
    for cb in b_copies:
        cb.wait_send()
    for t, k in enumerate(slab_order):
        q = (zi + nh - k) % nh
        for kb in range(1, ny):
            jb = (pos_b + ny - kb) % ny
            sb = fwd_base + t * (ny - 1) + kb - 1
            pltpu.make_async_remote_copy(
                src_ref=z_full, dst_ref=x_wide.at[y_piece(jb), slab(q)], send_sem=send_sem.at[sb],
                recv_sem=recv_sem.at[sb], device_id=y_dev(jb), device_id_type=MESH).wait_recv()
    half_off = core * rc
    other_off = (1 - core) * rc

    def out_rows(off, j):
        return pl.ds(pl.multiple_of(off + j * rx, 8), rx)

    a_sends = []
    for k in far_first(nx):
        j = (pos_a + k) % nx
        s = next_sem()
        c = pltpu.make_async_remote_copy(
            src_ref=x_out, dst_ref=core_out.at[x_piece(pos_a)], send_sem=send_sem.at[s],
            recv_sem=recv_sem.at[s], device_id=x_dev(j), device_id_type=MESH)
        c.start()
        a_sends.append((c, s, k))
    fwd = []
    s = next_sem()
    c = pltpu.make_async_remote_copy(
        src_ref=x_out, dst_ref=out_ref.at[out_rows(half_off, pos_a)], send_sem=send_sem.at[s],
        recv_sem=recv_sem.at[s], device_id=core_dev(0), device_id_type=MESH)
    c.start()
    fwd.append((c, s, pos_a))
    core_out[x_piece(pos_a)] = x_out[...]
    for c, s, k in sorted(a_sends, key=lambda t: t[2]):
        j = (pos_a + nx - k) % nx
        pltpu.make_async_remote_copy(
            src_ref=x_out, dst_ref=core_out.at[x_piece(j)], send_sem=send_sem.at[s],
            recv_sem=recv_sem.at[s], device_id=x_dev(j), device_id_type=MESH).wait_recv()
        s2 = next_sem()
        c2 = pltpu.make_async_remote_copy(
            src_ref=core_out.at[x_piece(j)], dst_ref=out_ref.at[out_rows(half_off, j)], send_sem=send_sem.at[s2],
            recv_sem=recv_sem.at[s2], device_id=core_dev(0), device_id_type=MESH)
        c2.start()
        fwd.append((c2, s2, j))
    for c, s, k in a_sends:
        c.wait_send()
    mine = core_out[...]
    out_ref[core_piece(core)] = mine
    own = jnp.sum(jnp.sum(mine * mine, axis=0, keepdims=True), axis=1, keepdims=True)
    for c, s, j in fwd:
        c.wait_send()
    partner_pos = xi + (yi - xi) * (1 - core)
    for idx, (c, s, j) in enumerate(fwd):
        jp = (partner_pos + nx - idx) % nx
        pltpu.make_async_remote_copy(
            src_ref=x_out, dst_ref=out_ref.at[out_rows(other_off, jp)], send_sem=send_sem.at[s],
            recv_sem=recv_sem.at[s], device_id=core_dev(0), device_id_type=MESH).wait_recv()
    other = out_ref[core_piece(1 - core)]
    rest = jnp.sum(jnp.sum(other * other, axis=0, keepdims=True), axis=1, keepdims=True)
    sq_ref[...] = jnp.broadcast_to(own + rest, sq_ref.shape)


def allreduce(g, tail, nx, ny, nz):
    assert nx == ny
    rows = g.shape[1]
    cols = g.shape[2] + tail.shape[1]
    nh = nz // 2
    rc = rows // 2
    rx = rc // nx
    ry = rx // ny
    zcols = 128 * nh * ((cols + 128 * nh - 1) // (128 * nh))
    cz = zcols // nh
    n_sems = 2 * (1 + (nx - 1) + (ny - 1) + (nh - 1)) + 1 + 2 * (nx - 1) + (nh - 1) * (ny - 1) + 2 * nz
    f32 = jnp.float32
    return pl.pallas_call(
        functools.partial(_allreduce_kernel, nx, ny, nz),
        out_shape=(jax.ShapeDtypeStruct((rows, cols), f32), jax.ShapeDtypeStruct((8, 128), f32)),
        in_specs=[pl.BlockSpec(memory_space=pltpu.VMEM)] * 2,
        out_specs=(pl.BlockSpec(memory_space=pltpu.VMEM),) * 2,
        scratch_shapes=[
            pltpu.VMEM((rows, cols), f32),
            pltpu.VMEM((1, rc, cols), f32),
            pltpu.VMEM((rc, cols), f32),
            pltpu.VMEM((nx - 1, rx, cols), f32),
            pltpu.VMEM((rx, cols), f32),
            pltpu.VMEM((ny - 1, ry, cols), f32),
            pltpu.VMEM((ry, zcols), f32),
            pltpu.VMEM((nh - 1, ry, cz), f32),
            pltpu.VMEM((ry, cz), f32),
            pltpu.VMEM((2, ry, zcols), f32),
            pltpu.VMEM((ry, cz), f32),
            pltpu.VMEM((ry, zcols), f32),
            pltpu.VMEM((rx, zcols), f32),
            pltpu.VMEM((rc, cols), f32),
            pltpu.SemaphoreType.DMA((n_sems,)),
            pltpu.SemaphoreType.DMA((n_sems,)),
        ],
        compiler_params=pltpu.CompilerParams(
            collective_id=0, has_side_effects=True, vmem_limit_bytes=48 * 1024 * 1024),
    )(g, tail)


def per_device(nx, ny, grads, vec_grads, weight, basis, moment, second, vectors, vec_moment, vec_second):
    shards = lax.axis_size("shard")
    width = grads.shape[-1]
    rows = weight.shape[0]
    cols = vectors.shape[1]
    vec_n = vectors.shape[0]
    me = lax.axis_index("shard")
    vec_local = vec_grads[0, 0, 0].astype(jnp.float32) + vec_grads[1, 0, 0].astype(jnp.float32)
    lanes = 128 * ((cols + 127) // 128)
    placed = vec_local.reshape(vec_n, shards, cols).transpose(1, 0, 2).reshape(shards * vec_n, cols)
    tail = jnp.pad(placed, ((0, width - shards * vec_n), (0, lanes - cols)))
    packed, sq = allreduce(grads[:, 0, 0], tail, nx, ny, shards)
    total = packed[:, :width]
    projected_all = matmul(total, basis)
    subspace = lax.dot_general(
        total,
        projected_all,
        (((0,), (0,)), ((), ())),
        precision=HIGH,
        preferred_element_type=jnp.float32,
    )
    squares = sq[0, 0]
    iterate = subspace / jnp.sqrt(jnp.sum(subspace * subspace) + 1e-06)
    for step in range(NS_STEPS):
        gram = matmul(iterate.T, iterate)
        iterate = 1.5 * iterate - 0.5 * matmul(iterate, gram)
    factor = 1.0 / jnp.maximum(jnp.sqrt(squares / (width * width + vec_n * width)), 1.0)
    projected = lax.dynamic_slice_in_dim(projected_all, me * rows, rows, axis=0)
    vec_sum = lax.dynamic_slice(packed, (me * vec_n, width), (vec_n, cols))
    first_fix = 1.0 - 0.9**STEP
    second_fix = 1.0 - 0.999**STEP
    grad_low = factor * projected
    new_moment = 0.9 * moment + 0.1 * grad_low
    new_second = 0.999 * second + 0.001 * grad_low * grad_low
    normalized = new_moment / first_fix / (jnp.sqrt(new_second / second_fix) + 1e-08)
    full = lax.dot_general(
        normalized,
        basis,
        (((1,), (1,)), ((), ())),
        precision=HIGH,
        preferred_element_type=jnp.float32,
    )
    new_weight = weight - 0.001 * (0.25 * full + 0.01 * weight)
    vec_grad = factor * vec_sum
    new_vec_moment = 0.9 * vec_moment + 0.1 * vec_grad
    new_vec_second = 0.999 * vec_second + 0.001 * vec_grad * vec_grad
    vec_step = new_vec_moment / first_fix / (jnp.sqrt(new_vec_second / second_fix) + 1e-08)
    new_vectors = vectors - 0.001 * (vec_step + 0.01 * vectors)
    return (
        new_weight,
        full.astype(jnp.bfloat16),
        new_moment,
        new_second,
        iterate,
        new_vectors,
        new_vec_moment,
        new_vec_second,
    )


def solution(mesh, nx=None):
    if nx is None:
        nx = math.isqrt(mesh.shape["grp"] // 2)
    ny = mesh.shape["grp"] // 2 // nx
    return jax.shard_map(
        functools.partial(per_device, nx, ny),
        mesh=mesh,
        in_specs=(
            P(None, "grp", "shard", None, None),
            P(None, "grp", "shard", None, None),
            P("shard", None),
            P(),
            P("shard", None),
            P("shard", None),
            P(None, "shard"),
            P(None, "shard"),
            P(None, "shard"),
        ),
        out_specs=(
            P("shard", None),
            P("shard", None),
            P("shard", None),
            P("shard", None),
            P(),
            P(None, "shard"),
            P(None, "shard"),
            P(None, "shard"),
        ),
        check_vma=False,
    )
```
